32 devices in a mesh: leaf: 4 (over x, core), blk: 8 (over z, y).
Axes of the slice: x: 2, y: 2, z: 4, core: 2. Of those that a mesh axis runs over, the one named last changes fastest.
Arguments:
- right_side: float32 [4, 8, 448, 128], P('leaf', 'blk'), may hold values from -6 to 6
- inverse_blocks: bfloat16 [4, 8, 448, 2048], P('leaf', 'blk'), may hold values from -0.125 to 0.125
- coupling: bfloat16 [4, 8, 640, 1024], P('leaf', 'blk'), may hold values from -0.0625 to 0.0625
- update_rows: int32 [10, 1024], replicated, may hold values from 0 to 2047, as said below
Outputs:
- solution: float32 [4, 8, 448, 128], P('leaf', 'blk')
The draws below stay inside these ranges and needn't reach their ends.
Inputs may be any that keep to these rules, and one draw needn't show every extreme that they name: `update_rows`: the 1024 entries of each row are distinct.
All inputs are finite; a program needn't handle non-finite values.
Results may differ from the reference program's by a relative error of at most 0.0075.
Values may be sent and summed in bfloat16 or wider, within the bound.
No kernel may reach another device: no remote copies, remote signals or barrier semaphores. Data moves between devices by JAX's collectives and lax.ppermute only.
A program may use at most 64 MiB of HBM per device.

```python
import jax
import jax.numpy as jnp
from jax import lax

W = 2048
UPD = 1024
CASES = 128
HEIGHT = 2
ROWS_DEV = 448
OFF_ROWS = 640
PAIRS = 10
N_LEAF = 4
N_BLK = 8


def draw_update_rows(key, part):
    keys = jax.random.split(key, PAIRS)
    return jax.vmap(lambda single: jax.random.permutation(single, W)[:UPD])(keys).astype(jnp.int32)


def steps_of(key, shape, cuts, low, largest):
    loudness = 1.0
    for dim, shards_of in cuts:
        draws = jax.random.uniform(jax.random.fold_in(jax.random.fold_in(key, 6), dim), (shards_of,), jnp.float32, low / len(cuts), largest / len(cuts))
        loudness = loudness * jnp.repeat(jnp.exp(draws), shape[dim] // shards_of).reshape((-1,) + (1,) * (len(shape) - 1 - dim))
    return loudness


def noise(stream_key, extent, deviation, bound, cuts=(), kind=jnp.bfloat16):
    values = deviation * jax.random.normal(stream_key, extent, jnp.float32)
    if cuts:
        values = values * steps_of(stream_key, extent, cuts, -0.22, 0.18)
    return jnp.clip(values, -bound, bound).astype(kind)


def setup_inputs(seed: int = 0) -> dict:
    arg_keys = jax.random.split(jax.random.key(seed), 5)
    return {
        "right_side": noise(arg_keys[0], (N_LEAF, N_BLK, ROWS_DEV, CASES), 1.0, 6.0, ((0, 4), (1, 8)), jnp.float32),
        "inverse_blocks": noise(arg_keys[1], (N_LEAF, N_BLK, ROWS_DEV, W), W ** -0.5, 0.125, ((0, 4), (1, 8))),
        "coupling": noise(arg_keys[2], (N_LEAF, N_BLK, OFF_ROWS, UPD), (4 * W) ** -0.5, 0.0625, ((0, 4), (1, 8))),
        "update_rows": draw_update_rows(jax.random.fold_in(arg_keys[4], 71), 0),
    }


def level_span(level_no):
    row_start = 0
    for lower_level in range(level_no):
        row_start += W // (N_BLK * 2 ** lower_level)
    return row_start, W // (N_BLK * 2 ** level_no)


def level_rows(stacked, level_no):
    row_start, row_count = level_span(level_no)
    section = stacked[:, :, row_start:row_start + row_count, :]
    return section.reshape(N_LEAF >> level_no, W, stacked.shape[-1])


def coupling_rows(coupling, level_no, ancestor):
    row_start = 0
    for lower_level in range(HEIGHT):
        row_count = W // (N_BLK * 2 ** lower_level)
        for upper_level in range(lower_level + 1, HEIGHT + 1):
            if lower_level == level_no and upper_level == ancestor:
                section = coupling[:, :, row_start:row_start + row_count, :]
                return section.reshape(N_LEAF >> level_no, W, coupling.shape[-1])
            row_start += row_count
    return None


def update_lists(update_rows, level_no, ancestor):
    pair_base = 0
    for lower_level in range(level_no):
        pair_base += (N_LEAF >> lower_level) * (HEIGHT - lower_level)
    node_count = N_LEAF >> level_no
    node_ids = jnp.arange(node_count, dtype=jnp.int32)
    pair_rows = pair_base + node_ids * (HEIGHT - level_no) + (ancestor - level_no - 1)
    parents = node_ids // (2 ** (ancestor - level_no))
    return update_rows[pair_rows], parents


def rounded(values):
    return lax.optimization_barrier(values.astype(jnp.bfloat16)).astype(jnp.float32)


def reference(right_side, inverse_blocks, coupling, update_rows):
    pending = {}
    y_levels = []
    for level_no in range(HEIGHT + 1):
        residual = level_rows(right_side, level_no)
        if level_no in pending:
            residual = residual - pending[level_no]
        inverse = level_rows(inverse_blocks, level_no).astype(jnp.float32)
        y_rows = jnp.einsum("nwv,nvk->nwk", inverse, rounded(residual))
        y_levels.append(y_rows)
        y_round = rounded(y_rows)
        for ancestor in range(level_no + 1, HEIGHT + 1):
            blocks = coupling_rows(coupling, level_no, ancestor).astype(jnp.float32)
            contrib = jnp.einsum("nwu,nwk->nuk", blocks, y_round)
            row_lists, parents = update_lists(update_rows, level_no, ancestor)
            summed = pending.get(ancestor, jnp.zeros((N_LEAF >> ancestor, W, CASES), jnp.float32))
            pending[ancestor] = summed.at[parents[:, None], row_lists].add(contrib)
    solved = {}
    sections = [None] * (HEIGHT + 1)
    for level_no in range(HEIGHT, -1, -1):
        z_rows = y_levels[level_no]
        for ancestor in range(level_no + 1, HEIGHT + 1):
            blocks = coupling_rows(coupling, level_no, ancestor).astype(jnp.float32)
            row_lists, parents = update_lists(update_rows, level_no, ancestor)
            picked = solved[ancestor][parents[:, None], row_lists].astype(jnp.float32)
            z_rows = z_rows - jnp.einsum("nwu,nuk->nwk", blocks, picked)
        inverse = level_rows(inverse_blocks, level_no).astype(jnp.float32)
        x_rows = jnp.einsum("nvw,nvk->nwk", inverse, rounded(z_rows))
        row_start, row_count = level_span(level_no)
        sections[level_no] = x_rows.reshape(N_LEAF, N_BLK, row_count, CASES)
        solved[level_no] = x_rows.astype(jnp.bfloat16)
    return jnp.concatenate(sections, axis=2)
```

```python
import jax
import jax.numpy as jnp
from jax import lax
from jax.sharding import PartitionSpec as P


BF16 = jnp.bfloat16
F32 = jnp.float32


def mm(a, b):
    return jnp.dot(a, b, preferred_element_type=F32)


def mm_t(a, b):
    return lax.dot_general(a, b, (((0,), (0,)), ((), ())), preferred_element_type=F32)


def local(right_side, inverse_blocks, coupling, update_rows):
    leaves = lax.axis_size("leaf")
    blocks = lax.axis_size("blk")
    depth = leaves.bit_length() - 1
    leaf_id = lax.axis_index("leaf")
    core = leaf_id & 1
    width = inverse_blocks.shape[-1]
    half = width // 2
    cases = right_side.shape[-1]
    rhs = right_side[0, 0]
    inverse = inverse_blocks[0, 0]
    couple = coupling[0, 0]
    counts = [width // (blocks << level) for level in range(depth + 1)]
    starts = [sum(counts[:level]) for level in range(depth + 1)]
    couple_starts = {}
    cursor = 0
    for level in range(depth):
        for above in range(level + 1, depth + 1):
            couple_starts[level, above] = cursor
            cursor += counts[level]
    pair_bases = []
    cursor = 0
    for level in range(depth + 1):
        pair_bases.append(cursor)
        cursor += (leaves >> level) * (depth - level)

    def core_order(rows, level):
        chunk = blocks * counts[level]
        member = rows // chunk
        upper = member >> 1
        side = (member & 1) ^ core
        return (side * (1 << (level - 1)) + upper) * chunk + rows % chunk

    def inverse_halves(level):
        rows = inverse[starts[level] : starts[level] + counts[level]]
        parts = rows.reshape(counts[level], 1 << (level - 1), 2, blocks * counts[level])
        mine = lax.dynamic_index_in_dim(parts, core, 2, keepdims=False)
        other = lax.dynamic_index_in_dim(parts, 1 - core, 2, keepdims=False)
        return mine.reshape(-1, half), other.reshape(-1, half)

    def expanded(level, above):
        begin = couple_starts[level, above]
        block = couple[begin : begin + counts[level]]
        node = leaf_id >> level
        pair = pair_bases[level] + node * (depth - level) + (above - level - 1)
        listed = lax.dynamic_index_in_dim(update_rows, pair, 0, keepdims=False)
        listed = core_order(listed, above)
        chosen = listed[:, None] == lax.broadcasted_iota(jnp.int32, (1, width), 1)
        return mm(block, chosen.astype(BF16)).astype(BF16)

    def swap_cores(value):
        pairs = [(i, i ^ 1) for i in range(leaves)]
        return lax.ppermute(value, "leaf", pairs)

    def exchange(value, level):
        if level <= 1:
            return lax.all_to_all(value, "blk", 0, 0, tiled=True)
        groups = []
        for node in range(leaves >> level):
            for side in range(2):
                groups.append(
                    [
                        ((node << level) + 2 * upper + side) * blocks + b
                        for upper in range(1 << (level - 1))
                        for b in range(blocks)
                    ]
                )
        return lax.all_to_all(
            value, ("leaf", "blk"), 0, 0, axis_index_groups=groups, tiled=True
        )

    def reduce_rows(mine, other, level):
        received = swap_cores(other.astype(BF16))
        summed = (mine + received.astype(F32)).astype(BF16)
        parts = exchange(summed, level)
        return parts.reshape(-1, counts[level], cases).astype(F32).sum(0)

    def gather_rows(rows, level):
        copies = (1 << max(level - 1, 0)) * blocks
        spread = jnp.broadcast_to(rows[None], (copies,) + rows.shape)
        return exchange(spread.reshape(-1, cases), level)

    def own_rhs(level):
        return rhs[starts[level] : starts[level] + counts[level]]

    dense = {}
    for level in range(depth):
        for above in range(level + 1, depth + 1):
            dense[level, above] = expanded(level, above)
    halves = {level: inverse_halves(level) for level in range(1, depth + 1)}

    solved_y = []
    for level in range(depth + 1):
        if level == 0:
            full = gather_rows(own_rhs(0).astype(BF16), 0)
            y = mm(inverse[: counts[0]], full)
        else:
            total = 0.0
            for below in range(level):
                total = total + mm_t(dense[below, level], solved_y[below].astype(BF16))
            residual = own_rhs(level) - reduce_rows(total[:half], total[half:], level)
            mine = gather_rows(residual.astype(BF16), level)
            other = swap_cores(mine)
            y = mm(halves[level][0], mine) + mm(halves[level][1], other)
        solved_y.append(y)

    solved = {}
    outputs = [None] * (depth + 1)
    for level in range(depth, -1, -1):
        z = solved_y[level]
        for above in range(level + 1, depth + 1):
            mine, other = solved[above]
            block = dense[level, above]
            z = z - mm(block[:, :half], mine) - mm(block[:, half:], other)
        z = z.astype(BF16)
        if level == 0:
            parts = exchange(mm_t(inverse[: counts[0]], z).astype(BF16), 0)
            outputs[0] = parts.reshape(-1, counts[0], cases).astype(F32).sum(0)
        else:
            x_mine = mm_t(halves[level][0], z)
            x_other = mm_t(halves[level][1], z)
            rows = reduce_rows(x_mine, x_other, level)
            outputs[level] = rows
            mine = gather_rows(rows.astype(BF16), level)
            solved[level] = (mine, swap_cores(mine))
    return jnp.concatenate(outputs, 0)[None, None]


def solution(mesh):
    spec = P("leaf", "blk", None, None)
    return jax.shard_map(
        local, mesh=mesh, in_specs=(spec, spec, spec, P()), out_specs=spec, check_vma=False
    )
```

```python
import jax
import jax.numpy as jnp
from jax import lax
from jax.sharding import PartitionSpec as P


BF16 = jnp.bfloat16
F32 = jnp.float32


def mm(a, b):
    return jnp.dot(a, b, preferred_element_type=F32)


def mm_tn(a, b):
    return lax.dot_general(a, b, (((0,), (0,)), ((), ())), preferred_element_type=F32)


def mm_nt(a, b):
    return lax.dot_general(a, b, (((1,), (1,)), ((), ())), preferred_element_type=F32)


class Level:
    def __init__(self, level, leaves, blocks, width, cases):
        self.level = level
        self.pair_x = 2 if level >= 2 else 1
        self.his = (1 << level) // (2 * self.pair_x)
        self.zbs = blocks // 2
        self.rows = width // (blocks << level)
        self.cells = self.his * self.zbs
        self.cell_rows = width // self.cells
        self.chunk = cases // (4 * self.pair_x)
        self.shape = (self.his, self.pair_x, 2, self.zbs, 2, self.rows)
        outer = []
        inner = []
        for node in range(leaves >> level):
            base = node << level
            for side in range(2):
                outer.append(
                    [
                        (base + 2 * upper + side) * blocks + b
                        for upper in range(1 << (level - 1))
                        for b in range(blocks)
                    ]
                )
                for xu in range(self.pair_x):
                    for yb in range(2):
                        inner.append(
                            [
                                (base + (hi * self.pair_x + xu) * 2 + side) * blocks + 2 * zb + yb
                                for hi in range(self.his)
                                for zb in range(self.zbs)
                            ]
                        )
        self.outer = outer
        self.inner = inner
        self.inner_blk = [[2 * zb + yb for zb in range(self.zbs)] for yb in range(2)]


def local(right_side, inverse_blocks, coupling, update_rows):
    leaves = lax.axis_size("leaf")
    blocks = lax.axis_size("blk")
    depth = leaves.bit_length() - 1
    leaf_id = lax.axis_index("leaf")
    blk_id = lax.axis_index("blk")
    core = leaf_id & 1
    yb = blk_id & 1
    zb = blk_id >> 1
    width = inverse_blocks.shape[-1]
    cases = right_side.shape[-1]
    rhs = right_side[0, 0]
    inverse = inverse_blocks[0, 0]
    couple = coupling[0, 0]
    counts = [width // (blocks << level) for level in range(depth + 1)]
    starts = [sum(counts[:level]) for level in range(depth + 1)]
    levels = [None] + [Level(l, leaves, blocks, width, cases) for l in range(1, depth + 1)]
    couple_starts = {}
    cursor = 0
    for level in range(depth):
        for above in range(level + 1, depth + 1):
            couple_starts[level, above] = cursor
            cursor += counts[level]
    pair_bases = []
    cursor = 0
    for level in range(depth + 1):
        pair_bases.append(cursor)
        cursor += (leaves >> level) * (depth - level)

    def xu_of(level):
        return (leaf_id >> 1) & 1 if levels[level].pair_x == 2 else 0

    def hi_of(level):
        member = leaf_id & ((1 << level) - 1)
        return member // (2 * levels[level].pair_x)

    def swap_core(value):
        return lax.ppermute(value, "leaf", [(i, i ^ 1) for i in range(leaves)])

    def swap_x(value):
        return lax.ppermute(value, "leaf", [(i, i ^ 2) for i in range(leaves)])

    def swap_y(value):
        return lax.ppermute(value, "blk", [(i, i ^ 1) for i in range(blocks)])

    def replicate(value, level):
        value = jnp.concatenate([value, swap_y(value)], 0)
        if levels[level].pair_x == 2:
            value = jnp.concatenate([value, swap_x(value)], 0)
        return jnp.concatenate([value, swap_core(value)], 0)

    def cell_position(rows, level):
        info = levels[level]
        t = rows % (2 * info.rows)
        block = rows // (2 * info.rows)
        zpos = block % info.zbs
        block = block // info.zbs
        side = block % (2 * info.pair_x)
        hi = block // (2 * info.pair_x)
        cell = hi * info.zbs + zpos
        return (cell * (2 * info.pair_x) + side) * (2 * info.rows) + t

    def cell_columns(rows, level):
        info = levels[level]
        parts = rows.reshape(-1, info.his, 2 * info.pair_x, info.zbs, 2 * info.rows)
        return parts.transpose(0, 1, 3, 2, 4).reshape(-1, width)

    def own_position(level):
        info = levels[level]
        side = xu_of(level) * 2 + core
        cell = hi_of(level) * info.zbs + zb
        return ((cell * 2 * info.pair_x + side) * 2 + yb) * info.rows

    def exchange_outer(value, level):
        if level <= 1:
            return lax.all_to_all(value, "blk", 0, 0, tiled=True)
        return lax.all_to_all(
            value, ("leaf", "blk"), 0, 0, axis_index_groups=levels[level].outer, tiled=True
        )

    def exchange_inner(value, level):
        info = levels[level]
        if info.his == 1:
            return lax.all_to_all(
                value, "blk", 0, 0, axis_index_groups=info.inner_blk, tiled=True
            )
        return lax.all_to_all(
            value, ("leaf", "blk"), 0, 0, axis_index_groups=info.inner, tiled=True
        )

    def expanded(block, level, above):
        node = leaf_id >> level
        pair = pair_bases[level] + node * (depth - level) + (above - level - 1)
        listed = lax.dynamic_index_in_dim(update_rows, pair, 0, keepdims=False)
        listed = cell_position(listed, above)
        chosen = listed[:, None] == lax.broadcasted_iota(jnp.int32, (1, width), 1)
        return mm(block, chosen.astype(BF16)).astype(BF16)

    def own_rhs(level):
        return rhs[starts[level] : starts[level] + counts[level]]

    cell_inverse = {}
    dense = {}
    for level in range(1, depth + 1):
        rows = inverse[starts[level] : starts[level] + counts[level]]
        cell_inverse[level] = replicate(cell_columns(rows, level), level)
        for above in range(level + 1, depth + 1):
            begin = couple_starts[level, above]
            block = replicate(couple[begin : begin + counts[level]], level)
            dense[level, above] = expanded(block, level, above)
    placed = {}
    for above in range(1, depth + 1):
        begin = couple_starts[0, above]
        dense[0, above] = expanded(couple[begin : begin + counts[0]], 0, above)
        spots = own_position(above) + lax.broadcasted_iota(jnp.int32, (counts[above], 1), 0)
        spots = spots == lax.broadcasted_iota(jnp.int32, (1, width), 1)
        placed[above] = jnp.concatenate([-dense[0, above], spots.astype(BF16)], 0)

    spread = jnp.broadcast_to(own_rhs(0).astype(BF16)[None], (blocks, counts[0], cases))
    full = lax.all_to_all(spread, "blk", 0, 0, tiled=True).reshape(width, cases)
    y0 = mm(inverse[: counts[0]], full)
    y0_round = y0.astype(BF16)
    base = {}
    for above in range(1, depth + 1):
        known = jnp.concatenate([y0_round, own_rhs(above).astype(BF16)], 0)
        part = mm_tn(known, placed[above]).reshape(2, 2, cases // 4, width)
        mine = lax.dynamic_index_in_dim(part, core, 1, keepdims=False)
        other = lax.dynamic_index_in_dim(part, 1 - core, 1, keepdims=False)
        base[above] = (mine, swap_core(other.astype(BF16)))

    ys = {}
    for level in range(1, depth + 1):
        info = levels[level]
        mine, received = base[level]
        total = mine + received.astype(F32)
        total = total.reshape(2, info.pair_x, info.chunk, width)
        for below in range(1, level):
            term = mm(ys[below].astype(BF16), dense[below, level])
            if levels[below].pair_x == info.pair_x:
                term = term[None]
                hits = lax.broadcasted_iota(jnp.int32, (info.pair_x, 1, 1), 0) == xu_of(level)
                term = jnp.where(hits, term, 0.0)
            else:
                term = term.reshape(info.pair_x, info.chunk, width)
            hits = lax.broadcasted_iota(jnp.int32, (2, 1, 1, 1), 0) == yb
            total = total - jnp.where(hits, term[None], 0.0)
        parts = total.astype(BF16).reshape(
            2, info.pair_x, info.chunk, info.his, info.zbs, info.cell_rows
        )
        parts = parts.transpose(3, 1, 4, 0, 2, 5).reshape(-1, info.chunk, info.cell_rows)
        parts = exchange_outer(parts, level)
        residual = parts.astype(F32).sum(0).astype(BF16)
        spread = jnp.broadcast_to(residual[None], (info.cells,) + residual.shape)
        gathered = exchange_inner(spread, level)
        gathered = gathered.transpose(1, 0, 2).reshape(info.chunk, width)
        ys[level] = mm_nt(gathered, cell_inverse[level])

    xs = {}
    for level in range(depth, 0, -1):
        info = levels[level]
        z = ys[level]
        for above in range(level + 1, depth + 1):
            picked = lax.dynamic_index_in_dim(xs[above], yb, 0, keepdims=False)
            if info.pair_x == levels[above].pair_x:
                picked = lax.dynamic_index_in_dim(picked, xu_of(level), 0, keepdims=False)
            picked = picked.reshape(info.chunk, width)
            z = z - mm_nt(picked, dense[level, above])
        part = mm(z.astype(BF16), cell_inverse[level]).astype(BF16)
        part = part.reshape(info.chunk, info.cells, info.cell_rows).transpose(1, 0, 2)
        part = exchange_inner(part, level)
        rows = part.astype(F32).sum(0).astype(BF16)
        spread = jnp.broadcast_to(
            rows[None], (info.cells * info.pair_x * 2,) + rows.shape
        )
        gathered = exchange_outer(spread, level)
        gathered = gathered.reshape(
            info.his, info.pair_x, info.zbs, 2, info.chunk, info.cell_rows
        )
        xs[level] = gathered.transpose(3, 1, 4, 0, 2, 5).reshape(
            2, info.pair_x, info.chunk, width
        )

    z0 = y0
    outputs = [None] * (depth + 1)
    for above in range(depth, 0, -1):
        mine = xs[above].reshape(2, cases // 4, width)
        other = swap_core(mine)
        both = jnp.where(
            core == 0, jnp.stack([mine, other], 1), jnp.stack([other, mine], 1)
        ).reshape(cases, width)
        z0 = z0 - mm_nt(dense[0, above], both)
        rows = lax.dynamic_slice_in_dim(both, own_position(above), counts[above], 1)
        outputs[above] = rows.T.astype(F32)
    part = mm_tn(inverse[: counts[0]], z0.astype(BF16)).astype(BF16)
    parts = lax.all_to_all(part, "blk", 0, 0, tiled=True)
    outputs[0] = parts.reshape(-1, counts[0], cases).astype(F32).sum(0)
    return jnp.concatenate(outputs, 0)[None, None]


def solution(mesh):
    spec = P("leaf", "blk", None, None)
    return jax.shard_map(
        local, mesh=mesh, in_specs=(spec, spec, spec, P()), out_specs=spec, check_vma=False
    )
```

```python
import functools

import jax
import jax.numpy as jnp
from jax import lax
from jax.experimental import pallas as pl
from jax.experimental.pallas import tpu as pltpu
from jax.sharding import PartitionSpec as P


BF16 = jnp.bfloat16
F32 = jnp.float32


def mm(a, b):
    return jnp.dot(a, b, preferred_element_type=F32)


def mm_tn(a, b):
    return lax.dot_general(a, b, (((0,), (0,)), ((), ())), preferred_element_type=F32)


def mm_nt(a, b):
    return lax.dot_general(a, b, (((1,), (1,)), ((), ())), preferred_element_type=F32)


def shaped(shape, dtype):
    return jax.ShapeDtypeStruct(tuple(shape), dtype)


def kernel_call(body, outs, args, scalars=None, scratch=(), flops=0):
    moved = sum(a.size * a.dtype.itemsize for a in args)
    moved += sum(o.size * o.dtype.itemsize for o in outs)
    specs = [pl.BlockSpec(memory_space=pltpu.VMEM)] * len(args)
    if scalars is not None:
        specs = [pl.BlockSpec(memory_space=pltpu.SMEM)] + specs
        args = [scalars] + list(args)
    return pl.pallas_call(
        body,
        out_shape=list(outs),
        in_specs=specs,
        out_specs=[pl.BlockSpec(memory_space=pltpu.VMEM)] * len(outs),
        scratch_shapes=list(scratch),
        cost_estimate=pl.CostEstimate(flops=flops, bytes_accessed=moved, transcendentals=0),
    )(*args)


class Level:
    def __init__(self, level, leaves, blocks, width, cases):
        self.pair_x = 2 if level >= 2 else 1
        self.his = (1 << level) // (2 * self.pair_x)
        self.zbs = blocks // 2
        self.rows = width // (blocks << level)
        self.cells = self.his * self.zbs
        self.cell_rows = width // self.cells
        self.chunk = cases // (4 * self.pair_x)
        self.targets = self.cells * self.pair_x * 2
        outer = []
        inner = []
        for node in range(leaves >> level):
            base = node << level
            for side in range(2):
                outer.append(
                    [
                        (base + 2 * upper + side) * blocks + b
                        for upper in range(1 << (level - 1))
                        for b in range(blocks)
                    ]
                )
                for xu in range(self.pair_x):
                    for yb in range(2):
                        inner.append(
                            [
                                (base + (hi * self.pair_x + xu) * 2 + side) * blocks + 2 * zb + yb
                                for hi in range(self.his)
                                for zb in range(self.zbs)
                            ]
                        )
        self.outer = outer
        self.inner = inner
        self.inner_blk = [[2 * zb + yb for zb in range(self.zbs)] for yb in range(2)]

    def target(self, hi, xu, zb, yb):
        return ((hi * self.pair_x + xu) * self.zbs + zb) * 2 + yb

    def lanes(self, cell):
        return slice(cell * self.cell_rows, (cell + 1) * self.cell_rows)

    def all_targets(self):
        for hi in range(self.his):
            for xu in range(self.pair_x):
                for zb in range(self.zbs):
                    for yb in range(2):
                        yield hi * self.zbs + zb, xu, yb, self.target(hi, xu, zb, yb)


CORE, YB, XU, SPOT = 0, 1, 2, 3


def expand_kernel(count, spots_ref, *refs):
    blocks, outs = refs[:count], refs[count:]
    width = outs[0].shape[-1]
    step = min(512, width)
    for pair in range(len(outs)):
        listed = spots_ref[pair : pair + 1, :]
        mine = blocks if len(outs) == 1 else (blocks[pair],)
        for begin in range(0, width, step):
            ids = begin + lax.broadcasted_iota(jnp.int32, (step, listed.shape[-1]), 0)
            chosen = jnp.where(ids == listed, 1.0, 0.0).astype(BF16)
            for piece, block in enumerate(mine):
                value = mm_nt(block[...], chosen).astype(BF16)
                outs[pair][piece, :, begin : begin + step] = value


def subtree_kernel(infos, starts, at, full, inverse, rhs, *refs):
    depth = len(infos)
    dense, outs, total = refs[:depth], refs[depth:-1], refs[-1]
    y = mm(inverse[...], full[...])
    outs[0][...] = y
    y_round = y.astype(BF16)
    for n, info in enumerate(infos):
        begin = starts[n]
        own = rhs[begin : begin + info.rows, :].astype(BF16)
        width = info.cells * info.cell_rows
        row_ids = at[SPOT + n] + lax.broadcasted_iota(jnp.int32, (info.rows, width), 0)
        lane_ids = lax.broadcasted_iota(jnp.int32, (info.rows, width), 1)
        spots = jnp.where(row_ids == lane_ids, 1.0, 0.0).astype(BF16)
        total[...] = mm_tn(own, spots) - mm_tn(y_round, dense[n][0])
        mine, other = outs[1 + 2 * n], outs[2 + 2 * n]
        core = at[CORE]
        for cell, xu, yb, target in info.all_targets():
            for side, ref in ((core, mine), (1 - core, other)):
                row = ((yb * 2 + side) * info.pair_x + xu) * info.chunk
                row = pl.multiple_of(row, info.chunk)
                value = total[pl.ds(row, info.chunk), info.lanes(cell)]
                ref[target] = value.astype(ref.dtype)


def sum_spread_kernel(parts, out):
    total = parts[0].astype(F32)
    for n in range(1, parts.shape[0]):
        total = total + parts[n].astype(F32)
    rounded = total.astype(BF16)
    for n in range(out.shape[0]):
        out[n] = rounded


def solve_pieces(info, gathered, pieces):
    ys = []
    for piece in pieces:
        y = None
        for cell in range(info.cells):
            term = mm_nt(gathered[cell], piece[:, info.lanes(cell)])
            y = term if y is None else y + term
        ys.append(y)
    return ys


def forward_kernel(infos, k, at, gathered, mine, received, *refs):
    info, above = infos[k - 1], infos[k]
    count = 4 * info.pair_x
    pieces = refs[:count]
    lower_y = refs[count : count + k - 1]
    dense = refs[count + k - 1 : count + 2 * k - 1]
    y_ref, out, total = refs[count + 2 * k - 1 :]
    ys = solve_pieces(info, gathered, pieces)
    for n, y in enumerate(ys):
        y_ref[n] = y
    same = {}
    for j in range(1, k + 1):
        lower = infos[j - 1]
        values = ys if j == k else [lower_y[j - 1][n] for n in range(4 * lower.pair_x)]
        term = None
        for n, value in enumerate(values):
            product = mm(value.astype(BF16), dense[j - 1][n])
            term = product if term is None else term + product
        same.setdefault(lower.pair_x == above.pair_x, []).append(term)
    if False in same:
        total[...] = functools.reduce(jnp.add, same[False])
    else:
        total[...] = jnp.zeros(total.shape, F32)
    if True in same:
        term = functools.reduce(jnp.add, same[True])
        rows = pl.ds(pl.multiple_of(at[XU] * above.chunk, above.chunk), above.chunk)
        total[rows, :] = total[rows, :] + term
    for cell, xu, yb, target in above.all_targets():
        value = mine[target] + received[target].astype(F32)
        minus = total[xu * above.chunk : (xu + 1) * above.chunk, above.lanes(cell)]
        value = jnp.where(at[YB] == yb, value - minus, value)
        out[target] = value.astype(BF16)


def spread_product(info, zs, pieces, out):
    for cell in range(info.cells):
        total = None
        for z, piece in zip(zs, pieces):
            term = mm(z, piece[:, info.lanes(cell)])
            total = term if total is None else total + term
        out[cell] = total.astype(BF16)


def top_kernel(info, gathered, *refs):
    pieces, out = refs[:-1], refs[-1]
    ys = solve_pieces(info, gathered, pieces)
    spread_product(info, [y.astype(BF16) for y in ys], pieces, out)


def backward_kernel(infos, k, at, y, *refs):
    info = infos[k - 1]
    count = 4 * info.pair_x
    uppers = infos[k:]
    pieces = refs[:count]
    solved = refs[count : count + len(uppers)]
    dense = refs[count + len(uppers) : count + 2 * len(uppers)]
    out = refs[-1]
    zs = [y[n] for n in range(count)]
    for n_up, above in enumerate(uppers):
        for hi in range(above.his):
            for zb in range(above.zbs):
                cell = hi * above.zbs + zb
                if above.pair_x == info.pair_x:
                    slot = ((hi * above.pair_x + at[XU]) * above.zbs + zb) * 2 + at[YB]
                    picked = solved[n_up][slot]
                else:
                    slots = [
                        above.target(hi, xu, zb, 0) + at[YB] for xu in range(above.pair_x)
                    ]
                    picked = jnp.concatenate([solved[n_up][slot] for slot in slots], 0)
                for n in range(count):
                    zs[n] = zs[n] - mm_nt(picked, dense[n_up][n, :, above.lanes(cell)])
    spread_product(info, [z.astype(BF16) for z in zs], pieces, out)


def last_kernel(infos, at, y, inverse, *refs):
    depth = len(infos)
    dense = refs[:depth]
    mine = refs[depth : 2 * depth]
    other = refs[2 * depth : 3 * depth]
    out, full = refs[3 * depth :]
    z = y[...]
    core = at[CORE]
    for n in range(depth - 1, -1, -1):
        info = infos[n]
        for cell, xu, yb, target in info.all_targets():
            for side, ref in ((core, mine[n]), (1 - core, other[n])):
                row = ((yb * 2 + side) * info.pair_x + xu) * info.chunk
                row = pl.multiple_of(row, info.chunk)
                full[pl.ds(row, info.chunk), info.lanes(cell)] = ref[target]
        z = z - mm_nt(dense[n][0], full[...])
    out[...] = mm_tn(inverse[...], z.astype(BF16)).astype(BF16)


def solve(right_side, inverse_blocks, coupling, update_rows):
    leaves = lax.axis_size("leaf")
    blocks = lax.axis_size("blk")
    depth = leaves.bit_length() - 1
    leaf_id = lax.axis_index("leaf")
    blk_id = lax.axis_index("blk")
    core = leaf_id & 1
    yb = blk_id & 1
    zb = blk_id >> 1
    width = inverse_blocks.shape[-1]
    cases = right_side.shape[-1]
    rhs = right_side[0, 0]
    inverse = inverse_blocks[0, 0]
    couple = coupling[0, 0]
    listed_rows = coupling.shape[-1]
    counts = [width // (blocks << level) for level in range(depth + 1)]
    starts = [sum(counts[:level]) for level in range(depth + 1)]
    infos = [Level(l, leaves, blocks, width, cases) for l in range(1, depth + 1)]
    couple_starts = {}
    cursor = 0
    for level in range(depth):
        for above in range(level + 1, depth + 1):
            couple_starts[level, above] = cursor
            cursor += counts[level]
    pair_bases = []
    cursor = 0
    for level in range(depth + 1):
        pair_bases.append(cursor)
        cursor += (leaves >> level) * (depth - level)

    def own_position(level):
        info = infos[level - 1]
        member = leaf_id & ((1 << level) - 1)
        side = member & (2 * info.pair_x - 1)
        cell = member // (2 * info.pair_x) * info.zbs + zb
        return ((cell * 2 * info.pair_x + side) * 2 + yb) * info.rows

    at = jnp.stack(
        [core, yb, (leaf_id >> 1) & 1] + [own_position(l) for l in range(1, depth + 1)]
    ).astype(jnp.int32)

    def swap(value, axis, bit):
        size = leaves if axis == "leaf" else blocks
        return lax.ppermute(value, axis, [(i, i ^ bit) for i in range(size)])

    def cell_position(rows, level):
        info = infos[level - 1]
        t = rows % (2 * info.rows)
        block = rows // (2 * info.rows)
        zpos = block % info.zbs
        block = block // info.zbs
        side = block % (2 * info.pair_x)
        cell = block // (2 * info.pair_x) * info.zbs + zpos
        return (cell * (2 * info.pair_x) + side) * (2 * info.rows) + t

    def cell_columns(rows, level):
        info = infos[level - 1]
        parts = rows.reshape(-1, info.his, 2 * info.pair_x, info.zbs, 2 * info.rows)
        return parts.transpose(0, 1, 3, 2, 4).reshape(-1, width)

    def exchange_outer(value, level):
        if level <= 1:
            return lax.all_to_all(value, "blk", 0, 0, tiled=True)
        return lax.all_to_all(
            value,
            ("leaf", "blk"),
            0,
            0,
            axis_index_groups=infos[level - 1].outer,
            tiled=True,
        )

    def exchange_inner(value, level):
        info = infos[level - 1]
        if info.his == 1:
            return lax.all_to_all(
                value, "blk", 0, 0, axis_index_groups=info.inner_blk, tiled=True
            )
        return lax.all_to_all(
            value, ("leaf", "blk"), 0, 0, axis_index_groups=info.inner, tiled=True
        )

    def positions(level, above):
        node = leaf_id >> level
        pair = pair_bases[level] + node * (depth - level) + (above - level - 1)
        listed = lax.dynamic_index_in_dim(update_rows, pair, 0, keepdims=True)
        return cell_position(listed, above)

    def coupling_block(level, above):
        begin = couple_starts[level, above]
        return couple[begin : begin + counts[level]]

    uppers = range(1, depth + 1)
    lists = jnp.concatenate([positions(0, above) for above in uppers], 0)
    dense = {}
    expanded = kernel_call(
        functools.partial(expand_kernel, depth),
        [shaped((1, counts[0], width), BF16)] * depth,
        [lists] + [coupling_block(0, above) for above in uppers],
        flops=2 * depth * counts[0] * listed_rows * width,
    )
    for above in uppers:
        dense[0, above] = expanded[above - 1]

    spread = jnp.broadcast_to(rhs[: counts[0]].astype(BF16)[None], (blocks, counts[0], cases))
    full = lax.all_to_all(spread, "blk", 0, 0, tiled=True).reshape(width, cases)
    subtree_inverse = inverse[: counts[0]]
    outs = [shaped((counts[0], cases), F32)]
    for info in infos:
        shape = (info.targets, info.chunk, info.cell_rows)
        outs += [shaped(shape, F32), shaped(shape, BF16)]
    y0, *base = kernel_call(
        functools.partial(subtree_kernel, infos, starts[1:]),
        outs,
        [full, subtree_inverse, rhs] + [dense[0, above] for above in uppers],
        scalars=at,
        scratch=[pltpu.VMEM((cases, width), F32)],
        flops=2 * (1 + depth) * counts[0] * width * cases,
    )
    received = []
    for level in uppers:
        received.append(swap(base[2 * level - 1], "leaf", 1))

    def pieces_of(value, level):
        pieces = [value, swap(value, "blk", 1)]
        if infos[level - 1].pair_x == 2:
            pieces += [swap(piece, "leaf", 2) for piece in pieces]
        pieces += [swap(piece, "leaf", 1) for piece in pieces]
        return pieces

    inverse_pieces = {}
    for level in uppers:
        rows = inverse[starts[level] : starts[level] + counts[level]]
        rows = cell_columns(rows, level)
        inverse_pieces[level] = pieces_of(rows, level)
        for above in range(level + 1, depth + 1):
            pieces = pieces_of(coupling_block(level, above), level)
            dense[level, above] = kernel_call(
                functools.partial(expand_kernel, len(pieces)),
                [shaped((len(pieces), counts[level], width), BF16)],
                [positions(level, above)] + pieces,
                flops=2 * len(pieces) * counts[level] * listed_rows * width,
            )[0]

    def sum_spread(parts, copies):
        return kernel_call(
            sum_spread_kernel, [shaped((copies,) + parts.shape[1:], BF16)], [parts]
        )[0]

    ys = {}
    parts = (base[0] + received[0].astype(F32)).astype(BF16)
    for level in uppers:
        info = infos[level - 1]
        parts = exchange_outer(parts, level)
        gathered = exchange_inner(sum_spread(parts, info.cells), level)
        size = info.cell_rows * width * info.chunk
        if level == depth:
            parts = kernel_call(
                functools.partial(top_kernel, info),
                [shaped((info.cells, info.chunk, info.cell_rows), BF16)],
                [gathered] + inverse_pieces[level],
                flops=4 * size,
            )[0]
            break
        above = infos[level]
        lowers = [ys[j] for j in range(1, level)]
        ys[level], parts = kernel_call(
            functools.partial(forward_kernel, infos, level),
            [
                shaped((4 * info.pair_x, info.chunk, info.rows), F32),
                shaped((above.targets, above.chunk, above.cell_rows), BF16),
            ],
            [gathered, base[2 * level], received[level]]
            + inverse_pieces[level]
            + lowers
            + [dense[j, level + 1] for j in range(1, level + 1)],
            scalars=at,
            scratch=[pltpu.VMEM((above.chunk * above.pair_x, width), F32)],
            flops=4 * size,
        )

    solved = {}
    swapped = {}
    for level in range(depth, 0, -1):
        info = infos[level - 1]
        if level < depth:
            higher = range(level + 1, depth + 1)
            parts = kernel_call(
                functools.partial(backward_kernel, infos, level),
                [shaped((info.cells, info.chunk, info.cell_rows), BF16)],
                [ys[level]]
                + inverse_pieces[level]
                + [solved[above] for above in higher]
                + [dense[level, above] for above in higher],
                scalars=at,
                flops=4 * info.cell_rows * width * info.chunk,
            )[0]
        parts = exchange_inner(parts, level)
        solved[level] = exchange_outer(sum_spread(parts, info.targets), level)
        swapped[level] = swap(solved[level], "leaf", 1)

    part = kernel_call(
        functools.partial(last_kernel, infos),
        [shaped((width, cases), BF16)],
        [y0, subtree_inverse]
        + [dense[0, above] for above in uppers]
        + [solved[above] for above in uppers]
        + [swapped[above] for above in uppers],
        scalars=at,
        scratch=[pltpu.VMEM((cases, width), BF16)],
        flops=2 * (1 + depth) * counts[0] * width * cases,
    )[0]
    parts = lax.all_to_all(part, "blk", 0, 0, tiled=True)

    outputs = []
    for level in uppers:
        info = infos[level - 1]
        member = leaf_id & ((1 << level) - 1)
        side = member & (2 * info.pair_x - 1)
        hi = member // (2 * info.pair_x)
        offset = (side * 2 + yb) * info.rows

        def own(value):
            shape = (info.his, info.pair_x, info.zbs, 2, info.chunk, info.cell_rows)
            sizes = (1, info.pair_x, 1, 2, info.chunk, info.rows)
            taken = lax.dynamic_slice(value.reshape(shape), (hi, 0, zb, 0, 0, offset), sizes)
            return taken[0, :, 0].transpose(1, 0, 2, 3)

        mine, other = own(solved[level]), own(swapped[level])
        rows = jnp.where(
            core == 0, jnp.stack([mine, other], 1), jnp.stack([other, mine], 1)
        )
        outputs.append(rows.reshape(cases, info.rows).T.astype(F32))
    top = parts.reshape(-1, counts[0], cases).astype(F32).sum(0)
    return jnp.concatenate([top] + outputs, 0)[None, None]


def solution(mesh):
    spec = P("leaf", "blk", None, None)
    return jax.shard_map(
        solve, mesh=mesh, in_specs=(spec, spec, spec, P()), out_specs=spec, check_vma=False
    )
```

```python
import functools

import jax
import jax.numpy as jnp
from jax import lax
from jax.experimental import pallas as pl
from jax.experimental.pallas import tpu as pltpu
from jax.sharding import PartitionSpec as P


BF16 = jnp.bfloat16
F32 = jnp.float32


def mm(a, b):
    return jnp.dot(a, b, preferred_element_type=F32)


def mm_tn(a, b):
    return lax.dot_general(a, b, (((0,), (0,)), ((), ())), preferred_element_type=F32)


def mm_nt(a, b):
    return lax.dot_general(a, b, (((1,), (1,)), ((), ())), preferred_element_type=F32)


def shaped(shape, dtype):
    return jax.ShapeDtypeStruct(tuple(shape), dtype)


def kernel_call(body, outs, args, scalars=None, scratch=(), flops=0):
    values = []
    specs = []
    moved = sum(o.size * o.dtype.itemsize for o in outs)
    for arg in args:
        value, spec = arg if isinstance(arg, tuple) else (arg, pl.BlockSpec(memory_space=pltpu.VMEM))
        if spec is None:
            value = pltpu.with_memory_space_constraint(value, pltpu.HBM)
            spec = pl.BlockSpec(memory_space=pltpu.HBM)
        values.append(value)
        specs.append(spec)
        moved += value.size * value.dtype.itemsize
    if scalars is not None:
        specs = [pl.BlockSpec(memory_space=pltpu.SMEM)] + specs
        values = [scalars] + values
    return pl.pallas_call(
        body,
        out_shape=[pltpu.HBM(o.shape, o.dtype) for o in outs],
        in_specs=specs,
        out_specs=[pl.BlockSpec(memory_space=pltpu.VMEM)] * len(outs),
        scratch_shapes=list(scratch),
        compiler_params=pltpu.CompilerParams(vmem_limit_bytes=16 << 20),
        cost_estimate=pl.CostEstimate(flops=flops, bytes_accessed=moved, transcendentals=0),
    )(*values)


def hbm(values):
    return [(value, None) for value in values]


class Loads:
    def __init__(self, sems):
        self.sems = sems
        self.used = 0

    def start(self, pairs):
        copies = []
        for source, target in pairs:
            copies.append(pltpu.make_async_copy(source, target, self.sems.at[self.used]))
            copies[-1].start()
            self.used += 1
        return copies

    def rows(self, sources, target):
        pairs = []
        begin = 0
        for source in sources:
            count = source.shape[0]
            pairs.append((source, target.at[begin : begin + count, :]))
            begin += count
        return self.start(pairs)


def wait(copies):
    for copy in copies:
        copy.wait()


def split_power(value, size):
    bits = size.bit_length() - 1
    if size == 1 << bits:
        return value >> bits, value & (size - 1)
    return value // size, value % size


class Level:
    def __init__(self, level, leaves, blocks, width, cases):
        self.pair_x = 2 if level >= 2 else 1
        self.his = (1 << level) // (2 * self.pair_x)
        self.zbs = blocks // 2
        self.rows = width // (blocks << level)
        self.cells = self.his * self.zbs
        self.cell_rows = width // self.cells
        self.chunk = cases // (4 * self.pair_x)
        self.targets = self.cells * self.pair_x * 2
        outer = []
        inner = []
        for node in range(leaves >> level):
            base = node << level
            for side in range(2):
                outer.append(
                    [
                        (base + 2 * upper + side) * blocks + b
                        for upper in range(1 << (level - 1))
                        for b in range(blocks)
                    ]
                )
                for xu in range(self.pair_x):
                    for yb in range(2):
                        inner.append(
                            [
                                (base + (hi * self.pair_x + xu) * 2 + side) * blocks + 2 * zb + yb
                                for hi in range(self.his)
                                for zb in range(self.zbs)
                            ]
                        )
        self.outer = outer
        self.inner = inner
        self.inner_blk = [[2 * zb + yb for zb in range(self.zbs)] for yb in range(2)]

    @property
    def direct(self):
        return (2 * self.rows) % 128 == 0

    def natural(self):
        if not self.direct:
            return [(c * self.cell_rows, c, 0, self.cell_rows) for c in range(self.cells)]
        size = 2 * self.rows
        return [
            (
                ((hi * 2 * self.pair_x + side) * self.zbs + zb) * size,
                hi * self.zbs + zb,
                side * size,
                size,
            )
            for hi in range(self.his)
            for side in range(2 * self.pair_x)
            for zb in range(self.zbs)
        ]

    def position(self, rows):
        block, t = split_power(rows, 2 * self.rows)
        block, zpos = split_power(block, self.zbs)
        hi, side = split_power(block, 2 * self.pair_x)
        cell = hi * self.zbs + zpos
        return (cell * (2 * self.pair_x) + side) * (2 * self.rows) + t

    def target(self, hi, xu, zb, yb):
        return ((hi * self.pair_x + xu) * self.zbs + zb) * 2 + yb

    def lanes(self, cell):
        return slice(cell * self.cell_rows, (cell + 1) * self.cell_rows)

    def all_targets(self):
        for hi in range(self.his):
            for xu in range(self.pair_x):
                for zb in range(self.zbs):
                    for yb in range(2):
                        yield hi * self.zbs + zb, xu, yb, self.target(hi, xu, zb, yb)


CORE, YB, XU, SPOT = 0, 1, 2, 3


def first_kernel(rhs, out):
    rounded = rhs[0 : out.shape[1], :].astype(BF16)
    for n in range(out.shape[0]):
        out[n] = rounded


def expand_kernel(count, aboves, slots, begins, at, lists, *refs):
    blocks, outs = refs[:count], refs[count:]
    width = outs[0].shape[-1]
    step = min(512, width)
    for n, (info, out) in enumerate(zip(aboves, outs)):
        listed = info.position(lists[pl.ds(at[slots[n]], 1), :])
        if begins is None:
            block = jnp.concatenate([b[...] for b in blocks], 0)
        else:
            block = blocks[0][begins[n] : begins[n] + out.shape[0], :]
        for begin in range(0, width, step):
            ids = begin + lax.broadcasted_iota(jnp.int32, (step, listed.shape[-1]), 0)
            chosen = jnp.where(ids == listed, 1.0, 0.0).astype(BF16)
            out[:, begin : begin + step] = mm_nt(block, chosen).astype(BF16)


def subtree_kernel(infos, starts, at, full, inverse, rhs, *refs):
    depth = len(infos)
    sources = refs[:depth]
    outs = refs[depth : depth + 1 + 2 * depth]
    total, matrix, dense, sems = refs[depth + 1 + 2 * depth :]
    loads = Loads(sems)
    first = loads.start([(inverse.at[0 : matrix.shape[0], :], matrix)])
    later = [loads.start([(sources[n], dense.at[n])]) for n in range(depth)]
    core = at[CORE]
    width = total.shape[-1]
    placed = []
    for n, info in enumerate(infos):
        row_ids = at[SPOT + n] + lax.broadcasted_iota(jnp.int32, (info.rows, width), 0)
        lane_ids = lax.broadcasted_iota(jnp.int32, (info.rows, width), 1)
        spots = jnp.where(row_ids == lane_ids, 1.0, 0.0).astype(BF16)
        own = rhs[starts[n] : starts[n] + info.rows, :].astype(BF16)
        placed.append(mm_tn(own, spots))
    wait(first)
    y = mm(matrix[...], full[...])
    outs[0][...] = y
    y_round = y.astype(BF16)
    for n, info in enumerate(infos):
        wait(later[n])
        total[...] = placed[n] - mm_tn(y_round, dense[n])
        mine, other = outs[1 + 2 * n], outs[2 + 2 * n]
        for cell, xu, yb, target in info.all_targets():
            for side, ref in ((core, mine), (1 - core, other)):
                row = ((yb * 2 + side) * info.pair_x + xu) * info.chunk
                row = pl.multiple_of(row, info.chunk)
                value = total[pl.ds(row, info.chunk), info.lanes(cell)]
                ref[target] = value.astype(ref.dtype)


def sum_spread_kernel(parts, out):
    total = parts[0].astype(F32)
    for n in range(1, parts.shape[0]):
        total = total + parts[n].astype(F32)
    rounded = total.astype(BF16)
    for n in range(out.shape[0]):
        out[n] = rounded


def natural_rows(info, gathered):
    blocks = [
        gathered[cell][:, inside : inside + size]
        for _, cell, inside, size in info.natural()
    ]
    return jnp.concatenate(blocks, 1)


def spread_product(info, z, matrix, out):
    value = mm_tn(z, matrix[...]).astype(BF16)
    for lane, cell, inside, size in info.natural():
        out[cell, :, inside : inside + size] = value[:, lane : lane + size]


def forward_kernel(infos, k, at, gathered, mine, received, *refs):
    info, above = infos[k - 1], infos[k]
    count = 4 * info.pair_x
    pieces = refs[:count]
    lower_y = refs[count : count + k - 1]
    sources = refs[count + k - 1 : count + 2 * k - 1]
    y_ref, out, total, matrix, sems = refs[count + 2 * k - 1 : count + 2 * k + 4]
    dense = refs[count + 2 * k + 4 :]
    loads = Loads(sems)
    first = loads.rows(pieces, matrix)
    later = [loads.start([(source, dense[j])]) for j, source in enumerate(sources)]
    vector = natural_rows(info, gathered)
    wait(first)
    y = mm_nt(matrix[...], vector)
    y_ref[...] = y
    same = {}
    for j in range(1, k + 1):
        wait(later[j - 1])
        value = y if j == k else lower_y[j - 1][...]
        term = mm_tn(value.astype(BF16), dense[j - 1][...])
        same.setdefault(infos[j - 1].pair_x == above.pair_x, []).append(term)
    if False in same:
        total[...] = functools.reduce(jnp.add, same[False])
    else:
        total[...] = jnp.zeros(total.shape, F32)
    if True in same:
        term = functools.reduce(jnp.add, same[True])
        rows = pl.ds(pl.multiple_of(at[XU] * above.chunk, above.chunk), above.chunk)
        total[rows, :] = total[rows, :] + term
    for cell, xu, yb, target in above.all_targets():
        value = mine[target] + received[target].astype(F32)
        minus = total[xu * above.chunk : (xu + 1) * above.chunk, above.lanes(cell)]
        value = jnp.where(at[YB] == yb, value - minus, value)
        out[target] = value.astype(BF16)


def top_kernel(info, gathered, *refs):
    count = 4 * info.pair_x
    pieces = refs[:count]
    out, matrix, sems = refs[count:]
    first = Loads(sems).rows(pieces, matrix)
    vector = natural_rows(info, gathered)
    wait(first)
    y = mm_nt(matrix[...], vector)
    spread_product(info, y.astype(BF16), matrix, out)


def backward_kernel(infos, k, at, y, *refs):
    info = infos[k - 1]
    count = 4 * info.pair_x
    uppers = infos[k:]
    many = len(uppers)
    pieces = refs[:count]
    solved = refs[count : count + many]
    sources = refs[count + many : count + 2 * many]
    out, matrix, sems = refs[count + 2 * many : count + 2 * many + 3]
    dense = refs[count + 2 * many + 3 :]
    loads = Loads(sems)
    first = [loads.start([(source, dense[n])]) for n, source in enumerate(sources)]
    last = loads.rows(pieces, matrix)
    z = y[...]
    for n, above in enumerate(uppers):
        parts = []
        for hi in range(above.his):
            for zb in range(above.zbs):
                if above.pair_x == info.pair_x:
                    slot = ((hi * above.pair_x + at[XU]) * above.zbs + zb) * 2 + at[YB]
                    parts.append(solved[n][slot])
                else:
                    slots = [
                        above.target(hi, xu, zb, 0) + at[YB] for xu in range(above.pair_x)
                    ]
                    parts.append(jnp.concatenate([solved[n][slot] for slot in slots], 0))
        wait(first[n])
        z = z - mm_nt(dense[n][...], jnp.concatenate(parts, 1))
    wait(last)
    spread_product(info, z.astype(BF16), matrix, out)


def last_kernel(infos, at, y, inverse, *refs):
    depth = len(infos)
    sources = refs[:depth]
    mine = refs[depth : 2 * depth]
    other = refs[2 * depth : 3 * depth]
    out, full, matrix, dense, sems = refs[3 * depth :]
    loads = Loads(sems)
    first = {n: loads.start([(sources[n], dense.at[n])]) for n in range(depth - 1, -1, -1)}
    last = loads.start([(inverse.at[0 : matrix.shape[0], :], matrix)])
    z = y[...]
    core = at[CORE]
    for n in range(depth - 1, -1, -1):
        info = infos[n]
        for cell, xu, yb, target in info.all_targets():
            for side, ref in ((core, mine[n]), (1 - core, other[n])):
                row = ((yb * 2 + side) * info.pair_x + xu) * info.chunk
                row = pl.multiple_of(row, info.chunk)
                full[n, pl.ds(row, info.chunk), info.lanes(cell)] = ref[target]
        wait(first[n])
        z = z - mm_nt(dense[n], full[n])
    wait(last)
    value = mm_tn(z.astype(BF16), matrix[...]).astype(BF16)
    size = out.shape[-1]
    for n in range(out.shape[0]):
        out[n] = value[:, n * size : (n + 1) * size]


def output_kernel(parts, *refs):
    rows, out = refs[:-1], refs[-1]
    total = parts[0].astype(F32)
    for n in range(1, parts.shape[0]):
        total = total + parts[n].astype(F32)
    begin = total.shape[1]
    out[0:begin, :] = total.T
    for row in rows:
        out[begin : begin + row.shape[0], :] = row[...].astype(F32)
        begin += row.shape[0]


def solve(right_side, inverse_blocks, coupling, update_rows):
    leaves = lax.axis_size("leaf")
    blocks = lax.axis_size("blk")
    depth = leaves.bit_length() - 1
    leaf_id = lax.axis_index("leaf")
    blk_id = lax.axis_index("blk")
    core = leaf_id & 1
    yb = blk_id & 1
    zb = blk_id >> 1
    width = inverse_blocks.shape[-1]
    cases = right_side.shape[-1]
    rhs = right_side[0, 0]
    inverse = inverse_blocks[0, 0]
    couple = coupling[0, 0]
    listed_rows = coupling.shape[-1]
    counts = [width // (blocks << level) for level in range(depth + 1)]
    starts = [sum(counts[:level]) for level in range(depth + 1)]
    infos = [Level(l, leaves, blocks, width, cases) for l in range(1, depth + 1)]
    couple_starts = {}
    cursor = 0
    for level in range(depth):
        for above in range(level + 1, depth + 1):
            couple_starts[level, above] = cursor
            cursor += counts[level]
    pair_bases = []
    cursor = 0
    for level in range(depth + 1):
        pair_bases.append(cursor)
        cursor += (leaves >> level) * (depth - level)

    def own_position(level):
        info = infos[level - 1]
        member = leaf_id & ((1 << level) - 1)
        side = member & (2 * info.pair_x - 1)
        cell = member // (2 * info.pair_x) * info.zbs + zb
        return ((cell * 2 * info.pair_x + side) * 2 + yb) * info.rows

    pair_slot = {}
    pair_rows = []
    for level in range(depth):
        for above in range(level + 1, depth + 1):
            pair_slot[level, above] = SPOT + depth + len(pair_rows)
            node = leaf_id >> level
            pair_rows.append(pair_bases[level] + node * (depth - level) + (above - level - 1))
    at = jnp.stack(
        [core, yb, (leaf_id >> 1) & 1]
        + [own_position(l) for l in range(1, depth + 1)]
        + pair_rows
    ).astype(jnp.int32)

    def swap(value, axis, bit):
        size = leaves if axis == "leaf" else blocks
        return lax.ppermute(value, axis, [(i, i ^ bit) for i in range(size)])

    def cell_columns(rows, level):
        info = infos[level - 1]
        parts = rows.reshape(-1, info.his, 2 * info.pair_x, info.zbs, 2 * info.rows)
        return parts.transpose(0, 1, 3, 2, 4).reshape(-1, width)

    def exchange_outer(value, level):
        if level <= 1:
            return lax.all_to_all(value, "blk", 0, 0, tiled=True)
        return lax.all_to_all(
            value,
            ("leaf", "blk"),
            0,
            0,
            axis_index_groups=infos[level - 1].outer,
            tiled=True,
        )

    def exchange_inner(value, level):
        info = infos[level - 1]
        if info.his == 1:
            return lax.all_to_all(value, "blk", 0, 0, axis_index_groups=info.inner_blk, tiled=True)
        return lax.all_to_all(
            value, ("leaf", "blk"), 0, 0, axis_index_groups=info.inner, tiled=True
        )

    def coupling_block(level, above):
        begin = couple_starts[level, above]
        return couple[begin : begin + counts[level]]

    uppers = range(1, depth + 1)
    dense = {}
    expanded = kernel_call(
        functools.partial(
            expand_kernel,
            1,
            infos,
            [pair_slot[0, above] for above in uppers],
            [couple_starts[0, above] for above in uppers],
        ),
        [shaped((counts[0], width), BF16)] * depth,
        [update_rows, couple],
        scalars=at,
        flops=2 * depth * counts[0] * listed_rows * width,
    )
    for above in uppers:
        dense[0, above] = expanded[above - 1]

    spread = kernel_call(first_kernel, [shaped((blocks, counts[0], cases), BF16)], [rhs])[0]
    full = lax.all_to_all(spread, "blk", 0, 0, tiled=True).reshape(width, cases)
    outs = [shaped((counts[0], cases), F32)]
    for info in infos:
        shape = (info.targets, info.chunk, info.cell_rows)
        outs += [shaped(shape, F32), shaped(shape, BF16)]
    matrix_scratch = pltpu.VMEM((counts[0], width), BF16)
    dense_scratch = pltpu.VMEM((depth, counts[0], width), BF16)
    y0, *base = kernel_call(
        functools.partial(subtree_kernel, infos, starts[1:]),
        outs,
        [full, (inverse, None), rhs] + hbm([dense[0, above] for above in uppers]),
        scalars=at,
        scratch=[
            pltpu.VMEM((cases, width), F32),
            matrix_scratch,
            dense_scratch,
            pltpu.SemaphoreType.DMA((1 + depth,)),
        ],
        flops=2 * (1 + depth) * counts[0] * width * cases,
    )
    received = []
    for level in uppers:
        received.append(swap(base[2 * level - 1], "leaf", 1))

    def pieces_of(value, level):
        pieces = [value]
        if infos[level - 1].pair_x == 2:
            pieces += [swap(piece, "leaf", 2) for piece in pieces]
        pieces += [swap(piece, "blk", 1) for piece in pieces]
        pieces += [swap(piece, "leaf", 1) for piece in pieces]
        return pieces

    inverse_pieces = {}
    for level in uppers:
        rows = inverse[starts[level] : starts[level] + counts[level]]
        if not infos[level - 1].direct:
            rows = cell_columns(rows, level)
        inverse_pieces[level] = pieces_of(rows, level)
        for above in range(level + 1, depth + 1):
            pieces = pieces_of(coupling_block(level, above), level)
            rows = len(pieces) * counts[level]
            dense[level, above] = kernel_call(
                functools.partial(
                    expand_kernel,
                    len(pieces),
                    [infos[above - 1]],
                    [pair_slot[level, above]],
                    None,
                ),
                [shaped((rows, width), BF16)],
                [update_rows] + pieces,
                scalars=at,
                flops=2 * rows * listed_rows * width,
            )[0]

    def sum_spread(parts, copies):
        return kernel_call(
            sum_spread_kernel, [shaped((copies,) + parts.shape[1:], BF16)], [parts]
        )[0]

    def cell_scratch(info):
        return pltpu.VMEM((info.cell_rows, width), BF16)

    ys = {}
    parts = (base[0] + received[0].astype(F32)).astype(BF16)
    for level in uppers:
        info = infos[level - 1]
        parts = exchange_outer(parts, level)
        gathered = exchange_inner(sum_spread(parts, info.cells), level)
        size = info.cell_rows * width * info.chunk
        count = 4 * info.pair_x
        if level == depth:
            parts = kernel_call(
                functools.partial(top_kernel, info),
                [shaped((info.cells, info.chunk, info.cell_rows), BF16)],
                [gathered] + hbm(inverse_pieces[level]),
                scratch=[cell_scratch(info), pltpu.SemaphoreType.DMA((count,))],
                flops=4 * size,
            )[0]
            break
        above = infos[level]
        ys[level], parts = kernel_call(
            functools.partial(forward_kernel, infos, level),
            [
                shaped((info.cell_rows, info.chunk), F32),
                shaped((above.targets, above.chunk, above.cell_rows), BF16),
            ],
            [gathered, base[2 * level], received[level]]
            + hbm(inverse_pieces[level])
            + [ys[j] for j in range(1, level)]
            + hbm([dense[j, level + 1] for j in range(1, level + 1)]),
            scalars=at,
            scratch=[
                pltpu.VMEM((above.chunk * above.pair_x, width), F32),
                cell_scratch(info),
                pltpu.SemaphoreType.DMA((count + level,)),
            ]
            + [cell_scratch(infos[j - 1]) for j in range(1, level + 1)],
            flops=4 * size,
        )

    solved = {}
    swapped = {}
    for level in range(depth, 0, -1):
        info = infos[level - 1]
        if level < depth:
            higher = range(level + 1, depth + 1)
            count = 4 * info.pair_x
            parts = kernel_call(
                functools.partial(backward_kernel, infos, level),
                [shaped((info.cells, info.chunk, info.cell_rows), BF16)],
                [ys[level]]
                + hbm(inverse_pieces[level])
                + [solved[above] for above in higher]
                + hbm([dense[level, above] for above in higher]),
                scalars=at,
                scratch=[cell_scratch(info), pltpu.SemaphoreType.DMA((count + len(higher),))]
                + [cell_scratch(info)] * len(higher),
                flops=4 * info.cell_rows * width * info.chunk,
            )[0]
        parts = exchange_inner(parts, level)
        solved[level] = exchange_outer(sum_spread(parts, info.targets), level)
        swapped[level] = swap(solved[level], "leaf", 1)

    part = kernel_call(
        functools.partial(last_kernel, infos),
        [shaped((blocks, cases, counts[0]), BF16)],
        [y0, (inverse, None)]
        + hbm([dense[0, above] for above in uppers])
        + [solved[above] for above in uppers]
        + [swapped[above] for above in uppers],
        scalars=at,
        scratch=[
            pltpu.VMEM((depth, cases, width), BF16),
            matrix_scratch,
            dense_scratch,
            pltpu.SemaphoreType.DMA((1 + depth,)),
        ],
        flops=2 * (1 + depth) * counts[0] * width * cases,
    )[0]
    parts = lax.all_to_all(part, "blk", 0, 0, tiled=True)

    outputs = []
    for level in uppers:
        info = infos[level - 1]
        member = leaf_id & ((1 << level) - 1)
        side = member & (2 * info.pair_x - 1)
        hi = member // (2 * info.pair_x)
        offset = (side * 2 + yb) * info.rows

        def own(value):
            shape = (info.his, info.pair_x, info.zbs, 2, info.chunk, info.cell_rows)
            sizes = (1, info.pair_x, 1, 2, info.chunk, info.rows)
            taken = lax.dynamic_slice(value.reshape(shape), (hi, 0, zb, 0, 0, offset), sizes)
            return taken[0, :, 0].transpose(1, 0, 2, 3)

        mine, other = own(solved[level]), own(swapped[level])
        rows = jnp.where(
            core == 0, jnp.stack([mine, other], 1), jnp.stack([other, mine], 1)
        )
        outputs.append(rows.reshape(cases, info.rows).T)
    out = kernel_call(output_kernel, [shaped((sum(counts), cases), F32)], [parts] + outputs)[0]
    return out[None, None]


def solution(mesh):
    spec = P("leaf", "blk", None, None)
    return jax.shard_map(
        solve, mesh=mesh, in_specs=(spec, spec, spec, P()), out_specs=spec, check_vma=False
    )
```

```python
import functools

import jax
import jax.numpy as jnp
from jax import lax
from jax.experimental import pallas as pl
from jax.experimental.pallas import tpu as pltpu
from jax.sharding import PartitionSpec as P


BF16 = jnp.bfloat16
F32 = jnp.float32


def mm(a, b):
    return jnp.dot(a, b, preferred_element_type=F32)


def mm_tn(a, b):
    return lax.dot_general(a, b, (((0,), (0,)), ((), ())), preferred_element_type=F32)


def mm_nt(a, b):
    return lax.dot_general(a, b, (((1,), (1,)), ((), ())), preferred_element_type=F32)


def shaped(shape, dtype):
    return jax.ShapeDtypeStruct(tuple(shape), dtype)


def kernel_call(body, outs, args, scalars=None, scratch=(), flops=0, stay=None):
    stay = [True] * len(outs) if stay is None else stay
    values = []
    specs = []
    moved = sum(o.size * o.dtype.itemsize for o in outs)
    for arg in args:
        value, spec = arg, pl.BlockSpec(memory_space=pltpu.VMEM)
        if isinstance(arg, tuple):
            value = pltpu.with_memory_space_constraint(arg[0], pltpu.HBM)
            spec = pl.BlockSpec(memory_space=pltpu.HBM)
        values.append(value)
        specs.append(spec)
        moved += value.size * value.dtype.itemsize
    if scalars is not None:
        specs = [pl.BlockSpec(memory_space=pltpu.SMEM)] + specs
        values = [scalars] + values
    return pl.pallas_call(
        body,
        out_shape=[
            pltpu.HBM(o.shape, o.dtype) if keep else o for o, keep in zip(outs, stay)
        ],
        in_specs=specs,
        out_specs=[pl.BlockSpec(memory_space=pltpu.VMEM)] * len(outs),
        scratch_shapes=list(scratch),
        compiler_params=pltpu.CompilerParams(vmem_limit_bytes=16 << 20),
        cost_estimate=pl.CostEstimate(flops=flops, bytes_accessed=moved, transcendentals=0),
    )(*values)


def hbm(values):
    return [(value, None) for value in values]


class Loads:
    def __init__(self, sems):
        self.sems = sems
        self.used = 0

    def start(self, pairs):
        copies = []
        for source, target in pairs:
            copies.append(pltpu.make_async_copy(source, target, self.sems.at[self.used]))
            copies[-1].start()
            self.used += 1
        return copies

    def rows(self, sources, target):
        pairs = []
        begin = 0
        for source in sources:
            count = source.shape[0]
            pairs.append((source, target.at[begin : begin + count, :]))
            begin += count
        return self.start(pairs)

    def groups(self, sources, target, order):
        rows = target.shape[0] // order
        if len(sources) == 1:
            source = sources[0]
            return [
                lambda g=g: self.start(
                    [(source.at[g * rows : (g + 1) * rows, :], target.at[g * rows : (g + 1) * rows, :])]
                )
                for g in range(order)
            ]
        each = len(sources) // order
        return [
            lambda g=g: self.rows(
                sources[g * each : (g + 1) * each], target.at[g * rows : (g + 1) * rows, :]
            )
            for g in range(order)
        ]


GROUPS = 2


def group_rows(total):
    size = total // GROUPS
    return [slice(g * size, (g + 1) * size) for g in range(GROUPS)]


def accumulate(total, left, right):
    half = right.shape[1] // 2
    terms = [mm_tn(left, right[:, :half]), mm_tn(left, right[:, half:])]
    return terms if total is None else [t + term for t, term in zip(total, terms)]


def wait(copies):
    for copy in copies:
        copy.wait()


def split_power(value, size):
    bits = size.bit_length() - 1
    if size == 1 << bits:
        return value >> bits, value & (size - 1)
    return value // size, value % size


class Level:
    def __init__(self, level, leaves, blocks, width, cases):
        self.pair_x = 2 if level >= 2 else 1
        self.his = (1 << level) // (2 * self.pair_x)
        self.zbs = blocks // 2
        self.rows = width // (blocks << level)
        self.cells = self.his * self.zbs
        self.cell_rows = width // self.cells
        self.chunk = cases // (4 * self.pair_x)
        self.targets = self.cells * self.pair_x * 2
        outer = []
        inner = []
        for node in range(leaves >> level):
            base = node << level
            for side in range(2):
                outer.append(
                    [
                        (base + 2 * upper + side) * blocks + b
                        for upper in range(1 << (level - 1))
                        for b in range(blocks)
                    ]
                )
                for xu in range(self.pair_x):
                    for yb in range(2):
                        inner.append(
                            [
                                (base + (hi * self.pair_x + xu) * 2 + side) * blocks + 2 * zb + yb
                                for hi in range(self.his)
                                for zb in range(self.zbs)
                            ]
                        )
        self.outer = outer
        self.inner = inner
        self.inner_blk = [[2 * zb + yb for zb in range(self.zbs)] for yb in range(2)]

    @property
    def direct(self):
        return (2 * self.rows) % 128 == 0

    def natural(self):
        if not self.direct:
            return [(c * self.cell_rows, c, 0, self.cell_rows) for c in range(self.cells)]
        size = 2 * self.rows
        return [
            (
                ((hi * 2 * self.pair_x + side) * self.zbs + zb) * size,
                hi * self.zbs + zb,
                side * size,
                size,
            )
            for hi in range(self.his)
            for side in range(2 * self.pair_x)
            for zb in range(self.zbs)
        ]

    def position(self, rows):
        block, t = split_power(rows, 2 * self.rows)
        block, zpos = split_power(block, self.zbs)
        hi, side = split_power(block, 2 * self.pair_x)
        cell = hi * self.zbs + zpos
        return (cell * (2 * self.pair_x) + side) * (2 * self.rows) + t

    def target(self, hi, xu, zb, yb):
        return ((hi * self.pair_x + xu) * self.zbs + zb) * 2 + yb

    def lanes(self, cell):
        return slice(cell * self.cell_rows, (cell + 1) * self.cell_rows)

    def all_targets(self):
        for hi in range(self.his):
            for xu in range(self.pair_x):
                for zb in range(self.zbs):
                    for yb in range(2):
                        yield hi * self.zbs + zb, xu, yb, self.target(hi, xu, zb, yb)


CORE, YB, XU, SPOT = 0, 1, 2, 3


def first_kernel(rhs, out):
    rounded = rhs[0 : out.shape[1], :].astype(BF16)
    for n in range(out.shape[0]):
        out[n] = rounded


def expand_kernel(count, aboves, slots, begins, at, lists, *refs):
    blocks, outs = refs[:count], refs[count:]
    width = outs[0].shape[-1]
    step = min(512, width)
    for n, (info, out) in enumerate(zip(aboves, outs)):
        listed = info.position(lists[pl.ds(at[slots[n]], 1), :])
        if begins is None:
            block = jnp.concatenate([b[...] for b in blocks], 0)
        else:
            block = blocks[0][begins[n] : begins[n] + out.shape[0], :]
        for begin in range(0, width, step):
            ids = begin + lax.broadcasted_iota(jnp.int32, (step, listed.shape[-1]), 0)
            chosen = jnp.where(ids == listed, 1.0, 0.0).astype(BF16)
            out[:, begin : begin + step] = mm_nt(block, chosen).astype(BF16)


def subtree_kernel(infos, starts, at, full, inverse, rhs, *refs):
    depth = len(infos)
    sources = refs[:depth]
    outs = refs[depth : depth + 1 + 2 * depth]
    total, matrix, dense, sems = refs[depth + 1 + 2 * depth :]
    loads = Loads(sems)
    groups = group_rows(matrix.shape[0])
    first = [start() for start in loads.groups([inverse], matrix, GROUPS)]
    later = [
        [start() for start in loads.groups([sources[n]], dense.at[n], GROUPS)]
        for n in range(depth)
    ]
    core = at[CORE]
    width = total.shape[-1]
    placed = []
    for n, info in enumerate(infos):
        row_ids = at[SPOT + n] + lax.broadcasted_iota(jnp.int32, (info.rows, width), 0)
        lane_ids = lax.broadcasted_iota(jnp.int32, (info.rows, width), 1)
        spots = jnp.where(row_ids == lane_ids, 1.0, 0.0).astype(BF16)
        own = rhs[starts[n] : starts[n] + info.rows, :].astype(BF16)
        placed.append(accumulate(None, own, spots))
    rounded = []
    for g, rows in enumerate(groups):
        wait(first[g])
        y = mm(matrix[rows, :], full[...])
        outs[0][rows, :] = y
        rounded.append(y.astype(BF16))
    half = width // 2
    for n, info in enumerate(infos):
        term = None
        for g, rows in enumerate(groups):
            wait(later[n][g])
            term = accumulate(term, rounded[g], dense[n, rows, :])
        total[:, :half] = placed[n][0] - term[0]
        total[:, half:] = placed[n][1] - term[1]
        mine, other = outs[1 + 2 * n], outs[2 + 2 * n]
        for cell, xu, yb, target in info.all_targets():
            for side, ref in ((core, mine), (1 - core, other)):
                row = ((yb * 2 + side) * info.pair_x + xu) * info.chunk
                row = pl.multiple_of(row, info.chunk)
                value = total[pl.ds(row, info.chunk), info.lanes(cell)]
                ref[target] = value.astype(ref.dtype)


def sum_spread_kernel(parts, out):
    total = parts[0].astype(F32)
    for n in range(1, parts.shape[0]):
        total = total + parts[n].astype(F32)
    rounded = total.astype(BF16)
    for n in range(out.shape[0]):
        out[n] = rounded


def natural_rows(info, gathered):
    blocks = [
        gathered[cell][:, inside : inside + size]
        for _, cell, inside, size in info.natural()
    ]
    return jnp.concatenate(blocks, 1)


def put_spread(info, halves, out):
    value = jnp.concatenate(halves, 1).astype(BF16)
    for lane, cell, inside, size in info.natural():
        out[cell, :, inside : inside + size] = value[:, lane : lane + size]


def forward_kernel(infos, k, at, gathered, mine, received, *refs):
    info, above = infos[k - 1], infos[k]
    count = 4 * info.pair_x
    pieces = refs[:count]
    lower_y = refs[count : count + k - 1]
    sources = refs[count + k - 1 : count + 2 * k - 1]
    y_ref, out, total, matrix, sems = refs[count + 2 * k - 1 : count + 2 * k + 4]
    dense = refs[count + 2 * k + 4 :]
    loads = Loads(sems)
    groups = group_rows(matrix.shape[0])
    first = [start() for start in loads.groups(pieces, matrix, GROUPS)]
    later = [
        [start() for start in loads.groups([source], dense[j], GROUPS)]
        for j, source in enumerate(sources)
    ]
    vector = natural_rows(info, gathered)
    ys = []
    for g, rows in enumerate(groups):
        wait(first[g])
        y = mm_nt(matrix[rows, :], vector)
        y_ref[rows, :] = y
        ys.append(y)
    same = {}
    for j in range(1, k + 1):
        term = None
        for g, rows in enumerate(group_rows(dense[j - 1].shape[0])):
            value = ys[g] if j == k else lower_y[j - 1][rows, :]
            wait(later[j - 1][g])
            term = accumulate(term, value.astype(BF16), dense[j - 1][rows, :])
        term = jnp.concatenate(term, 1)
        same.setdefault(infos[j - 1].pair_x == above.pair_x, []).append(term)
    if False in same:
        total[...] = functools.reduce(jnp.add, same[False])
    else:
        total[...] = jnp.zeros(total.shape, F32)
    if True in same:
        term = functools.reduce(jnp.add, same[True])
        rows = pl.ds(pl.multiple_of(at[XU] * above.chunk, above.chunk), above.chunk)
        total[rows, :] = total[rows, :] + term
    for cell, xu, yb, target in above.all_targets():
        value = mine[target].astype(F32) + received[target].astype(F32)
        minus = total[xu * above.chunk : (xu + 1) * above.chunk, above.lanes(cell)]
        value = jnp.where(at[YB] == yb, value - minus, value)
        out[target] = value.astype(BF16)


def top_kernel(info, gathered, *refs):
    count = 4 * info.pair_x
    pieces = refs[:count]
    out, matrix, sems = refs[count:]
    first = [start() for start in Loads(sems).groups(pieces, matrix, GROUPS)]
    vector = natural_rows(info, gathered)
    halves = None
    for g, rows in enumerate(group_rows(matrix.shape[0])):
        wait(first[g])
        y = mm_nt(matrix[rows, :], vector)
        halves = accumulate(halves, y.astype(BF16), matrix[rows, :])
    put_spread(info, halves, out)


def backward_kernel(infos, k, at, y, *refs):
    info = infos[k - 1]
    count = 4 * info.pair_x
    uppers = infos[k:]
    many = len(uppers)
    pieces = refs[:count]
    solved = refs[count : count + many]
    sources = refs[count + many : count + 2 * many]
    out, matrix, sems = refs[count + 2 * many : count + 2 * many + 3]
    dense = refs[count + 2 * many + 3 :]
    loads = Loads(sems)
    dense_loads = [loads.groups([source], dense[n], GROUPS) for n, source in enumerate(sources)]
    matrix_loads = loads.groups(pieces, matrix, GROUPS)
    first = []
    last = []
    for g in range(GROUPS):
        first.append([start[g]() for start in dense_loads])
        last.append(matrix_loads[g]())
    vectors = []
    for n, above in enumerate(uppers):
        parts = []
        for hi in range(above.his):
            for zb in range(above.zbs):
                if above.pair_x == info.pair_x:
                    slot = ((hi * above.pair_x + at[XU]) * above.zbs + zb) * 2 + at[YB]
                    parts.append(solved[n][slot])
                else:
                    slots = [
                        above.target(hi, xu, zb, 0) + at[YB] for xu in range(above.pair_x)
                    ]
                    parts.append(jnp.concatenate([solved[n][slot] for slot in slots], 0))
        vectors.append(jnp.concatenate(parts, 1))
    halves = None
    for g, rows in enumerate(group_rows(matrix.shape[0])):
        z = y[rows, :]
        for n in range(many):
            wait(first[g][n])
            z = z - mm_nt(dense[n][rows, :], vectors[n])
        wait(last[g])
        halves = accumulate(halves, z.astype(BF16), matrix[rows, :])
    put_spread(info, halves, out)


def full_cases(info, core, mine, other, full):
    for cell, xu, yb, target in info.all_targets():
        for side, ref in ((core, mine), (1 - core, other)):
            row = ((yb * 2 + side) * info.pair_x + xu) * info.chunk
            row = pl.multiple_of(row, info.chunk)
            full[pl.ds(row, info.chunk), info.lanes(cell)] = ref[target]


def subtract_kernel(info, at, y, source, mine, other, out, full, dense, sems):
    loads = [start() for start in Loads(sems).groups([source], dense, GROUPS)]
    full_cases(info, at[CORE], mine, other, full)
    for g, rows in enumerate(group_rows(dense.shape[0])):
        wait(loads[g])
        out[rows, :] = y[rows, :] - mm_nt(dense[rows, :], full[...])


def last_kernel(info, at, y, source, mine, other, inverse, out, full, dense, matrix, sems):
    loads = Loads(sems)
    dense_loads = loads.groups([source], dense, GROUPS)
    matrix_loads = loads.groups([inverse], matrix, GROUPS)
    copies = [(dense_loads[g](), matrix_loads[g]()) for g in range(GROUPS)]
    full_cases(info, at[CORE], mine, other, full)
    halves = None
    for g, rows in enumerate(group_rows(dense.shape[0])):
        wait(copies[g][0])
        z = y[rows, :] - mm_nt(dense[rows, :], full[...])
        wait(copies[g][1])
        halves = accumulate(halves, z.astype(BF16), matrix[rows, :])
    value = jnp.concatenate(halves, 1).astype(BF16)
    size = out.shape[-1]
    for n in range(out.shape[0]):
        out[n] = value[:, n * size : (n + 1) * size]


def output_kernel(parts, *refs):
    rows, out = refs[:-1], refs[-1]
    total = parts[0].astype(F32)
    for n in range(1, parts.shape[0]):
        total = total + parts[n].astype(F32)
    begin = total.shape[1]
    out[0:begin, :] = total.T
    for row in rows:
        out[begin : begin + row.shape[0], :] = row[...].astype(F32)
        begin += row.shape[0]


def solve(right_side, inverse_blocks, coupling, update_rows):
    leaves = lax.axis_size("leaf")
    blocks = lax.axis_size("blk")
    depth = leaves.bit_length() - 1
    leaf_id = lax.axis_index("leaf")
    blk_id = lax.axis_index("blk")
    core = leaf_id & 1
    yb = blk_id & 1
    zb = blk_id >> 1
    width = inverse_blocks.shape[-1]
    cases = right_side.shape[-1]
    rhs = right_side[0, 0]
    inverse = inverse_blocks[0, 0]
    couple = coupling[0, 0]
    listed_rows = coupling.shape[-1]
    counts = [width // (blocks << level) for level in range(depth + 1)]
    starts = [sum(counts[:level]) for level in range(depth + 1)]
    infos = [Level(l, leaves, blocks, width, cases) for l in range(1, depth + 1)]
    couple_starts = {}
    cursor = 0
    for level in range(depth):
        for above in range(level + 1, depth + 1):
            couple_starts[level, above] = cursor
            cursor += counts[level]
    pair_bases = []
    cursor = 0
    for level in range(depth + 1):
        pair_bases.append(cursor)
        cursor += (leaves >> level) * (depth - level)

    def own_position(level):
        info = infos[level - 1]
        member = leaf_id & ((1 << level) - 1)
        side = member & (2 * info.pair_x - 1)
        cell = member // (2 * info.pair_x) * info.zbs + zb
        return ((cell * 2 * info.pair_x + side) * 2 + yb) * info.rows

    pair_slot = {}
    pair_rows = []
    for level in range(depth):
        for above in range(level + 1, depth + 1):
            pair_slot[level, above] = SPOT + depth + len(pair_rows)
            node = leaf_id >> level
            pair_rows.append(pair_bases[level] + node * (depth - level) + (above - level - 1))
    at = jnp.stack(
        [core, yb, (leaf_id >> 1) & 1]
        + [own_position(l) for l in range(1, depth + 1)]
        + pair_rows
    ).astype(jnp.int32)

    def swap(value, axis, bit):
        size = leaves if axis == "leaf" else blocks
        return lax.ppermute(value, axis, [(i, i ^ bit) for i in range(size)])

    def cell_columns(rows, level):
        info = infos[level - 1]
        parts = rows.reshape(-1, info.his, 2 * info.pair_x, info.zbs, 2 * info.rows)
        return parts.transpose(0, 1, 3, 2, 4).reshape(-1, width)

    def exchange_outer(value, level):
        if level <= 1:
            return lax.all_to_all(value, "blk", 0, 0, tiled=True)
        return lax.all_to_all(
            value,
            ("leaf", "blk"),
            0,
            0,
            axis_index_groups=infos[level - 1].outer,
            tiled=True,
        )

    def exchange_inner(value, level):
        info = infos[level - 1]
        if info.his == 1:
            return lax.all_to_all(
                value, "blk", 0, 0, axis_index_groups=info.inner_blk, tiled=True
            )
        return lax.all_to_all(
            value, ("leaf", "blk"), 0, 0, axis_index_groups=info.inner, tiled=True
        )

    def coupling_block(level, above):
        begin = couple_starts[level, above]
        return couple[begin : begin + counts[level]]

    uppers = range(1, depth + 1)
    dense = {}
    expanded = kernel_call(
        functools.partial(
            expand_kernel,
            1,
            infos,
            [pair_slot[0, above] for above in uppers],
            [couple_starts[0, above] for above in uppers],
        ),
        [shaped((counts[0], width), BF16)] * depth,
        [update_rows, couple],
        scalars=at,
        flops=2 * depth * counts[0] * listed_rows * width,
    )
    for above in uppers:
        dense[0, above] = expanded[above - 1]

    spread = kernel_call(
        first_kernel, [shaped((blocks, counts[0], cases), BF16)], [rhs]
    )[0]
    full = lax.all_to_all(spread, "blk", 0, 0, tiled=True).reshape(width, cases)
    outs = [shaped((counts[0], cases), F32)]
    for info in infos:
        shape = (info.targets, info.chunk, info.cell_rows)
        outs += [shaped(shape, BF16), shaped(shape, BF16)]
    matrix_scratch = pltpu.VMEM((counts[0], width), BF16)
    y0, *base = kernel_call(
        functools.partial(subtree_kernel, infos, starts[1:]),
        outs,
        [full, (inverse, None), rhs] + hbm([dense[0, above] for above in uppers]),
        scalars=at,
        scratch=[
            pltpu.VMEM((cases, width), F32),
            matrix_scratch,
            pltpu.VMEM((depth, counts[0], width), BF16),
            pltpu.SemaphoreType.DMA((GROUPS * (1 + depth),)),
        ],
        flops=2 * (1 + depth) * counts[0] * width * cases,
        stay=[True, False, False] + [True, True] * (depth - 1),
    )
    received = []
    for level in uppers:
        received.append(swap(base[2 * level - 1], "leaf", 1))

    def pieces_of(value, level):
        pieces = [value]
        if infos[level - 1].pair_x == 2:
            pieces += [swap(piece, "leaf", 2) for piece in pieces]
        pieces += [swap(piece, "blk", 1) for piece in pieces]
        pieces += [swap(piece, "leaf", 1) for piece in pieces]
        return pieces

    inverse_pieces = {}
    for level in uppers:
        rows = inverse[starts[level] : starts[level] + counts[level]]
        if not infos[level - 1].direct:
            rows = cell_columns(rows, level)
        inverse_pieces[level] = pieces_of(rows, level)
        for above in range(level + 1, depth + 1):
            pieces = pieces_of(coupling_block(level, above), level)
            rows = len(pieces) * counts[level]
            dense[level, above] = kernel_call(
                functools.partial(
                    expand_kernel,
                    len(pieces),
                    [infos[above - 1]],
                    [pair_slot[level, above]],
                    None,
                ),
                [shaped((rows, width), BF16)],
                [update_rows] + pieces,
                scalars=at,
                flops=2 * rows * listed_rows * width,
            )[0]

    def sum_spread(parts, copies):
        return kernel_call(
            sum_spread_kernel, [shaped((copies,) + parts.shape[1:], BF16)], [parts]
        )[0]

    def cell_scratch(info):
        return pltpu.VMEM((info.cell_rows, width), BF16)

    ys = {}
    parts = (base[0].astype(F32) + received[0].astype(F32)).astype(BF16)
    for level in uppers:
        info = infos[level - 1]
        parts = exchange_outer(parts, level)
        gathered = exchange_inner(sum_spread(parts, info.cells), level)
        size = info.cell_rows * width * info.chunk
        count = 4 * info.pair_x
        if level == depth:
            parts = kernel_call(
                functools.partial(top_kernel, info),
                [shaped((info.cells, info.chunk, info.cell_rows), BF16)],
                [gathered] + hbm(inverse_pieces[level]),
                scratch=[cell_scratch(info), pltpu.SemaphoreType.DMA((count,))],
                flops=4 * size,
                stay=[False],
            )[0]
            break
        above = infos[level]
        ys[level], parts = kernel_call(
            functools.partial(forward_kernel, infos, level),
            [
                shaped((info.cell_rows, info.chunk), F32),
                shaped((above.targets, above.chunk, above.cell_rows), BF16),
            ],
            [gathered, base[2 * level], received[level]]
            + hbm(inverse_pieces[level])
            + [ys[j] for j in range(1, level)]
            + hbm([dense[j, level + 1] for j in range(1, level + 1)]),
            scalars=at,
            scratch=[
                pltpu.VMEM((above.chunk * above.pair_x, width), F32),
                cell_scratch(info),
                pltpu.SemaphoreType.DMA((count + GROUPS * level,)),
            ]
            + [cell_scratch(infos[j - 1]) for j in range(1, level + 1)],
            flops=4 * size,
        )

    solved = {}
    swapped = {}
    z0 = y0
    for level in range(depth, 0, -1):
        info = infos[level - 1]
        if level < depth:
            higher = range(level + 1, depth + 1)
            count = 4 * info.pair_x
            parts = kernel_call(
                functools.partial(backward_kernel, infos, level),
                [shaped((info.cells, info.chunk, info.cell_rows), BF16)],
                [ys[level]]
                + hbm(inverse_pieces[level])
                + [solved[above] for above in higher]
                + hbm([dense[level, above] for above in higher]),
                scalars=at,
                scratch=[cell_scratch(info), pltpu.SemaphoreType.DMA((count + GROUPS * len(higher),))]
                + [cell_scratch(info)] * len(higher),
                flops=4 * info.cell_rows * width * info.chunk,
                stay=[False],
            )[0]
        parts = exchange_inner(parts, level)
        solved[level] = exchange_outer(sum_spread(parts, info.targets), level)
        swapped[level] = swap(solved[level], "leaf", 1)
        if level > 1:
            z0 = kernel_call(
                functools.partial(subtract_kernel, info),
                [shaped((counts[0], cases), F32)],
                [z0, (dense[0, level], None), solved[level], swapped[level]],
                scalars=at,
                scratch=[
                    pltpu.VMEM((cases, width), BF16),
                    matrix_scratch,
                    pltpu.SemaphoreType.DMA((GROUPS,)),
                ],
                flops=2 * counts[0] * width * cases,
            )[0]

    part = kernel_call(
        functools.partial(last_kernel, infos[0]),
        [shaped((blocks, cases, counts[0]), BF16)],
        [z0, (dense[0, 1], None), solved[1], swapped[1], (inverse, None)],
        scalars=at,
        scratch=[
            pltpu.VMEM((cases, width), BF16),
            matrix_scratch,
            matrix_scratch,
            pltpu.SemaphoreType.DMA((2 * GROUPS,)),
        ],
        flops=4 * counts[0] * width * cases,
    )[0]
    parts = lax.all_to_all(part, "blk", 0, 0, tiled=True)

    outputs = []
    for level in uppers:
        info = infos[level - 1]
        member = leaf_id & ((1 << level) - 1)
        side = member & (2 * info.pair_x - 1)
        hi = member // (2 * info.pair_x)
        offset = (side * 2 + yb) * info.rows

        def own(value):
            shape = (info.his, info.pair_x, info.zbs, 2, info.chunk, info.cell_rows)
            sizes = (1, info.pair_x, 1, 2, info.chunk, info.rows)
            taken = lax.dynamic_slice(value.reshape(shape), (hi, 0, zb, 0, 0, offset), sizes)
            return taken[0, :, 0].transpose(1, 0, 2, 3)

        mine, other = own(solved[level]), own(swapped[level])
        rows = jnp.where(
            core == 0, jnp.stack([mine, other], 1), jnp.stack([other, mine], 1)
        )
        outputs.append(rows.reshape(cases, info.rows).T)
    out = kernel_call(
        output_kernel, [shaped((sum(counts), cases), F32)], [parts] + outputs
    )[0]
    return out[None, None]


def solution(mesh):
    spec = P("leaf", "blk", None, None)
    return jax.shard_map(
        solve, mesh=mesh, in_specs=(spec, spec, spec, P()), out_specs=spec, check_vma=False
    )
```

```python
import functools

import jax
import jax.numpy as jnp
from jax import lax
from jax.experimental import pallas as pl
from jax.experimental.pallas import tpu as pltpu
from jax.sharding import PartitionSpec as P


BF16 = jnp.bfloat16
F32 = jnp.float32


def mm(a, b):
    return jnp.dot(a, b, preferred_element_type=F32)


def mm_tn(a, b):
    return lax.dot_general(a, b, (((0,), (0,)), ((), ())), preferred_element_type=F32)


def mm_nt(a, b):
    return lax.dot_general(a, b, (((1,), (1,)), ((), ())), preferred_element_type=F32)


def shaped(shape, dtype):
    return jax.ShapeDtypeStruct(tuple(shape), dtype)


def kernel_call(body, outs, args, scalars=None, scratch=(), flops=0, stay=None):
    stay = [True] * len(outs) if stay is None else stay
    values = []
    specs = []
    moved = sum(o.size * o.dtype.itemsize for o in outs)
    for arg in args:
        value, spec = arg, pl.BlockSpec(memory_space=pltpu.VMEM)
        if isinstance(arg, tuple):
            value = pltpu.with_memory_space_constraint(arg[0], pltpu.HBM)
            if arg[1] is None:
                spec = pl.BlockSpec(memory_space=pltpu.HBM)
        values.append(value)
        specs.append(spec)
        moved += value.size * value.dtype.itemsize
    return pl.pallas_call(
        body if scalars is None else lambda *refs: body(scalars(), *refs),
        out_shape=[
            pltpu.HBM(o.shape, o.dtype) if keep else o for o, keep in zip(outs, stay)
        ],
        in_specs=specs,
        out_specs=[pl.BlockSpec(memory_space=pltpu.VMEM)] * len(outs),
        scratch_shapes=list(scratch),
        compiler_params=pltpu.CompilerParams(vmem_limit_bytes=16 << 20),
        cost_estimate=pl.CostEstimate(flops=flops, bytes_accessed=moved, transcendentals=0),
    )(*values)


def hbm(values):
    return [(value, None) for value in values]


class Loads:
    def __init__(self, sems):
        self.sems = sems
        self.used = 0

    def start(self, pairs):
        copies = []
        for source, target in pairs:
            copies.append(pltpu.make_async_copy(source, target, self.sems.at[self.used]))
            copies[-1].start()
            self.used += 1
        return copies

    def rows(self, sources, target):
        pairs = []
        begin = 0
        for source in sources:
            count = source.shape[0]
            pairs.append((source, target.at[begin : begin + count, :]))
            begin += count
        return self.start(pairs)

    def groups(self, sources, target, order):
        rows = target.shape[0] // order
        if len(sources) == 1:
            source = sources[0]
            return [
                lambda g=g: self.start(
                    [(source.at[g * rows : (g + 1) * rows, :], target.at[g * rows : (g + 1) * rows, :])]
                )
                for g in range(order)
            ]
        each = len(sources) // order
        return [
            lambda g=g: self.rows(
                sources[g * each : (g + 1) * each], target.at[g * rows : (g + 1) * rows, :]
            )
            for g in range(order)
        ]


GROUPS = 2


def group_rows(total):
    size = total // GROUPS
    return [slice(g * size, (g + 1) * size) for g in range(GROUPS)]


def accumulate(total, left, right):
    half = right.shape[1] // 2
    terms = [mm_tn(left, right[:, :half]), mm_tn(left, right[:, half:])]
    return terms if total is None else [t + term for t, term in zip(total, terms)]


def wait(copies):
    for copy in copies:
        copy.wait()


def split_power(value, size):
    bits = size.bit_length() - 1
    if size == 1 << bits:
        return value >> bits, value & (size - 1)
    return value // size, value % size


class Level:
    def __init__(self, level, leaves, blocks, width, cases):
        self.level = level
        self.pair_x = 2 if level >= 2 else 1
        self.his = (1 << level) // (2 * self.pair_x)
        self.zbs = blocks // 2
        self.rows = width // (blocks << level)
        self.cells = self.his * self.zbs
        self.cell_rows = width // self.cells
        self.chunk = cases // (4 * self.pair_x)
        self.targets = self.cells * self.pair_x * 2
        outer = []
        inner = []
        for node in range(leaves >> level):
            base = node << level
            for side in range(2):
                outer.append(
                    [
                        (base + 2 * upper + side) * blocks + b
                        for upper in range(1 << (level - 1))
                        for b in range(blocks)
                    ]
                )
                for xu in range(self.pair_x):
                    for yb in range(2):
                        inner.append(
                            [
                                (base + (hi * self.pair_x + xu) * 2 + side) * blocks + 2 * zb + yb
                                for hi in range(self.his)
                                for zb in range(self.zbs)
                            ]
                        )
        self.outer = outer
        self.inner = inner
        self.inner_blk = [[2 * zb + yb for zb in range(self.zbs)] for yb in range(2)]

    @property
    def direct(self):
        return (2 * self.rows) % 128 == 0

    def natural(self):
        if not self.direct:
            return [(c * self.cell_rows, c, 0, self.cell_rows) for c in range(self.cells)]
        size = 2 * self.rows
        return [
            (
                ((hi * 2 * self.pair_x + side) * self.zbs + zb) * size,
                hi * self.zbs + zb,
                side * size,
                size,
            )
            for hi in range(self.his)
            for side in range(2 * self.pair_x)
            for zb in range(self.zbs)
        ]

    def position(self, rows):
        block, t = split_power(rows, 2 * self.rows)
        block, zpos = split_power(block, self.zbs)
        hi, side = split_power(block, 2 * self.pair_x)
        cell = hi * self.zbs + zpos
        return (cell * (2 * self.pair_x) + side) * (2 * self.rows) + t

    def target(self, hi, xu, zb, yb):
        return ((hi * self.pair_x + xu) * self.zbs + zb) * 2 + yb

    def lanes(self, cell):
        return slice(cell * self.cell_rows, (cell + 1) * self.cell_rows)

    def all_targets(self):
        for hi in range(self.his):
            for xu in range(self.pair_x):
                for zb in range(self.zbs):
                    for yb in range(2):
                        yield hi * self.zbs + zb, xu, yb, self.target(hi, xu, zb, yb)


CORE, YB, XU, SPOT = 0, 1, 2, 3


def first_kernel(rhs, out, rows, sem):
    copy = pltpu.make_async_copy(rhs.at[0 : rows.shape[0], :], rows, sem)
    copy.start()
    copy.wait()
    rounded = rows[...].astype(BF16)
    for n in range(out.shape[0]):
        out[n] = rounded


def expand_kernel(count, aboves, slots, begins, at, lists, *refs):
    blocks, outs = refs[:count], refs[count:]
    width = outs[0].shape[-1]
    step = min(512, width)
    for n, (info, out) in enumerate(zip(aboves, outs)):
        listed = info.position(lists[pl.ds(at[slots[n]], 1), :])
        if begins is None:
            block = jnp.concatenate([b[...] for b in blocks], 0)
        else:
            block = blocks[0][begins[n] : begins[n] + out.shape[0], :]
        for begin in range(0, width, step):
            ids = begin + lax.broadcasted_iota(jnp.int32, (step, listed.shape[-1]), 0)
            chosen = jnp.where(ids == listed, 1.0, 0.0).astype(BF16)
            out[:, begin : begin + step] = mm_nt(block, chosen).astype(BF16)


def subtree_kernel(infos, starts, at, full, inverse, rhs, *refs):
    depth = len(infos)
    sources = refs[:depth]
    outs = refs[depth : depth + 1 + 2 * depth]
    total, matrix, dense, rhs_copy, sems = refs[depth + 1 + 2 * depth :]
    loads = Loads(sems)
    rhs_load = loads.start([(rhs, rhs_copy)])
    groups = group_rows(matrix.shape[0])
    first = [start() for start in loads.groups([inverse], matrix, GROUPS)]
    later = [
        [start() for start in loads.groups([sources[n]], dense.at[n], GROUPS)]
        for n in range(depth)
    ]
    core = at[CORE]
    width = total.shape[-1]
    placed = []
    wait(rhs_load)
    for n, info in enumerate(infos):
        row_ids = at[SPOT + n] + lax.broadcasted_iota(jnp.int32, (info.rows, width), 0)
        lane_ids = lax.broadcasted_iota(jnp.int32, (info.rows, width), 1)
        spots = jnp.where(row_ids == lane_ids, 1.0, 0.0).astype(BF16)
        own = rhs_copy[starts[n] : starts[n] + info.rows, :].astype(BF16)
        placed.append(accumulate(None, own, spots))
    rounded = []
    for g, rows in enumerate(groups):
        wait(first[g])
        y = mm(matrix[rows, :], full[...])
        outs[0][rows, :] = y
        rounded.append(y.astype(BF16))
    half = width // 2
    for n, info in enumerate(infos):
        term = None
        for g, rows in enumerate(groups):
            wait(later[n][g])
            term = accumulate(term, rounded[g], dense[n, rows, :])
        total[:, :half] = placed[n][0] - term[0]
        total[:, half:] = placed[n][1] - term[1]
        mine, other = outs[1 + 2 * n], outs[2 + 2 * n]
        for cell, xu, yb, target in info.all_targets():
            for side, ref in ((core, mine), (1 - core, other)):
                row = ((yb * 2 + side) * info.pair_x + xu) * info.chunk
                row = pl.multiple_of(row, info.chunk)
                value = total[pl.ds(row, info.chunk), info.lanes(cell)]
                ref[target] = value.astype(ref.dtype)


def sum_spread_kernel(parts, out):
    total = parts[0].astype(F32)
    for n in range(1, parts.shape[0]):
        total = total + parts[n].astype(F32)
    rounded = total.astype(BF16)
    for n in range(out.shape[0]):
        out[n] = rounded


def natural_rows(info, gathered):
    blocks = [
        gathered[cell][:, inside : inside + size]
        for _, cell, inside, size in info.natural()
    ]
    return jnp.concatenate(blocks, 1)


def put_spread(info, halves, out):
    value = jnp.concatenate(halves, 1).astype(BF16)
    for lane, cell, inside, size in info.natural():
        out[cell, :, inside : inside + size] = value[:, lane : lane + size]


def forward_kernel(infos, k, at, gathered, mine_hbm, received_hbm, *refs):
    info, above = infos[k - 1], infos[k]
    count = 4 * info.pair_x
    pieces = refs[:count]
    lower_y = refs[count : count + k - 1]
    sources = refs[count + k - 1 : count + 2 * k - 1]
    y_ref, out, total, matrix, mine, received, sems = refs[count + 2 * k - 1 : count + 2 * k + 6]
    dense = refs[count + 2 * k + 6 : count + 3 * k + 6]
    lower_copies = refs[count + 3 * k + 6 :]
    loads = Loads(sems)
    groups = group_rows(matrix.shape[0])
    first = [start() for start in loads.groups(pieces, matrix, GROUPS)]
    later = [
        [start() for start in loads.groups([source], dense[j], GROUPS)]
        for j, source in enumerate(sources)
    ]
    base = loads.start([(mine_hbm, mine), (received_hbm, received)])
    base += loads.start(list(zip(lower_y, lower_copies)))
    lower_y = lower_copies
    vector = natural_rows(info, gathered)
    ys = []
    for g, rows in enumerate(groups):
        wait(first[g])
        y = mm_nt(matrix[rows, :], vector)
        y_ref[rows, :] = y
        ys.append(y)
    wait(base)
    same = {}
    for j in range(1, k + 1):
        term = None
        for g, rows in enumerate(group_rows(dense[j - 1].shape[0])):
            value = ys[g] if j == k else lower_y[j - 1][rows, :]
            wait(later[j - 1][g])
            term = accumulate(term, value.astype(BF16), dense[j - 1][rows, :])
        term = jnp.concatenate(term, 1)
        same.setdefault(infos[j - 1].pair_x == above.pair_x, []).append(term)
    if False in same:
        total[...] = functools.reduce(jnp.add, same[False])
    else:
        total[...] = jnp.zeros(total.shape, F32)
    if True in same:
        term = functools.reduce(jnp.add, same[True])
        rows = pl.ds(pl.multiple_of(at[XU] * above.chunk, above.chunk), above.chunk)
        total[rows, :] = total[rows, :] + term
    for cell, xu, yb, target in above.all_targets():
        value = mine[target].astype(F32) + received[target].astype(F32)
        minus = total[xu * above.chunk : (xu + 1) * above.chunk, above.lanes(cell)]
        value = jnp.where(at[YB] == yb, value - minus, value)
        out[target] = value.astype(BF16)


def top_kernel(info, gathered, *refs):
    pieces, out = refs[:-1], refs[-1]
    each = len(pieces) // GROUPS
    vector = natural_rows(info, gathered)
    halves = None
    for g in range(GROUPS):
        matrix = jnp.concatenate([p[...] for p in pieces[g * each : (g + 1) * each]], 0)
        y = mm_nt(matrix, vector)
        halves = accumulate(halves, y.astype(BF16), matrix)
    put_spread(info, halves, out)


def backward_kernel(infos, k, at, y_hbm, *refs):
    info = infos[k - 1]
    count = 4 * info.pair_x
    uppers = infos[k:]
    many = len(uppers)
    pieces = refs[:count]
    solved = refs[count : count + many]
    sources = refs[count + many : count + 2 * many]
    out, matrix, y, sems = refs[count + 2 * many : count + 2 * many + 4]
    dense = refs[count + 2 * many + 4 :]
    loads = Loads(sems)
    y_load = loads.start([(y_hbm, y)])
    dense_loads = [loads.groups([source], dense[n], GROUPS) for n, source in enumerate(sources)]
    matrix_loads = loads.groups(pieces, matrix, GROUPS)
    first = []
    last = []
    for g in range(GROUPS):
        first.append([start[g]() for start in dense_loads])
        last.append(matrix_loads[g]())
    vectors = []
    for n, above in enumerate(uppers):
        parts = []
        for hi in range(above.his):
            for zb in range(above.zbs):
                if above.pair_x == info.pair_x:
                    slot = ((hi * above.pair_x + at[XU]) * above.zbs + zb) * 2 + at[YB]
                    parts.append(solved[n][slot])
                else:
                    slots = [
                        above.target(hi, xu, zb, 0) + at[YB] for xu in range(above.pair_x)
                    ]
                    parts.append(jnp.concatenate([solved[n][slot] for slot in slots], 0))
        vectors.append(jnp.concatenate(parts, 1))
    wait(y_load)
    halves = None
    for g, rows in enumerate(group_rows(matrix.shape[0])):
        z = y[rows, :]
        for n in range(many):
            wait(first[g][n])
            z = z - mm_nt(dense[n][rows, :], vectors[n])
        wait(last[g])
        halves = accumulate(halves, z.astype(BF16), matrix[rows, :])
    put_spread(info, halves, out)


def full_cases(info, core, mine, other, full):
    for cell, xu, yb, target in info.all_targets():
        for side, ref in ((core, mine), (1 - core, other)):
            row = ((yb * 2 + side) * info.pair_x + xu) * info.chunk
            row = pl.multiple_of(row, info.chunk)
            full[pl.ds(row, info.chunk), info.lanes(cell)] = ref[target]


def subtract_kernel(info, at, y_hbm, source, mine, other, out, full, dense, y, sems):
    copies = Loads(sems)
    y_load = copies.start([(y_hbm, y)])
    loads = [start() for start in copies.groups([source], dense, GROUPS)]
    full_cases(info, at[CORE], mine, other, full)
    wait(y_load)
    for g, rows in enumerate(group_rows(dense.shape[0])):
        wait(loads[g])
        out[rows, :] = y[rows, :] - mm_nt(dense[rows, :], full[...])


def last_kernel(
    info, at, y_hbm, source, mine, other, inverse, out, full, dense, matrix, y, sems
):
    loads = Loads(sems)
    y_load = loads.start([(y_hbm, y)])
    dense_loads = loads.groups([source], dense, GROUPS)
    matrix_loads = loads.groups([inverse], matrix, GROUPS)
    copies = [(dense_loads[g](), matrix_loads[g]()) for g in range(GROUPS)]
    full_cases(info, at[CORE], mine, other, full)
    wait(y_load)
    halves = None
    for g, rows in enumerate(group_rows(dense.shape[0])):
        wait(copies[g][0])
        z = y[rows, :] - mm_nt(dense[rows, :], full[...])
        wait(copies[g][1])
        halves = accumulate(halves, z.astype(BF16), matrix[rows, :])
    value = jnp.concatenate(halves, 1).astype(BF16)
    size = out.shape[-1]
    for n in range(out.shape[0]):
        out[n] = value[:, n * size : (n + 1) * size]


def output_kernel(parts, *refs):
    rows, out = refs[:-1], refs[-1]
    total = parts[0].astype(F32)
    for n in range(1, parts.shape[0]):
        total = total + parts[n].astype(F32)
    begin = total.shape[1]
    out[0:begin, :] = total.T
    for row in rows:
        out[begin : begin + row.shape[0], :] = row[...].astype(F32)
        begin += row.shape[0]


def solve(right_side, inverse_blocks, coupling, update_rows):
    leaves = lax.axis_size("leaf")
    blocks = lax.axis_size("blk")
    depth = leaves.bit_length() - 1
    leaf_id = lax.axis_index("leaf")
    blk_id = lax.axis_index("blk")
    core = leaf_id & 1
    yb = blk_id & 1
    zb = blk_id >> 1
    width = inverse_blocks.shape[-1]
    cases = right_side.shape[-1]
    rhs = right_side[0, 0]
    inverse = inverse_blocks[0, 0]
    couple = coupling[0, 0]
    listed_rows = coupling.shape[-1]
    counts = [width // (blocks << level) for level in range(depth + 1)]
    starts = [sum(counts[:level]) for level in range(depth + 1)]
    infos = [Level(l, leaves, blocks, width, cases) for l in range(1, depth + 1)]
    couple_starts = {}
    cursor = 0
    for level in range(depth):
        for above in range(level + 1, depth + 1):
            couple_starts[level, above] = cursor
            cursor += counts[level]
    pair_bases = []
    cursor = 0
    for level in range(depth + 1):
        pair_bases.append(cursor)
        cursor += (leaves >> level) * (depth - level)

    pair_slot = {}
    for level in range(depth):
        for above in range(level + 1, depth + 1):
            pair_slot[level, above] = SPOT + depth + len(pair_slot)

    def at():
        leaf = lax.axis_index("leaf")
        blk = lax.axis_index("blk")
        scalars = [leaf & 1, blk & 1, (leaf >> 1) & 1]
        for info in infos:
            member = leaf & ((1 << info.level) - 1)
            hi, side = split_power(member, 2 * info.pair_x)
            cell = hi * info.zbs + (blk >> 1)
            scalars.append(((cell * 2 * info.pair_x + side) * 2 + (blk & 1)) * info.rows)
        for level, above in pair_slot:
            node = leaf >> level
            scalars.append(pair_bases[level] + node * (depth - level) + (above - level - 1))
        return scalars

    def swap(value, axis, bit):
        size = leaves if axis == "leaf" else blocks
        return lax.ppermute(value, axis, [(i, i ^ bit) for i in range(size)])

    def cell_columns(rows, level):
        info = infos[level - 1]
        parts = rows.reshape(-1, info.his, 2 * info.pair_x, info.zbs, 2 * info.rows)
        return parts.transpose(0, 1, 3, 2, 4).reshape(-1, width)

    def exchange_outer(value, level):
        if level <= 1:
            return lax.all_to_all(value, "blk", 0, 0, tiled=True)
        return lax.all_to_all(
            value,
            ("leaf", "blk"),
            0,
            0,
            axis_index_groups=infos[level - 1].outer,
            tiled=True,
        )

    def exchange_inner(value, level):
        info = infos[level - 1]
        if info.his == 1:
            return lax.all_to_all(value, "blk", 0, 0, axis_index_groups=info.inner_blk, tiled=True)
        return lax.all_to_all(
            value, ("leaf", "blk"), 0, 0, axis_index_groups=info.inner, tiled=True
        )

    def coupling_block(level, above):
        begin = couple_starts[level, above]
        return couple[begin : begin + counts[level]]

    uppers = range(1, depth + 1)
    dense = {}
    expanded = kernel_call(
        functools.partial(
            expand_kernel,
            1,
            infos,
            [pair_slot[0, above] for above in uppers],
            [couple_starts[0, above] for above in uppers],
        ),
        [shaped((counts[0], width), BF16)] * depth,
        [update_rows, couple],
        scalars=at,
        flops=2 * depth * counts[0] * listed_rows * width,
    )
    for above in uppers:
        dense[0, above] = expanded[above - 1]

    spread = kernel_call(
        first_kernel,
        [shaped((blocks, counts[0], cases), BF16)],
        [(rhs, None)],
        scratch=[pltpu.VMEM((counts[0], cases), F32), pltpu.SemaphoreType.DMA],
    )[0]
    full = lax.all_to_all(spread, "blk", 0, 0, tiled=True).reshape(width, cases)
    outs = [shaped((counts[0], cases), F32)]
    for info in infos:
        shape = (info.targets, info.chunk, info.cell_rows)
        outs += [shaped(shape, BF16), shaped(shape, BF16)]
    matrix_scratch = pltpu.VMEM((counts[0], width), BF16)
    y0, *base = kernel_call(
        functools.partial(subtree_kernel, infos, starts[1:]),
        outs,
        [full, (inverse, None), (rhs, None)] + hbm([dense[0, above] for above in uppers]),
        scalars=at,
        scratch=[
            pltpu.VMEM((cases, width), F32),
            matrix_scratch,
            pltpu.VMEM((depth, counts[0], width), BF16),
            pltpu.VMEM(rhs.shape, F32),
            pltpu.SemaphoreType.DMA((1 + GROUPS * (1 + depth),)),
        ],
        flops=2 * (1 + depth) * counts[0] * width * cases,
        stay=[True, False, False] + [True, True] * (depth - 1),
    )
    received = []
    for level in uppers:
        received.append(swap(base[2 * level - 1], "leaf", 1))

    def pieces_of(value, level):
        pieces = [value]
        if infos[level - 1].pair_x == 2:
            pieces += [swap(piece, "leaf", 2) for piece in pieces]
        pieces += [swap(piece, "blk", 1) for piece in pieces]
        pieces += [swap(piece, "leaf", 1) for piece in pieces]
        return pieces

    inverse_pieces = {}
    for level in uppers:
        rows = inverse[starts[level] : starts[level] + counts[level]]
        if not infos[level - 1].direct:
            rows = cell_columns(rows, level)
        inverse_pieces[level] = pieces_of(rows, level)
        for above in range(level + 1, depth + 1):
            pieces = pieces_of(coupling_block(level, above), level)
            rows = len(pieces) * counts[level]
            dense[level, above] = kernel_call(
                functools.partial(
                    expand_kernel,
                    len(pieces),
                    [infos[above - 1]],
                    [pair_slot[level, above]],
                    None,
                ),
                [shaped((rows, width), BF16)],
                [update_rows] + pieces,
                scalars=at,
                flops=2 * rows * listed_rows * width,
            )[0]

    def sum_spread(parts, copies):
        return kernel_call(
            sum_spread_kernel, [shaped((copies,) + parts.shape[1:], BF16)], [parts]
        )[0]

    def cell_scratch(info):
        return pltpu.VMEM((info.cell_rows, width), BF16)

    ys = {}
    parts = (base[0].astype(F32) + received[0].astype(F32)).astype(BF16)
    for level in uppers:
        info = infos[level - 1]
        parts = exchange_outer(parts, level)
        gathered = exchange_inner(sum_spread(parts, info.cells), level)
        size = info.cell_rows * width * info.chunk
        count = 4 * info.pair_x
        if level == depth:
            parts = kernel_call(
                functools.partial(top_kernel, info),
                [shaped((info.cells, info.chunk, info.cell_rows), BF16)],
                [gathered] + [(piece, True) for piece in inverse_pieces[level]],
                flops=4 * size,
                stay=[False],
            )[0]
            break
        above = infos[level]
        ys[level], parts = kernel_call(
            functools.partial(forward_kernel, infos, level),
            [
                shaped((info.cell_rows, info.chunk), F32),
                shaped((above.targets, above.chunk, above.cell_rows), BF16),
            ],
            [gathered]
            + hbm(
                [base[2 * level], received[level]]
                + inverse_pieces[level]
                + [ys[j] for j in range(1, level)]
                + [dense[j, level + 1] for j in range(1, level + 1)]
            ),
            scalars=at,
            scratch=[
                pltpu.VMEM((above.chunk * above.pair_x, width), F32),
                cell_scratch(info),
                pltpu.VMEM((above.targets, above.chunk, above.cell_rows), BF16),
                pltpu.VMEM((above.targets, above.chunk, above.cell_rows), BF16),
                pltpu.SemaphoreType.DMA((count + GROUPS * level + 1 + level,)),
            ]
            + [cell_scratch(infos[j - 1]) for j in range(1, level + 1)]
            + [pltpu.VMEM(ys[j].shape, F32) for j in range(1, level)],
            flops=4 * size,
        )

    solved = {}
    swapped = {}
    z0 = y0
    for level in range(depth, 0, -1):
        info = infos[level - 1]
        if level < depth:
            higher = range(level + 1, depth + 1)
            count = 4 * info.pair_x
            parts = kernel_call(
                functools.partial(backward_kernel, infos, level),
                [shaped((info.cells, info.chunk, info.cell_rows), BF16)],
                hbm([ys[level]] + inverse_pieces[level])
                + [solved[above] for above in higher]
                + hbm([dense[level, above] for above in higher]),
                scalars=at,
                scratch=[
                    cell_scratch(info),
                    pltpu.VMEM(ys[level].shape, F32),
                    pltpu.SemaphoreType.DMA((1 + count + GROUPS * len(higher),)),
                ]
                + [cell_scratch(info)] * len(higher),
                flops=4 * info.cell_rows * width * info.chunk,
                stay=[False],
            )[0]
        parts = exchange_inner(parts, level)
        solved[level] = exchange_outer(sum_spread(parts, info.targets), level)
        swapped[level] = swap(solved[level], "leaf", 1)
        if level > 1:
            z0 = kernel_call(
                functools.partial(subtract_kernel, info),
                [shaped((counts[0], cases), F32)],
                [(z0, None), (dense[0, level], None), solved[level], swapped[level]],
                scalars=at,
                scratch=[
                    pltpu.VMEM((cases, width), BF16),
                    matrix_scratch,
                    pltpu.VMEM((counts[0], cases), F32),
                    pltpu.SemaphoreType.DMA((1 + GROUPS,)),
                ],
                flops=2 * counts[0] * width * cases,
            )[0]

    part = kernel_call(
        functools.partial(last_kernel, infos[0]),
        [shaped((blocks, cases, counts[0]), BF16)],
        [(z0, None), (dense[0, 1], None), solved[1], swapped[1], (inverse, None)],
        scalars=at,
        scratch=[
            pltpu.VMEM((cases, width), BF16),
            matrix_scratch,
            matrix_scratch,
            pltpu.VMEM((counts[0], cases), F32),
            pltpu.SemaphoreType.DMA((1 + 2 * GROUPS,)),
        ],
        flops=4 * counts[0] * width * cases,
    )[0]
    parts = lax.all_to_all(part, "blk", 0, 0, tiled=True)

    outputs = []
    for level in uppers:
        info = infos[level - 1]
        member = leaf_id & ((1 << level) - 1)
        side = member & (2 * info.pair_x - 1)
        hi = member // (2 * info.pair_x)
        offset = (side * 2 + yb) * info.rows

        def own(value):
            shape = (info.his, info.pair_x, info.zbs, 2, info.chunk, info.cell_rows)
            sizes = (1, info.pair_x, 1, 2, info.chunk, info.rows)
            taken = lax.dynamic_slice(value.reshape(shape), (hi, 0, zb, 0, 0, offset), sizes)
            return taken[0, :, 0].transpose(1, 0, 2, 3)

        mine, other = own(solved[level]), own(swapped[level])
        rows = jnp.where(
            core == 0, jnp.stack([mine, other], 1), jnp.stack([other, mine], 1)
        )
        outputs.append(rows.reshape(cases, info.rows).T)
    out = kernel_call(output_kernel, [shaped((sum(counts), cases), F32)], [parts] + outputs)[0]
    return out[None, None]


def solution(mesh):
    spec = P("leaf", "blk", None, None)
    return jax.shard_map(
        solve, mesh=mesh, in_specs=(spec, spec, spec, P()), out_specs=spec, check_vma=False
    )
```

```python
import functools

import jax
import jax.numpy as jnp
from jax import lax
from jax.experimental import pallas as pl
from jax.experimental.pallas import tpu as pltpu
from jax.sharding import PartitionSpec as P


BF16 = jnp.bfloat16
F32 = jnp.float32


def mm(a, b):
    return jnp.dot(a, b, preferred_element_type=F32)


def mm_tn(a, b):
    return lax.dot_general(a, b, (((0,), (0,)), ((), ())), preferred_element_type=F32)


def mm_nt(a, b):
    return lax.dot_general(a, b, (((1,), (1,)), ((), ())), preferred_element_type=F32)


def shaped(shape, dtype):
    return jax.ShapeDtypeStruct(tuple(shape), dtype)


def kernel_call(body, outs, args, scalars=None, scratch=(), flops=0, stay=None):
    stay = [True] * len(outs) if stay is None else stay
    values = []
    specs = []
    moved = sum(o.size * o.dtype.itemsize for o in outs)
    for arg in args:
        value, spec = arg, pl.BlockSpec(memory_space=pltpu.VMEM)
        if isinstance(arg, tuple):
            value = pltpu.with_memory_space_constraint(arg[0], pltpu.HBM)
            if arg[1] is None:
                spec = pl.BlockSpec(memory_space=pltpu.HBM)
        values.append(value)
        specs.append(spec)
        moved += value.size * value.dtype.itemsize
    return pl.pallas_call(
        body if scalars is None else lambda *refs: body(scalars(), *refs),
        out_shape=[
            pltpu.HBM(o.shape, o.dtype) if keep else o for o, keep in zip(outs, stay)
        ],
        in_specs=specs,
        out_specs=[pl.BlockSpec(memory_space=pltpu.VMEM)] * len(outs),
        scratch_shapes=list(scratch),
        compiler_params=pltpu.CompilerParams(vmem_limit_bytes=16 << 20),
        cost_estimate=pl.CostEstimate(flops=flops, bytes_accessed=moved, transcendentals=0),
    )(*values)


def hbm(values):
    return [(value, None) for value in values]


class Loads:
    def __init__(self, sems):
        self.sems = sems
        self.used = 0

    def start(self, pairs):
        copies = []
        for source, target in pairs:
            copies.append(pltpu.make_async_copy(source, target, self.sems.at[self.used]))
            copies[-1].start()
            self.used += 1
        return copies

    def rows(self, sources, target):
        pairs = []
        begin = 0
        for source in sources:
            count = source.shape[0]
            pairs.append((source, target.at[begin : begin + count, :]))
            begin += count
        return self.start(pairs)

    def groups(self, sources, target, order):
        rows = target.shape[0] // order
        if len(sources) == 1:
            source = sources[0]
            return [
                lambda g=g: self.start(
                    [(source.at[g * rows : (g + 1) * rows, :], target.at[g * rows : (g + 1) * rows, :])]
                )
                for g in range(order)
            ]
        each = len(sources) // order
        return [
            lambda g=g: self.rows(
                sources[g * each : (g + 1) * each], target.at[g * rows : (g + 1) * rows, :]
            )
            for g in range(order)
        ]


GROUPS = 2


def group_rows(total):
    size = total // GROUPS
    return [slice(g * size, (g + 1) * size) for g in range(GROUPS)]


def accumulate(total, left, right):
    half = right.shape[1] // 2
    terms = [mm_tn(left, right[:, :half]), mm_tn(left, right[:, half:])]
    return terms if total is None else [t + term for t, term in zip(total, terms)]


def wait(copies):
    for copy in copies:
        copy.wait()


def split_power(value, size):
    bits = size.bit_length() - 1
    if size == 1 << bits:
        return value >> bits, value & (size - 1)
    return value // size, value % size


class Level:
    def __init__(self, level, leaves, blocks, width, cases):
        self.level = level
        self.pair_x = 2 if level >= 2 else 1
        self.his = (1 << level) // (2 * self.pair_x)
        self.zbs = blocks // 2
        self.rows = width // (blocks << level)
        self.cells = self.his * self.zbs
        self.cell_rows = width // self.cells
        self.chunk = cases // (4 * self.pair_x)
        self.targets = self.cells * self.pair_x * 2
        outer = []
        inner = []
        middle = []
        for node in range(leaves >> level):
            base = node << level
            for side in range(2):
                outer.append(
                    [
                        (base + 2 * upper + side) * blocks + b
                        for upper in range(1 << (level - 1))
                        for b in range(blocks)
                    ]
                )
                for yb in range(2):
                    middle.append(
                        [
                            (base + 2 * upper + side) * blocks + 2 * zb + yb
                            for upper in range(1 << (level - 1))
                            for zb in range(self.zbs)
                        ]
                    )
                for xu in range(self.pair_x):
                    for yb in range(2):
                        inner.append(
                            [
                                (base + (hi * self.pair_x + xu) * 2 + side) * blocks + 2 * zb + yb
                                for hi in range(self.his)
                                for zb in range(self.zbs)
                            ]
                        )
        self.outer = outer
        self.inner = inner
        self.middle = middle
        self.inner_blk = [[2 * zb + yb for zb in range(self.zbs)] for yb in range(2)]

    @property
    def direct(self):
        return (2 * self.rows) % 128 == 0

    def natural(self):
        if not self.direct:
            return [(c * self.cell_rows, c, 0, self.cell_rows) for c in range(self.cells)]
        size = 2 * self.rows
        return [
            (
                ((hi * 2 * self.pair_x + side) * self.zbs + zb) * size,
                hi * self.zbs + zb,
                side * size,
                size,
            )
            for hi in range(self.his)
            for side in range(2 * self.pair_x)
            for zb in range(self.zbs)
        ]

    def position(self, rows):
        block, t = split_power(rows, 2 * self.rows)
        block, zpos = split_power(block, self.zbs)
        hi, side = split_power(block, 2 * self.pair_x)
        cell = hi * self.zbs + zpos
        return (cell * (2 * self.pair_x) + side) * (2 * self.rows) + t

    def target(self, hi, xu, zb, yb):
        return ((hi * self.pair_x + xu) * self.zbs + zb) * 2 + yb

    def lanes(self, cell):
        return slice(cell * self.cell_rows, (cell + 1) * self.cell_rows)

    def slots(self):
        for hi in range(self.his):
            for xu in range(self.pair_x):
                for zb in range(self.zbs):
                    index = (hi * self.pair_x + xu) * self.zbs + zb
                    yield hi * self.zbs + zb, xu, index

    def all_targets(self):
        for hi in range(self.his):
            for xu in range(self.pair_x):
                for zb in range(self.zbs):
                    for yb in range(2):
                        yield hi * self.zbs + zb, xu, yb, self.target(hi, xu, zb, yb)


CORE, YB, XU, SPOT = 0, 1, 2, 3


def first_kernel(rhs, out, rows, sem):
    copy = pltpu.make_async_copy(rhs.at[0 : rows.shape[0], :], rows, sem)
    copy.start()
    copy.wait()
    rounded = rows[...].astype(BF16)
    for n in range(out.shape[0]):
        out[n] = rounded


def expand_kernel(count, aboves, slots, begins, at, lists, *refs):
    blocks, outs = refs[:count], refs[count:]
    width = outs[0].shape[-1]
    step = min(512, width)
    for n, (info, out) in enumerate(zip(aboves, outs)):
        listed = info.position(lists[pl.ds(at[slots[n]], 1), :])
        if begins is None:
            block = jnp.concatenate([b[...] for b in blocks], 0)
        else:
            block = blocks[0][begins[n] : begins[n] + out.shape[0], :]
        for begin in range(0, width, step):
            ids = begin + lax.broadcasted_iota(jnp.int32, (step, listed.shape[-1]), 0)
            chosen = jnp.where(ids == listed, 1.0, 0.0).astype(BF16)
            out[:, begin : begin + step] = mm_nt(block, chosen).astype(BF16)


def subtree_kernel(infos, starts, at, full, inverse, rhs, *refs):
    depth = len(infos)
    sources = refs[:depth]
    outs = refs[depth : depth + 2 + 2 * depth]
    total, matrix, dense, rhs_copy, sems = refs[depth + 2 + 2 * depth :]
    loads = Loads(sems)
    rhs_load = loads.start([(rhs, rhs_copy)])
    groups = group_rows(matrix.shape[0])
    first = [start() for start in loads.groups([inverse], matrix, GROUPS)]
    later = [
        [start() for start in loads.groups([sources[n]], dense.at[n], GROUPS)]
        for n in range(depth)
    ]
    core = at[CORE]
    width = total.shape[-1]
    placed = []
    wait(rhs_load)
    for n, info in enumerate(infos):
        row_ids = at[SPOT + n] + lax.broadcasted_iota(jnp.int32, (info.rows, width), 0)
        lane_ids = lax.broadcasted_iota(jnp.int32, (info.rows, width), 1)
        spots = jnp.where(row_ids == lane_ids, 1.0, 0.0).astype(BF16)
        own = rhs_copy[starts[n] : starts[n] + info.rows, :].astype(BF16)
        placed.append(accumulate(None, own, spots))
    rounded = []
    for g, rows in enumerate(groups):
        wait(first[g])
        y = mm(matrix[rows, :], full[...])
        cut = y.shape[1] // 2
        low = at[YB] == 0
        outs[0][rows, :] = jnp.where(low, y[:, :cut], y[:, cut:])
        outs[1][rows, :] = jnp.where(low, y[:, cut:], y[:, :cut])
        rounded.append(y.astype(BF16))
    half = width // 2
    for n, info in enumerate(infos):
        term = None
        for g, rows in enumerate(groups):
            wait(later[n][g])
            term = accumulate(term, rounded[g], dense[n, rows, :])
        total[:, :half] = placed[n][0] - term[0]
        total[:, half:] = placed[n][1] - term[1]
        mine, other = outs[2 + 2 * n], outs[3 + 2 * n]
        for cell, xu, yb, target in info.all_targets():
            for side, ref in ((core, mine), (1 - core, other)):
                row = ((yb * 2 + side) * info.pair_x + xu) * info.chunk
                row = pl.multiple_of(row, info.chunk)
                value = total[pl.ds(row, info.chunk), info.lanes(cell)]
                ref[target] = value.astype(ref.dtype)


def sum_spread_kernel(parts, out):
    total = parts[0].astype(F32)
    for n in range(1, parts.shape[0]):
        total = total + parts[n].astype(F32)
    rounded = total.astype(BF16)
    for n in range(out.shape[0]):
        out[n] = rounded


def natural_rows(info, gathered):
    blocks = [
        gathered[cell][:, inside : inside + size]
        for _, cell, inside, size in info.natural()
    ]
    return jnp.concatenate(blocks, 1)


def put_spread(info, halves, out):
    value = jnp.concatenate(halves, 1).astype(BF16)
    for lane, cell, inside, size in info.natural():
        out[cell, :, inside : inside + size] = value[:, lane : lane + size]


def forward_kernel(infos, k, at, gathered, mine_hbm, received_hbm, *refs):
    info, above = infos[k - 1], infos[k]
    count = 4 * info.pair_x
    pieces = refs[:count]
    lower_y = refs[count : count + k - 1]
    sources = refs[count + k - 1 : count + 2 * k - 1]
    y_ref, out, total, matrix, mine, received, sems = refs[count + 2 * k - 1 : count + 2 * k + 6]
    dense = refs[count + 2 * k + 6 : count + 3 * k + 6]
    lower_copies = refs[count + 3 * k + 6 :]
    loads = Loads(sems)
    groups = group_rows(matrix.shape[0])
    first = [start() for start in loads.groups(pieces, matrix, GROUPS)]
    later = [
        [start() for start in loads.groups([source], dense[j], GROUPS)]
        for j, source in enumerate(sources)
    ]
    base = loads.start([(mine_hbm, mine), (received_hbm, received)])
    base += loads.start(list(zip(lower_y, lower_copies)))
    lower_y = lower_copies
    vector = natural_rows(info, gathered)
    ys = []
    for g, rows in enumerate(groups):
        wait(first[g])
        y = mm_nt(matrix[rows, :], vector)
        y_ref[rows, :] = y
        ys.append(y)
    wait(base)
    same = {}
    for j in range(1, k + 1):
        term = None
        for g, rows in enumerate(group_rows(dense[j - 1].shape[0])):
            value = ys[g] if j == k else lower_y[j - 1][rows, :]
            wait(later[j - 1][g])
            term = accumulate(term, value.astype(BF16), dense[j - 1][rows, :])
        term = jnp.concatenate(term, 1)
        same.setdefault(infos[j - 1].pair_x == above.pair_x, []).append(term)
    if False in same:
        total[...] = functools.reduce(jnp.add, same[False])
    else:
        total[...] = jnp.zeros(total.shape, F32)
    if True in same:
        term = functools.reduce(jnp.add, same[True])
        rows = pl.ds(pl.multiple_of(at[XU] * above.chunk, above.chunk), above.chunk)
        total[rows, :] = total[rows, :] + term
    for cell, xu, yb, target in above.all_targets():
        value = mine[target].astype(F32) + received[target].astype(F32)
        minus = total[xu * above.chunk : (xu + 1) * above.chunk, above.lanes(cell)]
        value = jnp.where(at[YB] == yb, value - minus, value)
        out[target] = value.astype(BF16)


def top_kernel(info, gathered, *refs):
    pieces, out = refs[:-1], refs[-1]
    each = len(pieces) // GROUPS
    vector = natural_rows(info, gathered)
    halves = None
    for g in range(GROUPS):
        matrix = jnp.concatenate([p[...] for p in pieces[g * each : (g + 1) * each]], 0)
        y = mm_nt(matrix, vector)
        halves = accumulate(halves, y.astype(BF16), matrix)
    put_spread(info, halves, out)


def backward_kernel(infos, k, at, y_hbm, *refs):
    info = infos[k - 1]
    count = 4 * info.pair_x
    uppers = infos[k:]
    many = len(uppers)
    pieces = refs[:count]
    solved = refs[count : count + many]
    sources = refs[count + many : count + 2 * many]
    out, matrix, y, sems = refs[count + 2 * many : count + 2 * many + 4]
    dense = refs[count + 2 * many + 4 :]
    loads = Loads(sems)
    y_load = loads.start([(y_hbm, y)])
    dense_loads = [loads.groups([source], dense[n], GROUPS) for n, source in enumerate(sources)]
    matrix_loads = loads.groups(pieces, matrix, GROUPS)
    first = []
    last = []
    for g in range(GROUPS):
        first.append([start[g]() for start in dense_loads])
        last.append(matrix_loads[g]())
    vectors = []
    for n, above in enumerate(uppers):
        parts = []
        for hi in range(above.his):
            for zb in range(above.zbs):
                first_slot = hi * above.pair_x * above.zbs + zb
                if above.pair_x == info.pair_x:
                    parts.append(solved[n][first_slot + at[XU] * above.zbs])
                else:
                    slots = [first_slot + xu * above.zbs for xu in range(above.pair_x)]
                    parts.append(jnp.concatenate([solved[n][slot] for slot in slots], 0))
        vectors.append(jnp.concatenate(parts, 1))
    wait(y_load)
    halves = None
    for g, rows in enumerate(group_rows(matrix.shape[0])):
        z = y[rows, :]
        for n in range(many):
            wait(first[g][n])
            z = z - mm_nt(dense[n][rows, :], vectors[n])
        wait(last[g])
        halves = accumulate(halves, z.astype(BF16), matrix[rows, :])
    put_spread(info, halves, out)


def full_cases(info, core, mine, other, full):
    for cell, xu, index in info.slots():
        for side, ref in ((core, mine), (1 - core, other)):
            row = pl.multiple_of((side * info.pair_x + xu) * info.chunk, info.chunk)
            full[pl.ds(row, info.chunk), info.lanes(cell)] = ref[index]


def subtract_kernel(info, count, at, own, near, mine, other, *refs):
    y_parts = refs[:count]
    out, full, dense, y, sems = refs[count:]
    loads = Loads(sems)
    y_load = loads.rows(y_parts, y)
    copies = [start() for start in loads.groups([own, near], dense, GROUPS)]
    full_cases(info, at[CORE], mine, other, full)
    wait(y_load)
    for g, rows in enumerate(group_rows(dense.shape[0])):
        wait(copies[g])
        out[rows, :] = y[rows, :] - mm_nt(dense[rows, :], full[...])


def last_kernel(info, at, own, near, mine, other, inverse, inverse_near, y_hbm, *refs):
    out, full, dense, matrix, y, sems = refs
    loads = Loads(sems)
    y_load = loads.start([(y_hbm, y)])
    dense_loads = loads.groups([own, near], dense, GROUPS)
    inverse_own = inverse.at[0 : inverse_near.shape[0], :]
    matrix_loads = loads.groups([inverse_own, inverse_near], matrix, GROUPS)
    copies = [(dense_loads[g](), matrix_loads[g]()) for g in range(GROUPS)]
    full_cases(info, at[CORE], mine, other, full)
    wait(y_load)
    halves = None
    for g, rows in enumerate(group_rows(dense.shape[0])):
        wait(copies[g][0])
        z = y[rows, :] - mm_nt(dense[rows, :], full[...])
        wait(copies[g][1])
        halves = accumulate(halves, z.astype(BF16), matrix[rows, :])
    value = jnp.concatenate(halves, 1).astype(BF16)
    size = out.shape[-1]
    for n in range(out.shape[0]):
        out[n] = value[:, n * size : (n + 1) * size]


def output_kernel(parts, *refs):
    rows, out = refs[:-1], refs[-1]
    totals = [parts[0].astype(F32), parts[1].astype(F32)]
    for n in range(2, parts.shape[0]):
        totals[n % 2] = totals[n % 2] + parts[n].astype(F32)
    begin = totals[0].shape[1]
    out[0:begin, :] = jnp.concatenate(totals, 0).T
    for row in rows:
        out[begin : begin + row.shape[0], :] = row[...].astype(F32)
        begin += row.shape[0]


def solve(right_side, inverse_blocks, coupling, update_rows):
    leaves = lax.axis_size("leaf")
    blocks = lax.axis_size("blk")
    depth = leaves.bit_length() - 1
    leaf_id = lax.axis_index("leaf")
    blk_id = lax.axis_index("blk")
    core = leaf_id & 1
    yb = blk_id & 1
    zb = blk_id >> 1
    width = inverse_blocks.shape[-1]
    cases = right_side.shape[-1]
    rhs = right_side[0, 0]
    inverse = inverse_blocks[0, 0]
    couple = coupling[0, 0]
    listed_rows = coupling.shape[-1]
    counts = [width // (blocks << level) for level in range(depth + 1)]
    starts = [sum(counts[:level]) for level in range(depth + 1)]
    infos = [Level(l, leaves, blocks, width, cases) for l in range(1, depth + 1)]
    couple_starts = {}
    cursor = 0
    for level in range(depth):
        for above in range(level + 1, depth + 1):
            couple_starts[level, above] = cursor
            cursor += counts[level]
    pair_bases = []
    cursor = 0
    for level in range(depth + 1):
        pair_bases.append(cursor)
        cursor += (leaves >> level) * (depth - level)

    pair_slot = {}
    for level in range(depth):
        for above in range(level + 1, depth + 1):
            pair_slot[level, above] = SPOT + depth + len(pair_slot)

    def at():
        leaf = lax.axis_index("leaf")
        blk = lax.axis_index("blk")
        scalars = [leaf & 1, blk & 1, (leaf >> 1) & 1]
        for info in infos:
            member = leaf & ((1 << info.level) - 1)
            hi, side = split_power(member, 2 * info.pair_x)
            cell = hi * info.zbs + (blk >> 1)
            scalars.append(((cell * 2 * info.pair_x + side) * 2 + (blk & 1)) * info.rows)
        for level, above in pair_slot:
            node = leaf >> level
            scalars.append(pair_bases[level] + node * (depth - level) + (above - level - 1))
        return scalars

    def swap(value, axis, bit):
        size = leaves if axis == "leaf" else blocks
        return lax.ppermute(value, axis, [(i, i ^ bit) for i in range(size)])

    def cell_columns(rows, level):
        info = infos[level - 1]
        parts = rows.reshape(-1, info.his, 2 * info.pair_x, info.zbs, 2 * info.rows)
        return parts.transpose(0, 1, 3, 2, 4).reshape(-1, width)

    def exchange_outer(value, level):
        if level <= 1:
            return lax.all_to_all(value, "blk", 0, 0, tiled=True)
        return lax.all_to_all(
            value,
            ("leaf", "blk"),
            0,
            0,
            axis_index_groups=infos[level - 1].outer,
            tiled=True,
        )

    def exchange_middle(value, level):
        info = infos[level - 1]
        if level <= 1:
            return lax.all_to_all(
                value, "blk", 0, 0, axis_index_groups=info.inner_blk, tiled=True
            )
        return lax.all_to_all(
            value, ("leaf", "blk"), 0, 0, axis_index_groups=info.middle, tiled=True
        )

    def exchange_inner(value, level):
        info = infos[level - 1]
        if info.his == 1:
            return lax.all_to_all(
                value, "blk", 0, 0, axis_index_groups=info.inner_blk, tiled=True
            )
        return lax.all_to_all(
            value, ("leaf", "blk"), 0, 0, axis_index_groups=info.inner, tiled=True
        )

    def coupling_block(level, above):
        begin = couple_starts[level, above]
        return couple[begin : begin + counts[level]]

    uppers = range(1, depth + 1)
    dense = {}
    expanded = kernel_call(
        functools.partial(
            expand_kernel,
            1,
            infos,
            [pair_slot[0, above] for above in uppers],
            [couple_starts[0, above] for above in uppers],
        ),
        [shaped((counts[0], width), BF16)] * depth,
        [update_rows, couple],
        scalars=at,
        flops=2 * depth * counts[0] * listed_rows * width,
    )
    for above in uppers:
        dense[0, above] = expanded[above - 1]

    spread = kernel_call(
        first_kernel,
        [shaped((blocks, counts[0], cases), BF16)],
        [(rhs, None)],
        scratch=[pltpu.VMEM((counts[0], cases), F32), pltpu.SemaphoreType.DMA],
    )[0]
    full = lax.all_to_all(spread, "blk", 0, 0, tiled=True).reshape(width, cases)
    outs = [shaped((counts[0], cases // 2), F32)] * 2
    for info in infos:
        shape = (info.targets, info.chunk, info.cell_rows)
        outs += [shaped(shape, BF16), shaped(shape, BF16)]
    matrix_scratch = pltpu.VMEM((counts[0], width), BF16)
    y_keep, y_send, *base = kernel_call(
        functools.partial(subtree_kernel, infos, starts[1:]),
        outs,
        [full, (inverse, None), (rhs, None)] + hbm([dense[0, above] for above in uppers]),
        scalars=at,
        scratch=[
            pltpu.VMEM((cases, width), F32),
            matrix_scratch,
            pltpu.VMEM((depth, counts[0], width), BF16),
            pltpu.VMEM(rhs.shape, F32),
            pltpu.SemaphoreType.DMA((1 + GROUPS * (1 + depth),)),
        ],
        flops=2 * (1 + depth) * counts[0] * width * cases,
        stay=[True, True, False, False] + [True, True] * (depth - 1),
    )
    received = []
    for level in uppers:
        received.append(swap(base[2 * level - 1], "leaf", 1))

    def pieces_of(value, level):
        pieces = [value]
        if infos[level - 1].pair_x == 2:
            pieces += [swap(piece, "leaf", 2) for piece in pieces]
        pieces += [swap(piece, "blk", 1) for piece in pieces]
        pieces += [swap(piece, "leaf", 1) for piece in pieces]
        return pieces

    inverse_pieces = {}
    for level in uppers:
        rows = inverse[starts[level] : starts[level] + counts[level]]
        if not infos[level - 1].direct:
            rows = cell_columns(rows, level)
        inverse_pieces[level] = pieces_of(rows, level)
        for above in range(level + 1, depth + 1):
            pieces = pieces_of(coupling_block(level, above), level)
            rows = len(pieces) * counts[level]
            dense[level, above] = kernel_call(
                functools.partial(
                    expand_kernel,
                    len(pieces),
                    [infos[above - 1]],
                    [pair_slot[level, above]],
                    None,
                ),
                [shaped((rows, width), BF16)],
                [update_rows] + pieces,
                scalars=at,
                flops=2 * rows * listed_rows * width,
            )[0]

    y_near = swap(y_send, "blk", 1)
    dense_near = {}
    for above in range(depth, 0, -1):
        block = swap(coupling_block(0, above), "blk", 1)
        dense_near[above] = kernel_call(
            functools.partial(
                expand_kernel, 1, [infos[above - 1]], [pair_slot[0, above]], None
            ),
            [shaped((counts[0], width), BF16)],
            [update_rows, block],
            scalars=at,
            flops=2 * counts[0] * listed_rows * width,
        )[0]
    inverse_near = swap(inverse[: counts[0]], "blk", 1)

    def sum_spread(parts, copies):
        return kernel_call(
            sum_spread_kernel, [shaped((copies,) + parts.shape[1:], BF16)], [parts]
        )[0]

    def cell_scratch(info):
        return pltpu.VMEM((info.cell_rows, width), BF16)

    ys = {}
    parts = (base[0].astype(F32) + received[0].astype(F32)).astype(BF16)
    for level in uppers:
        info = infos[level - 1]
        parts = exchange_outer(parts, level)
        gathered = exchange_inner(sum_spread(parts, info.cells), level)
        size = info.cell_rows * width * info.chunk
        count = 4 * info.pair_x
        if level == depth:
            parts = kernel_call(
                functools.partial(top_kernel, info),
                [shaped((info.cells, info.chunk, info.cell_rows), BF16)],
                [gathered] + [(piece, True) for piece in inverse_pieces[level]],
                flops=4 * size,
                stay=[False],
            )[0]
            break
        above = infos[level]
        ys[level], parts = kernel_call(
            functools.partial(forward_kernel, infos, level),
            [
                shaped((info.cell_rows, info.chunk), F32),
                shaped((above.targets, above.chunk, above.cell_rows), BF16),
            ],
            [gathered]
            + hbm(
                [base[2 * level], received[level]]
                + inverse_pieces[level]
                + [ys[j] for j in range(1, level)]
                + [dense[j, level + 1] for j in range(1, level + 1)]
            ),
            scalars=at,
            scratch=[
                pltpu.VMEM((above.chunk * above.pair_x, width), F32),
                cell_scratch(info),
                pltpu.VMEM((above.targets, above.chunk, above.cell_rows), BF16),
                pltpu.VMEM((above.targets, above.chunk, above.cell_rows), BF16),
                pltpu.SemaphoreType.DMA((count + GROUPS * level + 1 + level,)),
            ]
            + [cell_scratch(infos[j - 1]) for j in range(1, level + 1)]
            + [pltpu.VMEM(ys[j].shape, F32) for j in range(1, level)],
            flops=4 * size,
        )

    solved = {}
    swapped = {}
    pair_scratch = pltpu.VMEM((2 * counts[0], width), BF16)
    half_cases = cases // 2
    low = [y_keep, y_near]
    for level in range(depth, 0, -1):
        info = infos[level - 1]
        if level < depth:
            higher = range(level + 1, depth + 1)
            count = 4 * info.pair_x
            parts = kernel_call(
                functools.partial(backward_kernel, infos, level),
                [shaped((info.cells, info.chunk, info.cell_rows), BF16)],
                hbm([ys[level]] + inverse_pieces[level])
                + [solved[above] for above in higher]
                + hbm([dense[level, above] for above in higher]),
                scalars=at,
                scratch=[
                    cell_scratch(info),
                    pltpu.VMEM(ys[level].shape, F32),
                    pltpu.SemaphoreType.DMA((1 + count + GROUPS * len(higher),)),
                ]
                + [cell_scratch(info)] * len(higher),
                flops=4 * info.cell_rows * width * info.chunk,
                stay=[False],
            )[0]
        parts = exchange_inner(parts, level)
        solved[level] = exchange_middle(sum_spread(parts, info.cells * info.pair_x), level)
        swapped[level] = swap(solved[level], "leaf", 1)
        if level > 1:
            low = kernel_call(
                functools.partial(subtract_kernel, info, len(low)),
                [shaped((2 * counts[0], half_cases), F32)],
                hbm([dense[0, level], dense_near[level]])
                + [solved[level], swapped[level]]
                + hbm(low),
                scalars=at,
                scratch=[
                    pltpu.VMEM((half_cases, width), BF16),
                    pair_scratch,
                    pltpu.VMEM((2 * counts[0], half_cases), F32),
                    pltpu.SemaphoreType.DMA((2 + GROUPS,)),
                ],
                flops=2 * counts[0] * width * cases,
            )

    part = kernel_call(
        functools.partial(last_kernel, infos[0]),
        [shaped((blocks, half_cases, counts[0]), BF16)],
        hbm([dense[0, 1], dense_near[1]])
        + [solved[1], swapped[1]]
        + hbm([inverse, inverse_near, low[0]]),
        scalars=at,
        scratch=[
            pltpu.VMEM((half_cases, width), BF16),
            pair_scratch,
            pair_scratch,
            pltpu.VMEM((2 * counts[0], half_cases), F32),
            pltpu.SemaphoreType.DMA((1 + 2 * GROUPS,)),
        ],
        flops=4 * counts[0] * width * cases,
    )[0]
    parts = lax.all_to_all(part, "blk", 0, 0, tiled=True)

    keeps = []
    sends = []
    for level in uppers:
        info = infos[level - 1]
        member = leaf_id & ((1 << level) - 1)
        side = member & (2 * info.pair_x - 1)
        hi = member // (2 * info.pair_x)

        def own(value):
            shape = (info.his, info.pair_x, info.zbs, info.chunk, info.cell_rows)
            sizes = (1, info.pair_x, 1, info.chunk, 2 * info.rows)
            start = (hi, 0, zb, 0, side * 2 * info.rows)
            taken = lax.dynamic_slice(value.reshape(shape), start, sizes)
            return taken.reshape(half_cases // 2, 2 * info.rows)

        mine, other = own(solved[level]), own(swapped[level])
        both = jnp.where(
            core == 0, jnp.concatenate([mine, other], 0), jnp.concatenate([other, mine], 0)
        )
        keeps.append(jnp.where(yb == 0, both[:, : info.rows], both[:, info.rows :]))
        sends.append(jnp.where(yb == 0, both[:, info.rows :], both[:, : info.rows]))
    keep = jnp.concatenate(keeps, 1)
    near = swap(jnp.concatenate(sends, 1), "blk", 1)
    rows = jnp.where(
        yb == 0, jnp.concatenate([keep, near], 0), jnp.concatenate([near, keep], 0)
    )
    outputs = [rows.T]
    out = kernel_call(
        output_kernel, [shaped((sum(counts), cases), F32)], [parts] + outputs
    )[0]
    return out[None, None]


def solution(mesh):
    spec = P("leaf", "blk", None, None)
    return jax.shard_map(
        solve, mesh=mesh, in_specs=(spec, spec, spec, P()), out_specs=spec, check_vma=False
    )
```

```python
import functools

import jax
import jax.numpy as jnp
from jax import lax
from jax.experimental import pallas as pl
from jax.experimental.pallas import tpu as pltpu
from jax.sharding import PartitionSpec as P


BF16 = jnp.bfloat16
F32 = jnp.float32


def mm(a, b):
    return jnp.dot(a, b, preferred_element_type=F32)


def mm_tn(a, b):
    return lax.dot_general(a, b, (((0,), (0,)), ((), ())), preferred_element_type=F32)


def mm_nt(a, b):
    return lax.dot_general(a, b, (((1,), (1,)), ((), ())), preferred_element_type=F32)


def shaped(shape, dtype):
    return jax.ShapeDtypeStruct(tuple(shape), dtype)


def kernel_call(body, outs, args, scalars=None, scratch=(), flops=0, stay=None):
    stay = [True] * len(outs) if stay is None else stay
    values = []
    specs = []
    moved = sum(o.size * o.dtype.itemsize for o in outs)
    for arg in args:
        value, spec = arg, pl.BlockSpec(memory_space=pltpu.VMEM)
        if isinstance(arg, tuple):
            value = pltpu.with_memory_space_constraint(arg[0], pltpu.HBM)
            if arg[1] is None:
                spec = pl.BlockSpec(memory_space=pltpu.HBM)
            elif arg[1] is False:
                value, spec = arg[0], pl.BlockSpec(memory_space=pl.ANY)
        values.append(value)
        specs.append(spec)
        moved += value.size * value.dtype.itemsize
    return pl.pallas_call(
        body if scalars is None else lambda *refs: body(scalars(), *refs),
        out_shape=[
            pltpu.HBM(o.shape, o.dtype) if keep else o for o, keep in zip(outs, stay)
        ],
        in_specs=specs,
        out_specs=[pl.BlockSpec(memory_space=pltpu.VMEM)] * len(outs),
        scratch_shapes=list(scratch),
        compiler_params=pltpu.CompilerParams(vmem_limit_bytes=16 << 20),
        cost_estimate=pl.CostEstimate(flops=flops, bytes_accessed=moved, transcendentals=0),
    )(*values)


def hbm(values):
    return [(value, None) for value in values]


class Loads:
    def __init__(self, sems):
        self.sems = sems
        self.used = 0

    def start(self, pairs):
        copies = []
        for source, target in pairs:
            copies.append(pltpu.make_async_copy(source, target, self.sems.at[self.used]))
            copies[-1].start()
            self.used += 1
        return copies

    def rows(self, sources, target):
        pairs = []
        begin = 0
        for source in sources:
            count = source.shape[0]
            pairs.append((source, target.at[begin : begin + count, :]))
            begin += count
        return self.start(pairs)

    def groups(self, sources, target, order):
        rows = target.shape[0] // order
        if len(sources) == 1:
            source = sources[0]
            return [
                lambda g=g: self.start(
                    [(source.at[g * rows : (g + 1) * rows, :], target.at[g * rows : (g + 1) * rows, :])]
                )
                for g in range(order)
            ]
        each = len(sources) // order
        return [
            lambda g=g: self.rows(
                sources[g * each : (g + 1) * each], target.at[g * rows : (g + 1) * rows, :]
            )
            for g in range(order)
        ]


GROUPS = 2


def group_rows(total):
    size = total // GROUPS
    return [slice(g * size, (g + 1) * size) for g in range(GROUPS)]


def accumulate(total, left, right):
    half = right.shape[1] // 2
    terms = [mm_tn(left, right[:, :half]), mm_tn(left, right[:, half:])]
    return terms if total is None else [t + term for t, term in zip(total, terms)]


def wait(copies):
    for copy in copies:
        copy.wait()


def split_power(value, size):
    bits = size.bit_length() - 1
    if size == 1 << bits:
        return value >> bits, value & (size - 1)
    return value // size, value % size


class Level:
    def __init__(self, level, leaves, blocks, width, cases):
        self.level = level
        self.pair_x = 2 if level >= 2 else 1
        self.his = (1 << level) // (2 * self.pair_x)
        self.zbs = blocks // 2
        self.rows = width // (blocks << level)
        self.cells = self.his * self.zbs
        self.cell_rows = width // self.cells
        self.chunk = cases // (4 * self.pair_x)
        self.targets = self.cells * self.pair_x * 2
        outer = []
        inner = []
        middle = []
        for node in range(leaves >> level):
            base = node << level
            for side in range(2):
                outer.append(
                    [
                        (base + 2 * upper + side) * blocks + b
                        for upper in range(1 << (level - 1))
                        for b in range(blocks)
                    ]
                )
                for yb in range(2):
                    middle.append(
                        [
                            (base + 2 * upper + side) * blocks + 2 * zb + yb
                            for upper in range(1 << (level - 1))
                            for zb in range(self.zbs)
                        ]
                    )
                for xu in range(self.pair_x):
                    for yb in range(2):
                        inner.append(
                            [
                                (base + (hi * self.pair_x + xu) * 2 + side) * blocks + 2 * zb + yb
                                for hi in range(self.his)
                                for zb in range(self.zbs)
                            ]
                        )
        self.outer = outer
        self.inner = inner
        self.middle = middle
        self.inner_blk = [[2 * zb + yb for zb in range(self.zbs)] for yb in range(2)]

    @property
    def direct(self):
        return (2 * self.rows) % 128 == 0

    def natural(self):
        if not self.direct:
            return [(c * self.cell_rows, c, 0, self.cell_rows) for c in range(self.cells)]
        size = 2 * self.rows
        return [
            (
                ((hi * 2 * self.pair_x + side) * self.zbs + zb) * size,
                hi * self.zbs + zb,
                side * size,
                size,
            )
            for hi in range(self.his)
            for side in range(2 * self.pair_x)
            for zb in range(self.zbs)
        ]

    def position(self, rows):
        block, t = split_power(rows, 2 * self.rows)
        block, zpos = split_power(block, self.zbs)
        hi, side = split_power(block, 2 * self.pair_x)
        cell = hi * self.zbs + zpos
        return (cell * (2 * self.pair_x) + side) * (2 * self.rows) + t

    def target(self, hi, xu, zb, yb):
        return ((hi * self.pair_x + xu) * self.zbs + zb) * 2 + yb

    def lanes(self, cell):
        return slice(cell * self.cell_rows, (cell + 1) * self.cell_rows)

    def slots(self):
        for hi in range(self.his):
            for xu in range(self.pair_x):
                for zb in range(self.zbs):
                    index = (hi * self.pair_x + xu) * self.zbs + zb
                    yield hi * self.zbs + zb, xu, index

    def all_targets(self):
        for hi in range(self.his):
            for xu in range(self.pair_x):
                for zb in range(self.zbs):
                    for yb in range(2):
                        yield hi * self.zbs + zb, xu, yb, self.target(hi, xu, zb, yb)


CORE, YB, XU, SPOT = 0, 1, 2, 3


def first_kernel(rhs, out, rows, sem):
    copy = pltpu.make_async_copy(rhs.at[0 : rows.shape[0], :], rows, sem)
    copy.start()
    copy.wait()
    rounded = rows[...].astype(BF16)
    for n in range(out.shape[0]):
        out[n] = rounded


def expand_kernel(count, aboves, slots, begins, at, lists, *refs):
    blocks, outs = refs[:count], refs[count:]
    width = outs[0].shape[-1]
    step = min(512, width)
    for n, (info, out) in enumerate(zip(aboves, outs)):
        listed = info.position(lists[pl.ds(at[slots[n]], 1), :])
        if begins is None:
            block = jnp.concatenate([b[...] for b in blocks], 0)
        else:
            block = blocks[0][begins[n] : begins[n] + out.shape[0], :]
        for begin in range(0, width, step):
            ids = begin + lax.broadcasted_iota(jnp.int32, (step, listed.shape[-1]), 0)
            chosen = jnp.where(ids == listed, 1.0, 0.0).astype(BF16)
            out[:, begin : begin + step] = mm_nt(block, chosen).astype(BF16)


def subtree_kernel(infos, starts, at, full, inverse, rhs, *refs):
    depth = len(infos)
    sources = refs[:depth]
    outs = refs[depth : depth + 2 + 2 * depth]
    total, matrix, dense, rhs_copy, sems = refs[depth + 2 + 2 * depth :]
    loads = Loads(sems)
    rhs_load = loads.start([(rhs, rhs_copy)])
    groups = group_rows(matrix.shape[0])
    first = [start() for start in loads.groups([inverse], matrix, GROUPS)]
    later = [
        [start() for start in loads.groups([sources[n]], dense.at[n], GROUPS)]
        for n in range(depth)
    ]
    core = at[CORE]
    width = total.shape[-1]
    placed = []
    wait(rhs_load)
    for n, info in enumerate(infos):
        row_ids = at[SPOT + n] + lax.broadcasted_iota(jnp.int32, (info.rows, width), 0)
        lane_ids = lax.broadcasted_iota(jnp.int32, (info.rows, width), 1)
        spots = jnp.where(row_ids == lane_ids, 1.0, 0.0).astype(BF16)
        own = rhs_copy[starts[n] : starts[n] + info.rows, :].astype(BF16)
        placed.append(accumulate(None, own, spots))
    rounded = []
    for g, rows in enumerate(groups):
        wait(first[g])
        y = mm(matrix[rows, :], full[...])
        cut = y.shape[1] // 2
        low = at[YB] == 0
        outs[0][rows, :] = jnp.where(low, y[:, :cut], y[:, cut:])
        outs[1][rows, :] = jnp.where(low, y[:, cut:], y[:, :cut])
        rounded.append(y.astype(BF16))
    half = width // 2
    for n, info in enumerate(infos):
        term = None
        for g, rows in enumerate(groups):
            wait(later[n][g])
            term = accumulate(term, rounded[g], dense[n, rows, :])
        total[:, :half] = placed[n][0] - term[0]
        total[:, half:] = placed[n][1] - term[1]
        mine, other = outs[2 + 2 * n], outs[3 + 2 * n]
        for cell, xu, yb, target in info.all_targets():
            for side, ref in ((core, mine), (1 - core, other)):
                row = ((yb * 2 + side) * info.pair_x + xu) * info.chunk
                row = pl.multiple_of(row, info.chunk)
                value = total[pl.ds(row, info.chunk), info.lanes(cell)]
                ref[target] = value.astype(ref.dtype)


def sum_spread_kernel(parts, out):
    total = parts[0].astype(F32)
    for n in range(1, parts.shape[0]):
        total = total + parts[n].astype(F32)
    rounded = total.astype(BF16)
    for n in range(out.shape[0]):
        out[n] = rounded


def natural_rows(info, gathered):
    blocks = [
        gathered[cell][:, inside : inside + size]
        for _, cell, inside, size in info.natural()
    ]
    return jnp.concatenate(blocks, 1)


def put_spread(info, halves, out):
    value = jnp.concatenate(halves, 1).astype(BF16)
    for lane, cell, inside, size in info.natural():
        out[cell, :, inside : inside + size] = value[:, lane : lane + size]


def forward_kernel(infos, k, at, gathered, mine_hbm, received_hbm, *refs):
    info, above = infos[k - 1], infos[k]
    count = 4 * info.pair_x
    pieces = refs[:count]
    lower_y = refs[count : count + k - 1]
    sources = refs[count + k - 1 : count + 2 * k - 1]
    y_ref, out, total, matrix, mine, received, sems = refs[count + 2 * k - 1 : count + 2 * k + 6]
    dense = refs[count + 2 * k + 6 : count + 3 * k + 6]
    lower_copies = refs[count + 3 * k + 6 :]
    loads = Loads(sems)
    groups = group_rows(matrix.shape[0])
    first = [start() for start in loads.groups(pieces, matrix, GROUPS)]
    later = [
        [start() for start in loads.groups([source], dense[j], GROUPS)]
        for j, source in enumerate(sources)
    ]
    base = loads.start([(mine_hbm, mine), (received_hbm, received)])
    base += loads.start(list(zip(lower_y, lower_copies)))
    lower_y = lower_copies
    vector = natural_rows(info, gathered)
    ys = []
    for g, rows in enumerate(groups):
        wait(first[g])
        y = mm_nt(matrix[rows, :], vector)
        y_ref[rows, :] = y
        ys.append(y)
    wait(base)
    same = {}
    for j in range(1, k + 1):
        term = None
        for g, rows in enumerate(group_rows(dense[j - 1].shape[0])):
            value = ys[g] if j == k else lower_y[j - 1][rows, :]
            wait(later[j - 1][g])
            term = accumulate(term, value.astype(BF16), dense[j - 1][rows, :])
        term = jnp.concatenate(term, 1)
        same.setdefault(infos[j - 1].pair_x == above.pair_x, []).append(term)
    if False in same:
        total[...] = functools.reduce(jnp.add, same[False])
    else:
        total[...] = jnp.zeros(total.shape, F32)
    if True in same:
        term = functools.reduce(jnp.add, same[True])
        rows = pl.ds(pl.multiple_of(at[XU] * above.chunk, above.chunk), above.chunk)
        total[rows, :] = total[rows, :] + term
    for cell, xu, index in above.slots():
        value = mine[index].astype(F32) + received[index].astype(F32)
        minus = total[xu * above.chunk : (xu + 1) * above.chunk, above.lanes(cell)]
        out[index] = (value - minus).astype(BF16)


def top_kernel(info, gathered, *refs):
    pieces, out = refs[:-1], refs[-1]
    each = len(pieces) // GROUPS
    vector = natural_rows(info, gathered)
    halves = None
    for g in range(GROUPS):
        matrix = jnp.concatenate([p[...] for p in pieces[g * each : (g + 1) * each]], 0)
        y = mm_nt(matrix, vector)
        halves = accumulate(halves, y.astype(BF16), matrix)
    put_spread(info, halves, out)


def backward_kernel(infos, k, at, y_hbm, *refs):
    info = infos[k - 1]
    count = 4 * info.pair_x
    uppers = infos[k:]
    many = len(uppers)
    pieces = refs[:count]
    solved = refs[count : count + many]
    sources = refs[count + many : count + 2 * many]
    out, matrix, y, sems = refs[count + 2 * many : count + 2 * many + 4]
    dense = refs[count + 2 * many + 4 :]
    loads = Loads(sems)
    y_load = loads.start([(y_hbm, y)])
    dense_loads = [loads.groups([source], dense[n], GROUPS) for n, source in enumerate(sources)]
    matrix_loads = loads.groups(pieces, matrix, GROUPS)
    first = []
    last = []
    for g in range(GROUPS):
        first.append([start[g]() for start in dense_loads])
        last.append(matrix_loads[g]())
    vectors = []
    for n, above in enumerate(uppers):
        parts = []
        for hi in range(above.his):
            for zb in range(above.zbs):
                first_slot = hi * above.pair_x * above.zbs + zb
                if above.pair_x == info.pair_x:
                    parts.append(solved[n][first_slot + at[XU] * above.zbs])
                else:
                    slots = [first_slot + xu * above.zbs for xu in range(above.pair_x)]
                    parts.append(jnp.concatenate([solved[n][slot] for slot in slots], 0))
        vectors.append(jnp.concatenate(parts, 1))
    wait(y_load)
    halves = None
    for g, rows in enumerate(group_rows(matrix.shape[0])):
        z = y[rows, :]
        for n in range(many):
            wait(first[g][n])
            z = z - mm_nt(dense[n][rows, :], vectors[n])
        wait(last[g])
        halves = accumulate(halves, z.astype(BF16), matrix[rows, :])
    put_spread(info, halves, out)


def full_cases(info, core, mine, other, full):
    for cell, xu, index in info.slots():
        for side, ref in ((core, mine), (1 - core, other)):
            row = pl.multiple_of((side * info.pair_x + xu) * info.chunk, info.chunk)
            full[pl.ds(row, info.chunk), info.lanes(cell)] = ref[index]


def subtract_kernel(info, count, at, own, near, mine, other, *refs):
    y_parts = refs[:count]
    out, full, dense, y, sems = refs[count:]
    loads = Loads(sems)
    y_load = loads.rows(y_parts, y)
    copies = [start() for start in loads.groups([own, near], dense, GROUPS)]
    full_cases(info, at[CORE], mine, other, full)
    wait(y_load)
    for g, rows in enumerate(group_rows(dense.shape[0])):
        wait(copies[g])
        out[rows, :] = y[rows, :] - mm_nt(dense[rows, :], full[...])


def last_kernel(info, at, own, near, mine, other, inverse, inverse_near, y_hbm, *refs):
    out, full, dense, matrix, y, sems = refs
    loads = Loads(sems)
    y_load = loads.start([(y_hbm, y)])
    dense_loads = loads.groups([own, near], dense, GROUPS)
    inverse_own = inverse.at[0 : inverse_near.shape[0], :]
    matrix_loads = loads.groups([inverse_own, inverse_near], matrix, GROUPS)
    copies = [(dense_loads[g](), matrix_loads[g]()) for g in range(GROUPS)]
    full_cases(info, at[CORE], mine, other, full)
    wait(y_load)
    halves = None
    for g, rows in enumerate(group_rows(dense.shape[0])):
        wait(copies[g][0])
        z = y[rows, :] - mm_nt(dense[rows, :], full[...])
        wait(copies[g][1])
        halves = accumulate(halves, z.astype(BF16), matrix[rows, :])
    value = jnp.concatenate(halves, 1).astype(BF16)
    size = out.shape[-1]
    for n in range(out.shape[0]):
        out[n] = value[:, n * size : (n + 1) * size]


def output_kernel(parts, *refs):
    rows, out = refs[:-1], refs[-1]
    totals = [parts[0].astype(F32), parts[1].astype(F32)]
    for n in range(2, parts.shape[0]):
        totals[n % 2] = totals[n % 2] + parts[n].astype(F32)
    begin = totals[0].shape[1]
    out[0:begin, :] = jnp.concatenate(totals, 0).T
    for row in rows:
        out[begin : begin + row.shape[0], :] = row[...].astype(F32)
        begin += row.shape[0]


def solve(right_side, inverse_blocks, coupling, update_rows):
    leaves = lax.axis_size("leaf")
    blocks = lax.axis_size("blk")
    depth = leaves.bit_length() - 1
    leaf_id = lax.axis_index("leaf")
    blk_id = lax.axis_index("blk")
    core = leaf_id & 1
    yb = blk_id & 1
    zb = blk_id >> 1
    width = inverse_blocks.shape[-1]
    cases = right_side.shape[-1]
    rhs = right_side[0, 0]
    inverse = inverse_blocks[0, 0]
    couple = coupling[0, 0]
    listed_rows = coupling.shape[-1]
    counts = [width // (blocks << level) for level in range(depth + 1)]
    starts = [sum(counts[:level]) for level in range(depth + 1)]
    infos = [Level(l, leaves, blocks, width, cases) for l in range(1, depth + 1)]
    couple_starts = {}
    cursor = 0
    for level in range(depth):
        for above in range(level + 1, depth + 1):
            couple_starts[level, above] = cursor
            cursor += counts[level]
    pair_bases = []
    cursor = 0
    for level in range(depth + 1):
        pair_bases.append(cursor)
        cursor += (leaves >> level) * (depth - level)

    pair_slot = {}
    for level in range(depth):
        for above in range(level + 1, depth + 1):
            pair_slot[level, above] = SPOT + depth + len(pair_slot)

    def at():
        leaf = lax.axis_index("leaf")
        blk = lax.axis_index("blk")
        scalars = [leaf & 1, blk & 1, (leaf >> 1) & 1]
        for info in infos:
            member = leaf & ((1 << info.level) - 1)
            hi, side = split_power(member, 2 * info.pair_x)
            cell = hi * info.zbs + (blk >> 1)
            scalars.append(((cell * 2 * info.pair_x + side) * 2 + (blk & 1)) * info.rows)
        for level, above in pair_slot:
            node = leaf >> level
            scalars.append(pair_bases[level] + node * (depth - level) + (above - level - 1))
        return scalars

    def swap(value, axis, bit):
        size = leaves if axis == "leaf" else blocks
        return lax.ppermute(value, axis, [(i, i ^ bit) for i in range(size)])

    def cell_columns(rows, level):
        info = infos[level - 1]
        parts = rows.reshape(-1, info.his, 2 * info.pair_x, info.zbs, 2 * info.rows)
        return parts.transpose(0, 1, 3, 2, 4).reshape(-1, width)

    def exchange_outer(value, level):
        if level <= 1:
            return lax.all_to_all(value, "blk", 0, 0, tiled=True)
        return lax.all_to_all(
            value,
            ("leaf", "blk"),
            0,
            0,
            axis_index_groups=infos[level - 1].outer,
            tiled=True,
        )

    def exchange_middle(value, level):
        info = infos[level - 1]
        if level <= 1:
            return lax.all_to_all(
                value, "blk", 0, 0, axis_index_groups=info.inner_blk, tiled=True
            )
        return lax.all_to_all(
            value, ("leaf", "blk"), 0, 0, axis_index_groups=info.middle, tiled=True
        )

    def exchange_inner(value, level):
        info = infos[level - 1]
        if info.his == 1:
            return lax.all_to_all(
                value, "blk", 0, 0, axis_index_groups=info.inner_blk, tiled=True
            )
        return lax.all_to_all(
            value, ("leaf", "blk"), 0, 0, axis_index_groups=info.inner, tiled=True
        )

    def coupling_block(level, above):
        begin = couple_starts[level, above]
        return couple[begin : begin + counts[level]]

    uppers = range(1, depth + 1)
    dense = {}
    expanded = kernel_call(
        functools.partial(
            expand_kernel,
            1,
            infos,
            [pair_slot[0, above] for above in uppers],
            [couple_starts[0, above] for above in uppers],
        ),
        [shaped((counts[0], width), BF16)] * depth,
        [update_rows, couple],
        scalars=at,
        flops=2 * depth * counts[0] * listed_rows * width,
    )
    for above in uppers:
        dense[0, above] = expanded[above - 1]

    spread = kernel_call(
        first_kernel,
        [shaped((blocks, counts[0], cases), BF16)],
        [(rhs, None)],
        scratch=[pltpu.VMEM((counts[0], cases), F32), pltpu.SemaphoreType.DMA],
    )[0]
    full = lax.all_to_all(spread, "blk", 0, 0, tiled=True).reshape(width, cases)
    outs = [shaped((counts[0], cases // 2), F32)] * 2
    for info in infos:
        shape = (info.targets, info.chunk, info.cell_rows)
        outs += [shaped(shape, BF16), shaped(shape, BF16)]
    matrix_scratch = pltpu.VMEM((counts[0], width), BF16)
    y_keep, y_send, *base = kernel_call(
        functools.partial(subtree_kernel, infos, starts[1:]),
        outs,
        [full, (inverse, None), (rhs, None)] + hbm([dense[0, above] for above in uppers]),
        scalars=at,
        scratch=[
            pltpu.VMEM((cases, width), F32),
            matrix_scratch,
            pltpu.VMEM((depth, counts[0], width), BF16),
            pltpu.VMEM(rhs.shape, F32),
            pltpu.SemaphoreType.DMA((1 + GROUPS * (1 + depth),)),
        ],
        flops=2 * (1 + depth) * counts[0] * width * cases,
        stay=[True, True, False, False] + [True, True] * (depth - 1),
    )
    received = []
    for level in uppers:
        received.append(swap(base[2 * level - 1], "leaf", 1))
    paired = {}
    for level in range(2, depth + 1):
        info = infos[level - 1]
        both = base[2 * level - 2].astype(F32) + received[level - 1].astype(F32)
        both = both.astype(BF16).reshape(-1, 2, info.chunk, info.cell_rows)
        keep = lax.dynamic_index_in_dim(both, yb, 1, keepdims=False)
        send = lax.dynamic_index_in_dim(both, 1 - yb, 1, keepdims=False)
        paired[level] = keep, swap(send, "blk", 1)

    def pieces_of(value, level):
        pieces = [value]
        if infos[level - 1].pair_x == 2:
            pieces += [swap(piece, "leaf", 2) for piece in pieces]
        pieces += [swap(piece, "blk", 1) for piece in pieces]
        pieces += [swap(piece, "leaf", 1) for piece in pieces]
        return pieces

    inverse_pieces = {}
    for level in uppers:
        rows = inverse[starts[level] : starts[level] + counts[level]]
        if not infos[level - 1].direct:
            rows = cell_columns(rows, level)
        inverse_pieces[level] = pieces_of(rows, level)
        for above in range(level + 1, depth + 1):
            pieces = pieces_of(coupling_block(level, above), level)
            rows = len(pieces) * counts[level]
            dense[level, above] = kernel_call(
                functools.partial(
                    expand_kernel,
                    len(pieces),
                    [infos[above - 1]],
                    [pair_slot[level, above]],
                    None,
                ),
                [shaped((rows, width), BF16)],
                [update_rows] + pieces,
                scalars=at,
                flops=2 * rows * listed_rows * width,
            )[0]

    y_near = swap(y_send, "blk", 1)
    dense_near = {}
    for above in range(depth, 0, -1):
        block = swap(coupling_block(0, above), "blk", 1)
        dense_near[above] = kernel_call(
            functools.partial(
                expand_kernel, 1, [infos[above - 1]], [pair_slot[0, above]], None
            ),
            [shaped((counts[0], width), BF16)],
            [update_rows, block],
            scalars=at,
            flops=2 * counts[0] * listed_rows * width,
        )[0]
    inverse_near = swap(inverse[: counts[0]], "blk", 1)

    def sum_spread(parts, copies):
        return kernel_call(
            sum_spread_kernel, [shaped((copies,) + parts.shape[1:], BF16)], [parts]
        )[0]

    def cell_scratch(info):
        return pltpu.VMEM((info.cell_rows, width), BF16)

    ys = {}
    parts = (base[0].astype(F32) + received[0].astype(F32)).astype(BF16)
    for level in uppers:
        info = infos[level - 1]
        parts = (exchange_outer if level == 1 else exchange_middle)(parts, level)
        gathered = exchange_inner(sum_spread(parts, info.cells), level)
        size = info.cell_rows * width * info.chunk
        count = 4 * info.pair_x
        if level == depth:
            parts = kernel_call(
                functools.partial(top_kernel, info),
                [shaped((info.cells, info.chunk, info.cell_rows), BF16)],
                [gathered] + [(piece, True) for piece in inverse_pieces[level]],
                flops=4 * size,
                stay=[False],
            )[0]
            break
        above = infos[level]
        ys[level], parts = kernel_call(
            functools.partial(forward_kernel, infos, level),
            [
                shaped((info.cell_rows, info.chunk), F32),
                shaped((above.targets // 2, above.chunk, above.cell_rows), BF16),
            ],
            [gathered]
            + hbm(
                list(paired[level + 1])
                + inverse_pieces[level]
                + [ys[j] for j in range(1, level)]
                + [dense[j, level + 1] for j in range(1, level + 1)]
            ),
            scalars=at,
            scratch=[
                pltpu.VMEM((above.chunk * above.pair_x, width), F32),
                cell_scratch(info),
                pltpu.VMEM((above.targets // 2, above.chunk, above.cell_rows), BF16),
                pltpu.VMEM((above.targets // 2, above.chunk, above.cell_rows), BF16),
                pltpu.SemaphoreType.DMA((count + GROUPS * level + 1 + level,)),
            ]
            + [cell_scratch(infos[j - 1]) for j in range(1, level + 1)]
            + [pltpu.VMEM(ys[j].shape, F32) for j in range(1, level)],
            flops=4 * size,
        )

    solved = {}
    swapped = {}
    pair_scratch = pltpu.VMEM((2 * counts[0], width), BF16)
    half_cases = cases // 2
    low = [y_keep, y_near]
    for level in range(depth, 0, -1):
        info = infos[level - 1]
        if level < depth:
            higher = range(level + 1, depth + 1)
            count = 4 * info.pair_x
            parts = kernel_call(
                functools.partial(backward_kernel, infos, level),
                [shaped((info.cells, info.chunk, info.cell_rows), BF16)],
                hbm([ys[level]] + inverse_pieces[level])
                + [solved[above] for above in higher]
                + hbm([dense[level, above] for above in higher]),
                scalars=at,
                scratch=[
                    cell_scratch(info),
                    pltpu.VMEM(ys[level].shape, F32),
                    pltpu.SemaphoreType.DMA((1 + count + GROUPS * len(higher),)),
                ]
                + [cell_scratch(info)] * len(higher),
                flops=4 * info.cell_rows * width * info.chunk,
                stay=[False],
            )[0]
        parts = exchange_inner(parts, level)
        solved[level] = exchange_middle(sum_spread(parts, info.cells * info.pair_x), level)
        swapped[level] = swap(solved[level], "leaf", 1)
        if level > 1:
            low = kernel_call(
                functools.partial(subtract_kernel, info, len(low)),
                [shaped((2 * counts[0], half_cases), F32)],
                hbm([dense[0, level], dense_near[level]])
                + [solved[level], swapped[level]]
                + [(low[0], None)]
                + [(value, False) for value in low[1:]],
                scalars=at,
                scratch=[
                    pltpu.VMEM((half_cases, width), BF16),
                    pair_scratch,
                    pltpu.VMEM((2 * counts[0], half_cases), F32),
                    pltpu.SemaphoreType.DMA((2 + GROUPS,)),
                ],
                flops=2 * counts[0] * width * cases,
            )

    part = kernel_call(
        functools.partial(last_kernel, infos[0]),
        [shaped((blocks, half_cases, counts[0]), BF16)],
        hbm([dense[0, 1], dense_near[1]])
        + [solved[1], swapped[1]]
        + [(inverse, None), (inverse_near, False), (low[0], None)],
        scalars=at,
        scratch=[
            pltpu.VMEM((half_cases, width), BF16),
            pair_scratch,
            pair_scratch,
            pltpu.VMEM((2 * counts[0], half_cases), F32),
            pltpu.SemaphoreType.DMA((1 + 2 * GROUPS,)),
        ],
        flops=4 * counts[0] * width * cases,
    )[0]
    parts = lax.all_to_all(part, "blk", 0, 0, tiled=True)

    keeps = []
    sends = []
    for level in uppers:
        info = infos[level - 1]
        member = leaf_id & ((1 << level) - 1)
        side = member & (2 * info.pair_x - 1)
        hi = member // (2 * info.pair_x)

        def own(value):
            shape = (info.his, info.pair_x, info.zbs, info.chunk, info.cell_rows)
            sizes = (1, info.pair_x, 1, info.chunk, 2 * info.rows)
            start = (hi, 0, zb, 0, side * 2 * info.rows)
            taken = lax.dynamic_slice(value.reshape(shape), start, sizes)
            return taken.reshape(half_cases // 2, 2 * info.rows)

        mine, other = own(solved[level]), own(swapped[level])
        both = jnp.where(
            core == 0, jnp.concatenate([mine, other], 0), jnp.concatenate([other, mine], 0)
        )
        keeps.append(jnp.where(yb == 0, both[:, : info.rows], both[:, info.rows :]))
        sends.append(jnp.where(yb == 0, both[:, info.rows :], both[:, : info.rows]))
    keep = jnp.concatenate(keeps, 1)
    near = swap(jnp.concatenate(sends, 1), "blk", 1)
    rows = jnp.where(
        yb == 0, jnp.concatenate([keep, near], 0), jnp.concatenate([near, keep], 0)
    )
    outputs = [rows.T]
    out = kernel_call(
        output_kernel, [shaped((sum(counts), cases), F32)], [parts] + outputs
    )[0]
    return out[None, None]


def solution(mesh):
    spec = P("leaf", "blk", None, None)
    return jax.shard_map(
        solve, mesh=mesh, in_specs=(spec, spec, spec, P()), out_specs=spec, check_vma=False
    )
```

```python
import functools

import jax
import jax.numpy as jnp
from jax import lax
from jax.experimental import pallas as pl
from jax.experimental.pallas import tpu as pltpu
from jax.sharding import PartitionSpec as P


BF16 = jnp.bfloat16
F32 = jnp.float32


def mm(a, b):
    return jnp.dot(a, b, preferred_element_type=F32)


def mm_tn(a, b):
    return lax.dot_general(a, b, (((0,), (0,)), ((), ())), preferred_element_type=F32)


def mm_nt(a, b):
    return lax.dot_general(a, b, (((1,), (1,)), ((), ())), preferred_element_type=F32)


def shaped(shape, dtype):
    return jax.ShapeDtypeStruct(tuple(shape), dtype)


def kernel_call(body, outs, args, scalars=None, scratch=(), flops=0, stay=None):
    stay = [True] * len(outs) if stay is None else stay
    values = []
    specs = []
    moved = sum(o.size * o.dtype.itemsize for o in outs)
    for arg in args:
        value, spec = arg, pl.BlockSpec(memory_space=pltpu.VMEM)
        if isinstance(arg, tuple):
            value = pltpu.with_memory_space_constraint(arg[0], pltpu.HBM)
            if arg[1] is None:
                spec = pl.BlockSpec(memory_space=pltpu.HBM)
            elif arg[1] is False:
                value, spec = arg[0], pl.BlockSpec(memory_space=pl.ANY)
        values.append(value)
        specs.append(spec)
        moved += value.size * value.dtype.itemsize
    return pl.pallas_call(
        body if scalars is None else lambda *refs: body(scalars(), *refs),
        out_shape=[
            pltpu.HBM(o.shape, o.dtype) if keep else o for o, keep in zip(outs, stay)
        ],
        in_specs=specs,
        out_specs=[pl.BlockSpec(memory_space=pltpu.VMEM)] * len(outs),
        scratch_shapes=list(scratch),
        compiler_params=pltpu.CompilerParams(vmem_limit_bytes=16 << 20),
        cost_estimate=pl.CostEstimate(flops=flops, bytes_accessed=moved, transcendentals=0),
    )(*values)


def hbm(values):
    return [(value, None) for value in values]


class Loads:
    def __init__(self, sems):
        self.sems = sems
        self.used = 0

    def start(self, pairs):
        copies = []
        for source, target in pairs:
            copies.append(pltpu.make_async_copy(source, target, self.sems.at[self.used]))
            copies[-1].start()
            self.used += 1
        return copies

    def rows(self, sources, target):
        pairs = []
        begin = 0
        for source in sources:
            count = source.shape[0]
            pairs.append((source, target.at[begin : begin + count, :]))
            begin += count
        return self.start(pairs)

    def groups(self, sources, target, order):
        rows = target.shape[0] // order
        if len(sources) == 1:
            source = sources[0]
            return [
                lambda g=g: self.start(
                    [(source.at[g * rows : (g + 1) * rows, :], target.at[g * rows : (g + 1) * rows, :])]
                )
                for g in range(order)
            ]
        each = len(sources) // order
        return [
            lambda g=g: self.rows(
                sources[g * each : (g + 1) * each], target.at[g * rows : (g + 1) * rows, :]
            )
            for g in range(order)
        ]


GROUPS = 2


def group_rows(total):
    size = total // GROUPS
    return [slice(g * size, (g + 1) * size) for g in range(GROUPS)]


def accumulate(total, left, right):
    half = right.shape[1] // 2
    terms = [mm_tn(left, right[:, :half]), mm_tn(left, right[:, half:])]
    return terms if total is None else [t + term for t, term in zip(total, terms)]


def wait(copies):
    for copy in copies:
        copy.wait()


def split_power(value, size):
    bits = size.bit_length() - 1
    if size == 1 << bits:
        return value >> bits, value & (size - 1)
    return value // size, value % size


class Level:
    def __init__(self, level, leaves, blocks, width, cases):
        self.level = level
        self.pair_x = 2 if level >= 2 else 1
        self.his = (1 << level) // (2 * self.pair_x)
        self.zbs = blocks // 2
        self.rows = width // (blocks << level)
        self.cells = self.his * self.zbs
        self.cell_rows = width // self.cells
        self.chunk = cases // (4 * self.pair_x)
        self.targets = self.cells * self.pair_x * 2
        outer = []
        inner = []
        middle = []
        for node in range(leaves >> level):
            base = node << level
            for side in range(2):
                outer.append(
                    [
                        (base + 2 * upper + side) * blocks + b
                        for upper in range(1 << (level - 1))
                        for b in range(blocks)
                    ]
                )
                for yb in range(2):
                    middle.append(
                        [
                            (base + 2 * upper + side) * blocks + 2 * zb + yb
                            for upper in range(1 << (level - 1))
                            for zb in range(self.zbs)
                        ]
                    )
                for xu in range(self.pair_x):
                    for yb in range(2):
                        inner.append(
                            [
                                (base + (hi * self.pair_x + xu) * 2 + side) * blocks + 2 * zb + yb
                                for hi in range(self.his)
                                for zb in range(self.zbs)
                            ]
                        )
        self.outer = outer
        self.inner = inner
        self.middle = middle
        self.inner_blk = [[2 * zb + yb for zb in range(self.zbs)] for yb in range(2)]

    @property
    def direct(self):
        return (2 * self.rows) % 128 == 0

    def natural(self):
        if not self.direct:
            return [(c * self.cell_rows, c, 0, self.cell_rows) for c in range(self.cells)]
        size = 2 * self.rows
        return [
            (
                ((hi * 2 * self.pair_x + side) * self.zbs + zb) * size,
                hi * self.zbs + zb,
                side * size,
                size,
            )
            for hi in range(self.his)
            for side in range(2 * self.pair_x)
            for zb in range(self.zbs)
        ]

    def position(self, rows):
        block, t = split_power(rows, 2 * self.rows)
        block, zpos = split_power(block, self.zbs)
        hi, side = split_power(block, 2 * self.pair_x)
        cell = hi * self.zbs + zpos
        return (cell * (2 * self.pair_x) + side) * (2 * self.rows) + t

    def target(self, hi, xu, zb, yb):
        return ((hi * self.pair_x + xu) * self.zbs + zb) * 2 + yb

    def lanes(self, cell):
        return slice(cell * self.cell_rows, (cell + 1) * self.cell_rows)

    def slots(self):
        for hi in range(self.his):
            for xu in range(self.pair_x):
                for zb in range(self.zbs):
                    index = (hi * self.pair_x + xu) * self.zbs + zb
                    yield hi * self.zbs + zb, xu, index

    def all_targets(self):
        for hi in range(self.his):
            for xu in range(self.pair_x):
                for zb in range(self.zbs):
                    for yb in range(2):
                        yield hi * self.zbs + zb, xu, yb, self.target(hi, xu, zb, yb)


CORE, YB, XU, SPOT = 0, 1, 2, 3


def first_kernel(rhs, out, rows, sem):
    copy = pltpu.make_async_copy(rhs.at[0 : rows.shape[0], :], rows, sem)
    copy.start()
    copy.wait()
    rounded = rows[...].astype(BF16)
    for n in range(out.shape[0]):
        out[n] = rounded


def expand_kernel(count, aboves, slots, begins, at, lists, *refs):
    blocks, outs = refs[:count], refs[count:]
    width = outs[0].shape[-1]
    step = min(512, width)
    for n, (info, out) in enumerate(zip(aboves, outs)):
        listed = info.position(lists[pl.ds(at[slots[n]], 1), :])
        if begins is None:
            block = jnp.concatenate([b[...] for b in blocks], 0)
        else:
            block = blocks[0][begins[n] : begins[n] + out.shape[0], :]
        for begin in range(0, width, step):
            ids = begin + lax.broadcasted_iota(jnp.int32, (step, listed.shape[-1]), 0)
            chosen = jnp.where(ids == listed, 1.0, 0.0).astype(BF16)
            out[:, begin : begin + step] = mm_nt(block, chosen).astype(BF16)


def subtree_kernel(infos, starts, at, full, inverse, rhs, *refs):
    depth = len(infos)
    sources = refs[:depth]
    outs = refs[depth : depth + 2 + 2 * depth]
    total, matrix, dense, rhs_copy, sems = refs[depth + 2 + 2 * depth :]
    loads = Loads(sems)
    rhs_load = loads.start([(rhs, rhs_copy)])
    groups = group_rows(matrix.shape[0])
    first = [start() for start in loads.groups([inverse], matrix, GROUPS)]
    later = [
        [start() for start in loads.groups([sources[n]], dense.at[n], GROUPS)]
        for n in range(depth)
    ]
    core = at[CORE]
    width = total.shape[-1]
    placed = []
    wait(rhs_load)
    for n, info in enumerate(infos):
        row_ids = at[SPOT + n] + lax.broadcasted_iota(jnp.int32, (info.rows, width), 0)
        lane_ids = lax.broadcasted_iota(jnp.int32, (info.rows, width), 1)
        spots = jnp.where(row_ids == lane_ids, 1.0, 0.0).astype(BF16)
        own = rhs_copy[starts[n] : starts[n] + info.rows, :].astype(BF16)
        placed.append(accumulate(None, own, spots))
    rounded = []
    for g, rows in enumerate(groups):
        wait(first[g])
        y = mm(matrix[rows, :], full[...])
        cut = y.shape[1] // 2
        low = at[YB] == 0
        outs[0][rows, :] = jnp.where(low, y[:, :cut], y[:, cut:])
        outs[1][rows, :] = jnp.where(low, y[:, cut:], y[:, :cut])
        rounded.append(y.astype(BF16))
    half = width // 2
    for n, info in enumerate(infos):
        term = None
        for g, rows in enumerate(groups):
            wait(later[n][g])
            term = accumulate(term, rounded[g], dense[n, rows, :])
        total[:, :half] = placed[n][0] - term[0]
        total[:, half:] = placed[n][1] - term[1]
        mine, other = outs[2 + 2 * n], outs[3 + 2 * n]
        for cell, xu, yb, target in info.all_targets():
            for side, ref in ((core, mine), (1 - core, other)):
                row = ((yb * 2 + side) * info.pair_x + xu) * info.chunk
                row = pl.multiple_of(row, info.chunk)
                value = total[pl.ds(row, info.chunk), info.lanes(cell)]
                ref[target] = value.astype(ref.dtype)


def sum_spread_kernel(parts, out):
    total = parts[0].astype(F32)
    for n in range(1, parts.shape[0]):
        total = total + parts[n].astype(F32)
    rounded = total.astype(BF16)
    for n in range(out.shape[0]):
        out[n] = rounded


def sum_parts_kernel(*refs):
    parts, out = refs[:-1], refs[-1]
    total = parts[0][...].astype(F32)
    for part in parts[1:]:
        total = total + part[...].astype(F32)
    rounded = total.astype(BF16)
    for n in range(out.shape[0]):
        out[n] = rounded


def natural_rows(info, gathered):
    blocks = [
        gathered[cell][:, inside : inside + size]
        for _, cell, inside, size in info.natural()
    ]
    return jnp.concatenate(blocks, 1)


def put_spread(info, halves, stage, own_cell, outs):
    value = jnp.concatenate(halves, 1).astype(BF16)
    for lane, cell, inside, size in info.natural():
        stage[cell, :, inside : inside + size] = value[:, lane : lane + size]
    for d, out in enumerate(outs):
        out[...] = stage[own_cell ^ d]


def forward_kernel(infos, k, at, gathered, mine_hbm, received_hbm, *refs):
    info, above = infos[k - 1], infos[k]
    count = 4 * info.pair_x
    pieces = refs[:count]
    lower_y = refs[count : count + k - 1]
    sources = refs[count + k - 1 : count + 2 * k - 1]
    y_ref, out, total, matrix, mine, received, sems = refs[count + 2 * k - 1 : count + 2 * k + 6]
    dense = refs[count + 2 * k + 6 : count + 3 * k + 6]
    lower_copies = refs[count + 3 * k + 6 :]
    loads = Loads(sems)
    groups = group_rows(matrix.shape[0])
    first = [start() for start in loads.groups(pieces, matrix, GROUPS)]
    later = [
        [start() for start in loads.groups([source], dense[j], GROUPS)]
        for j, source in enumerate(sources)
    ]
    base = loads.start([(mine_hbm, mine), (received_hbm, received)])
    base += loads.start(list(zip(lower_y, lower_copies)))
    lower_y = lower_copies
    vector = natural_rows(info, gathered)
    ys = []
    for g, rows in enumerate(groups):
        wait(first[g])
        y = mm_nt(matrix[rows, :], vector)
        y_ref[rows, :] = y
        ys.append(y)
    wait(base)
    same = {}
    for j in range(1, k + 1):
        term = None
        for g, rows in enumerate(group_rows(dense[j - 1].shape[0])):
            value = ys[g] if j == k else lower_y[j - 1][rows, :]
            wait(later[j - 1][g])
            term = accumulate(term, value.astype(BF16), dense[j - 1][rows, :])
        term = jnp.concatenate(term, 1)
        same.setdefault(infos[j - 1].pair_x == above.pair_x, []).append(term)
    if False in same:
        total[...] = functools.reduce(jnp.add, same[False])
    else:
        total[...] = jnp.zeros(total.shape, F32)
    if True in same:
        term = functools.reduce(jnp.add, same[True])
        rows = pl.ds(pl.multiple_of(at[XU] * above.chunk, above.chunk), above.chunk)
        total[rows, :] = total[rows, :] + term
    for cell, xu, index in above.slots():
        value = mine[index].astype(F32) + received[index].astype(F32)
        minus = total[xu * above.chunk : (xu + 1) * above.chunk, above.lanes(cell)]
        out[index] = (value - minus).astype(BF16)


def top_kernel(info, at, gathered, *refs):
    pieces = refs[: 4 * info.pair_x]
    outs, stage = refs[4 * info.pair_x : -1], refs[-1]
    each = len(pieces) // GROUPS
    vector = natural_rows(info, gathered)
    halves = None
    for g in range(GROUPS):
        matrix = jnp.concatenate([p[...] for p in pieces[g * each : (g + 1) * each]], 0)
        y = mm_nt(matrix, vector)
        halves = accumulate(halves, y.astype(BF16), matrix)
    put_spread(info, halves, stage, at[info.cell_slot], outs)


def backward_kernel(infos, k, at, y_hbm, *refs):
    info = infos[k - 1]
    count = 4 * info.pair_x
    uppers = infos[k:]
    many = len(uppers)
    pieces = refs[:count]
    solved = refs[count : count + many]
    sources = refs[count + many : count + 2 * many]
    begin = count + 2 * many
    outs = refs[begin : begin + info.cells]
    stage, matrix, y, sems = refs[begin + info.cells : begin + info.cells + 4]
    dense = refs[begin + info.cells + 4 :]
    loads = Loads(sems)
    y_load = loads.start([(y_hbm, y)])
    dense_loads = [loads.groups([source], dense[n], GROUPS) for n, source in enumerate(sources)]
    matrix_loads = loads.groups(pieces, matrix, GROUPS)
    first = []
    last = []
    for g in range(GROUPS):
        first.append([start[g]() for start in dense_loads])
        last.append(matrix_loads[g]())
    vectors = []
    for n, above in enumerate(uppers):
        parts = []
        for hi in range(above.his):
            for zb in range(above.zbs):
                first_slot = hi * above.pair_x * above.zbs + zb
                if above.pair_x == info.pair_x:
                    parts.append(solved[n][first_slot + at[XU] * above.zbs])
                else:
                    slots = [first_slot + xu * above.zbs for xu in range(above.pair_x)]
                    parts.append(jnp.concatenate([solved[n][slot] for slot in slots], 0))
        vectors.append(jnp.concatenate(parts, 1))
    wait(y_load)
    halves = None
    for g, rows in enumerate(group_rows(matrix.shape[0])):
        z = y[rows, :]
        for n in range(many):
            wait(first[g][n])
            z = z - mm_nt(dense[n][rows, :], vectors[n])
        wait(last[g])
        halves = accumulate(halves, z.astype(BF16), matrix[rows, :])
    put_spread(info, halves, stage, at[info.cell_slot], outs)


def full_cases(info, core, mine, other, full):
    for cell, xu, index in info.slots():
        for side, ref in ((core, mine), (1 - core, other)):
            row = pl.multiple_of((side * info.pair_x + xu) * info.chunk, info.chunk)
            full[pl.ds(row, info.chunk), info.lanes(cell)] = ref[index]


def subtract_kernel(info, count, at, own, near, mine, other, *refs):
    y_parts = refs[:count]
    out, full, dense, y, sems = refs[count:]
    loads = Loads(sems)
    y_load = loads.rows(y_parts, y)
    copies = [start() for start in loads.groups([own, near], dense, GROUPS)]
    full_cases(info, at[CORE], mine, other, full)
    wait(y_load)
    for g, rows in enumerate(group_rows(dense.shape[0])):
        wait(copies[g])
        out[rows, :] = y[rows, :] - mm_nt(dense[rows, :], full[...])


def last_kernel(info, at, own, near, mine, other, inverse, inverse_near, y_hbm, *refs):
    out, full, dense, matrix, y, sems = refs
    loads = Loads(sems)
    y_load = loads.start([(y_hbm, y)])
    dense_loads = loads.groups([own, near], dense, GROUPS)
    inverse_own = inverse.at[0 : inverse_near.shape[0], :]
    matrix_loads = loads.groups([inverse_own, inverse_near], matrix, GROUPS)
    copies = [(dense_loads[g](), matrix_loads[g]()) for g in range(GROUPS)]
    full_cases(info, at[CORE], mine, other, full)
    wait(y_load)
    halves = None
    for g, rows in enumerate(group_rows(dense.shape[0])):
        wait(copies[g][0])
        z = y[rows, :] - mm_nt(dense[rows, :], full[...])
        wait(copies[g][1])
        halves = accumulate(halves, z.astype(BF16), matrix[rows, :])
    value = jnp.concatenate(halves, 1).astype(BF16)
    size = out.shape[-1]
    for n in range(out.shape[0]):
        out[n] = value[:, n * size : (n + 1) * size]


def output_kernel(parts, *refs):
    rows, out = refs[:-1], refs[-1]
    totals = [parts[0].astype(F32), parts[1].astype(F32)]
    for n in range(2, parts.shape[0]):
        totals[n % 2] = totals[n % 2] + parts[n].astype(F32)
    begin = totals[0].shape[1]
    out[0:begin, :] = jnp.concatenate(totals, 0).T
    for row in rows:
        out[begin : begin + row.shape[0], :] = row[...].astype(F32)
        begin += row.shape[0]


def solve(right_side, inverse_blocks, coupling, update_rows):
    leaves = lax.axis_size("leaf")
    blocks = lax.axis_size("blk")
    depth = leaves.bit_length() - 1
    leaf_id = lax.axis_index("leaf")
    blk_id = lax.axis_index("blk")
    core = leaf_id & 1
    yb = blk_id & 1
    zb = blk_id >> 1
    width = inverse_blocks.shape[-1]
    cases = right_side.shape[-1]
    rhs = right_side[0, 0]
    inverse = inverse_blocks[0, 0]
    couple = coupling[0, 0]
    listed_rows = coupling.shape[-1]
    counts = [width // (blocks << level) for level in range(depth + 1)]
    starts = [sum(counts[:level]) for level in range(depth + 1)]
    infos = [Level(l, leaves, blocks, width, cases) for l in range(1, depth + 1)]
    couple_starts = {}
    cursor = 0
    for level in range(depth):
        for above in range(level + 1, depth + 1):
            couple_starts[level, above] = cursor
            cursor += counts[level]
    pair_bases = []
    cursor = 0
    for level in range(depth + 1):
        pair_bases.append(cursor)
        cursor += (leaves >> level) * (depth - level)

    pair_slot = {}
    for level in range(depth):
        for above in range(level + 1, depth + 1):
            pair_slot[level, above] = SPOT + depth + len(pair_slot)

    def at():
        leaf = lax.axis_index("leaf")
        blk = lax.axis_index("blk")
        scalars = [leaf & 1, blk & 1, (leaf >> 1) & 1]
        own_cells = []
        for info in infos:
            member = leaf & ((1 << info.level) - 1)
            hi, side = split_power(member, 2 * info.pair_x)
            cell = hi * info.zbs + (blk >> 1)
            own_cells.append(cell)
            scalars.append(((cell * 2 * info.pair_x + side) * 2 + (blk & 1)) * info.rows)
        for level, above in pair_slot:
            node = leaf >> level
            scalars.append(pair_bases[level] + node * (depth - level) + (above - level - 1))
        return scalars + own_cells

    for n, info in enumerate(infos):
        info.cell_slot = SPOT + depth + len(pair_slot) + n

    def swap(value, axis, bit):
        size = leaves if axis == "leaf" else blocks
        return lax.ppermute(value, axis, [(i, i ^ bit) for i in range(size)])

    def cell_columns(rows, level):
        info = infos[level - 1]
        parts = rows.reshape(-1, info.his, 2 * info.pair_x, info.zbs, 2 * info.rows)
        return parts.transpose(0, 1, 3, 2, 4).reshape(-1, width)

    def exchange_outer(value, level):
        if level <= 1:
            return lax.all_to_all(value, "blk", 0, 0, tiled=True)
        return lax.all_to_all(
            value,
            ("leaf", "blk"),
            0,
            0,
            axis_index_groups=infos[level - 1].outer,
            tiled=True,
        )

    def exchange_middle(value, level):
        info = infos[level - 1]
        if level <= 1:
            return lax.all_to_all(
                value, "blk", 0, 0, axis_index_groups=info.inner_blk, tiled=True
            )
        return lax.all_to_all(
            value, ("leaf", "blk"), 0, 0, axis_index_groups=info.middle, tiled=True
        )

    def exchange_inner(value, level):
        info = infos[level - 1]
        if info.his == 1:
            return lax.all_to_all(
                value, "blk", 0, 0, axis_index_groups=info.inner_blk, tiled=True
            )
        return lax.all_to_all(
            value, ("leaf", "blk"), 0, 0, axis_index_groups=info.inner, tiled=True
        )

    def swap_inner(value, level, d):
        info = infos[level - 1]
        groups = info.inner_blk if info.his == 1 else info.inner
        axes = "blk" if info.his == 1 else ("leaf", "blk")
        pairs = [(device, group[i ^ d]) for group in groups for i, device in enumerate(group)]
        return lax.ppermute(value, axes, pairs)

    def coupling_block(level, above):
        begin = couple_starts[level, above]
        return couple[begin : begin + counts[level]]

    uppers = range(1, depth + 1)
    dense = {}
    expanded = kernel_call(
        functools.partial(
            expand_kernel,
            1,
            infos,
            [pair_slot[0, above] for above in uppers],
            [couple_starts[0, above] for above in uppers],
        ),
        [shaped((counts[0], width), BF16)] * depth,
        [update_rows, couple],
        scalars=at,
        flops=2 * depth * counts[0] * listed_rows * width,
    )
    for above in uppers:
        dense[0, above] = expanded[above - 1]

    spread = kernel_call(
        first_kernel,
        [shaped((blocks, counts[0], cases), BF16)],
        [(rhs, None)],
        scratch=[pltpu.VMEM((counts[0], cases), F32), pltpu.SemaphoreType.DMA],
    )[0]
    full = lax.all_to_all(spread, "blk", 0, 0, tiled=True).reshape(width, cases)
    outs = [shaped((counts[0], cases // 2), F32)] * 2
    for info in infos:
        shape = (info.targets, info.chunk, info.cell_rows)
        outs += [shaped(shape, BF16), shaped(shape, BF16)]
    matrix_scratch = pltpu.VMEM((counts[0], width), BF16)
    y_keep, y_send, *base = kernel_call(
        functools.partial(subtree_kernel, infos, starts[1:]),
        outs,
        [full, (inverse, None), (rhs, None)] + hbm([dense[0, above] for above in uppers]),
        scalars=at,
        scratch=[
            pltpu.VMEM((cases, width), F32),
            matrix_scratch,
            pltpu.VMEM((depth, counts[0], width), BF16),
            pltpu.VMEM(rhs.shape, F32),
            pltpu.SemaphoreType.DMA((1 + GROUPS * (1 + depth),)),
        ],
        flops=2 * (1 + depth) * counts[0] * width * cases,
        stay=[True, True, False, False] + [True, True] * (depth - 1),
    )
    received = []
    for level in uppers:
        received.append(swap(base[2 * level - 1], "leaf", 1))
    paired = {}
    for level in range(2, depth + 1):
        info = infos[level - 1]
        both = base[2 * level - 2].astype(F32) + received[level - 1].astype(F32)
        both = both.astype(BF16).reshape(-1, 2, info.chunk, info.cell_rows)
        keep = lax.dynamic_index_in_dim(both, yb, 1, keepdims=False)
        send = lax.dynamic_index_in_dim(both, 1 - yb, 1, keepdims=False)
        paired[level] = keep, swap(send, "blk", 1)

    def pieces_of(value, level):
        pieces = [value]
        if infos[level - 1].pair_x == 2:
            pieces += [swap(piece, "leaf", 2) for piece in pieces]
        pieces += [swap(piece, "blk", 1) for piece in pieces]
        pieces += [swap(piece, "leaf", 1) for piece in pieces]
        return pieces

    inverse_pieces = {}
    for level in uppers:
        rows = inverse[starts[level] : starts[level] + counts[level]]
        if not infos[level - 1].direct:
            rows = cell_columns(rows, level)
        inverse_pieces[level] = pieces_of(rows, level)
        for above in range(level + 1, depth + 1):
            pieces = pieces_of(coupling_block(level, above), level)
            rows = len(pieces) * counts[level]
            dense[level, above] = kernel_call(
                functools.partial(
                    expand_kernel,
                    len(pieces),
                    [infos[above - 1]],
                    [pair_slot[level, above]],
                    None,
                ),
                [shaped((rows, width), BF16)],
                [update_rows] + pieces,
                scalars=at,
                flops=2 * rows * listed_rows * width,
            )[0]

    y_near = swap(y_send, "blk", 1)
    dense_near = {}
    for above in range(depth, 0, -1):
        block = swap(coupling_block(0, above), "blk", 1)
        dense_near[above] = kernel_call(
            functools.partial(
                expand_kernel, 1, [infos[above - 1]], [pair_slot[0, above]], None
            ),
            [shaped((counts[0], width), BF16)],
            [update_rows, block],
            scalars=at,
            flops=2 * counts[0] * listed_rows * width,
        )[0]
    inverse_near = swap(inverse[: counts[0]], "blk", 1)

    def sum_spread(parts, copies):
        return kernel_call(
            sum_spread_kernel, [shaped((copies,) + parts.shape[1:], BF16)], [parts]
        )[0]

    def sum_parts(parts, copies):
        return kernel_call(
            sum_parts_kernel, [shaped((copies,) + parts[0].shape, BF16)], parts
        )[0]

    def stage_scratch(info):
        return pltpu.VMEM((info.cells, info.chunk, info.cell_rows), BF16)

    def cell_scratch(info):
        return pltpu.VMEM((info.cell_rows, width), BF16)

    ys = {}
    parts = (base[0].astype(F32) + received[0].astype(F32)).astype(BF16)
    for level in uppers:
        info = infos[level - 1]
        parts = (exchange_outer if level == 1 else exchange_middle)(parts, level)
        gathered = exchange_inner(sum_spread(parts, info.cells), level)
        size = info.cell_rows * width * info.chunk
        count = 4 * info.pair_x
        if level == depth:
            parts = kernel_call(
                functools.partial(top_kernel, info),
                [shaped((info.chunk, info.cell_rows), BF16)] * info.cells,
                [gathered] + [(piece, True) for piece in inverse_pieces[level]],
                scalars=at,
                scratch=[stage_scratch(info)],
                flops=4 * size,
                stay=[False] * info.cells,
            )
            break
        above = infos[level]
        ys[level], parts = kernel_call(
            functools.partial(forward_kernel, infos, level),
            [
                shaped((info.cell_rows, info.chunk), F32),
                shaped((above.targets // 2, above.chunk, above.cell_rows), BF16),
            ],
            [gathered]
            + hbm(
                list(paired[level + 1])
                + inverse_pieces[level]
                + [ys[j] for j in range(1, level)]
                + [dense[j, level + 1] for j in range(1, level + 1)]
            ),
            scalars=at,
            scratch=[
                pltpu.VMEM((above.chunk * above.pair_x, width), F32),
                cell_scratch(info),
                pltpu.VMEM((above.targets // 2, above.chunk, above.cell_rows), BF16),
                pltpu.VMEM((above.targets // 2, above.chunk, above.cell_rows), BF16),
                pltpu.SemaphoreType.DMA((count + GROUPS * level + 1 + level,)),
            ]
            + [cell_scratch(infos[j - 1]) for j in range(1, level + 1)]
            + [pltpu.VMEM(ys[j].shape, F32) for j in range(1, level)],
            flops=4 * size,
        )

    solved = {}
    swapped = {}
    pair_scratch = pltpu.VMEM((2 * counts[0], width), BF16)
    half_cases = cases // 2
    low = [y_keep, y_near]
    for level in range(depth, 0, -1):
        info = infos[level - 1]
        if level < depth:
            higher = range(level + 1, depth + 1)
            count = 4 * info.pair_x
            parts = kernel_call(
                functools.partial(backward_kernel, infos, level),
                [shaped((info.chunk, info.cell_rows), BF16)] * info.cells,
                hbm([ys[level]] + inverse_pieces[level])
                + [solved[above] for above in higher]
                + hbm([dense[level, above] for above in higher]),
                scalars=at,
                scratch=[
                    stage_scratch(info),
                    cell_scratch(info),
                    pltpu.VMEM(ys[level].shape, F32),
                    pltpu.SemaphoreType.DMA((1 + count + GROUPS * len(higher),)),
                ]
                + [cell_scratch(info)] * len(higher),
                flops=4 * info.cell_rows * width * info.chunk,
                stay=[False] * info.cells,
            )
        parts = [parts[0]] + [
            swap_inner(parts[d], level, d) for d in range(1, info.cells)
        ]
        solved[level] = exchange_middle(sum_parts(parts, info.cells * info.pair_x), level)
        swapped[level] = swap(solved[level], "leaf", 1)
        if level > 1:
            low = kernel_call(
                functools.partial(subtract_kernel, info, len(low)),
                [shaped((2 * counts[0], half_cases), F32)],
                hbm([dense[0, level], dense_near[level]])
                + [solved[level], swapped[level]]
                + [(low[0], None)]
                + [(value, False) for value in low[1:]],
                scalars=at,
                scratch=[
                    pltpu.VMEM((half_cases, width), BF16),
                    pair_scratch,
                    pltpu.VMEM((2 * counts[0], half_cases), F32),
                    pltpu.SemaphoreType.DMA((2 + GROUPS,)),
                ],
                flops=2 * counts[0] * width * cases,
            )

    part = kernel_call(
        functools.partial(last_kernel, infos[0]),
        [shaped((blocks, half_cases, counts[0]), BF16)],
        hbm([dense[0, 1], dense_near[1]])
        + [solved[1], swapped[1]]
        + [(inverse, None), (inverse_near, False), (low[0], None)],
        scalars=at,
        scratch=[
            pltpu.VMEM((half_cases, width), BF16),
            pair_scratch,
            pair_scratch,
            pltpu.VMEM((2 * counts[0], half_cases), F32),
            pltpu.SemaphoreType.DMA((1 + 2 * GROUPS,)),
        ],
        flops=4 * counts[0] * width * cases,
    )[0]
    parts = lax.all_to_all(part, "blk", 0, 0, tiled=True)

    keeps = []
    sends = []
    for level in uppers:
        info = infos[level - 1]
        member = leaf_id & ((1 << level) - 1)
        side = member & (2 * info.pair_x - 1)
        hi = member // (2 * info.pair_x)

        def own(value):
            shape = (info.his, info.pair_x, info.zbs, info.chunk, info.cell_rows)
            sizes = (1, info.pair_x, 1, info.chunk, 2 * info.rows)
            start = (hi, 0, zb, 0, side * 2 * info.rows)
            taken = lax.dynamic_slice(value.reshape(shape), start, sizes)
            return taken.reshape(half_cases // 2, 2 * info.rows)

        mine, other = own(solved[level]), own(swapped[level])
        both = jnp.where(
            core == 0, jnp.concatenate([mine, other], 0), jnp.concatenate([other, mine], 0)
        )
        keeps.append(jnp.where(yb == 0, both[:, : info.rows], both[:, info.rows :]))
        sends.append(jnp.where(yb == 0, both[:, info.rows :], both[:, : info.rows]))
    keep = jnp.concatenate(keeps, 1)
    near = swap(jnp.concatenate(sends, 1), "blk", 1)
    rows = jnp.where(
        yb == 0, jnp.concatenate([keep, near], 0), jnp.concatenate([near, keep], 0)
    )
    outputs = [rows.T]
    out = kernel_call(
        output_kernel, [shaped((sum(counts), cases), F32)], [parts] + outputs
    )[0]
    return out[None, None]


def solution(mesh):
    spec = P("leaf", "blk", None, None)
    return jax.shard_map(
        solve, mesh=mesh, in_specs=(spec, spec, spec, P()), out_specs=spec, check_vma=False
    )
```

```python
import functools

import jax
import jax.numpy as jnp
from jax import lax
from jax.experimental import pallas as pl
from jax.experimental.pallas import tpu as pltpu
from jax.sharding import PartitionSpec as P


BF16 = jnp.bfloat16
F32 = jnp.float32


def mm(a, b):
    return jnp.dot(a, b, preferred_element_type=F32)


def mm_tn(a, b):
    return lax.dot_general(a, b, (((0,), (0,)), ((), ())), preferred_element_type=F32)


def mm_nt(a, b):
    return lax.dot_general(a, b, (((1,), (1,)), ((), ())), preferred_element_type=F32)


def shaped(shape, dtype):
    return jax.ShapeDtypeStruct(tuple(shape), dtype)


def kernel_call(body, outs, args, scalars=None, scratch=(), flops=0, stay=None):
    stay = [True] * len(outs) if stay is None else stay
    values = []
    specs = []
    moved = sum(o.size * o.dtype.itemsize for o in outs)
    for arg in args:
        value, spec = arg, pl.BlockSpec(memory_space=pltpu.VMEM)
        if isinstance(arg, tuple):
            value = pltpu.with_memory_space_constraint(arg[0], pltpu.HBM)
            if arg[1] is None:
                spec = pl.BlockSpec(memory_space=pltpu.HBM)
            elif arg[1] is False:
                value, spec = arg[0], pl.BlockSpec(memory_space=pl.ANY)
        values.append(value)
        specs.append(spec)
        moved += value.size * value.dtype.itemsize
    return pl.pallas_call(
        body if scalars is None else lambda *refs: body(scalars(), *refs),
        out_shape=[
            pltpu.HBM(o.shape, o.dtype) if keep else o for o, keep in zip(outs, stay)
        ],
        in_specs=specs,
        out_specs=[pl.BlockSpec(memory_space=pltpu.VMEM)] * len(outs),
        scratch_shapes=list(scratch),
        compiler_params=pltpu.CompilerParams(vmem_limit_bytes=16 << 20),
        cost_estimate=pl.CostEstimate(flops=flops, bytes_accessed=moved, transcendentals=0),
    )(*values)


def hbm(values):
    return [(value, None) for value in values]


class Loads:
    def __init__(self, sems):
        self.sems = sems
        self.used = 0

    def start(self, pairs):
        copies = []
        for source, target in pairs:
            copies.append(pltpu.make_async_copy(source, target, self.sems.at[self.used]))
            copies[-1].start()
            self.used += 1
        return copies

    def rows(self, sources, target):
        pairs = []
        begin = 0
        for source in sources:
            count = source.shape[0]
            pairs.append((source, target.at[begin : begin + count, :]))
            begin += count
        return self.start(pairs)

    def groups(self, sources, target, order):
        rows = target.shape[0] // order
        if len(sources) == 1:
            source = sources[0]
            return [
                lambda g=g: self.start(
                    [(source.at[g * rows : (g + 1) * rows, :], target.at[g * rows : (g + 1) * rows, :])]
                )
                for g in range(order)
            ]
        each = len(sources) // order
        return [
            lambda g=g: self.rows(
                sources[g * each : (g + 1) * each], target.at[g * rows : (g + 1) * rows, :]
            )
            for g in range(order)
        ]


GROUPS = 2


def group_rows(total):
    size = total // GROUPS
    return [slice(g * size, (g + 1) * size) for g in range(GROUPS)]


def accumulate(total, left, right):
    half = right.shape[1] // 2
    terms = [mm_tn(left, right[:, :half]), mm_tn(left, right[:, half:])]
    return terms if total is None else [t + term for t, term in zip(total, terms)]


def wait(copies):
    for copy in copies:
        copy.wait()


def split_power(value, size):
    bits = size.bit_length() - 1
    if size == 1 << bits:
        return value >> bits, value & (size - 1)
    return value // size, value % size


class Level:
    def __init__(self, level, leaves, blocks, width, cases):
        self.level = level
        self.pair_x = 2 if level >= 2 else 1
        self.his = (1 << level) // (2 * self.pair_x)
        self.zbs = blocks // 2
        self.rows = width // (blocks << level)
        self.cells = self.his * self.zbs
        self.cell_rows = width // self.cells
        self.chunk = cases // (4 * self.pair_x)
        self.targets = self.cells * self.pair_x * 2
        outer = []
        inner = []
        middle = []
        for node in range(leaves >> level):
            base = node << level
            for side in range(2):
                outer.append(
                    [
                        (base + 2 * upper + side) * blocks + b
                        for upper in range(1 << (level - 1))
                        for b in range(blocks)
                    ]
                )
                for yb in range(2):
                    middle.append(
                        [
                            (base + 2 * upper + side) * blocks + 2 * zb + yb
                            for upper in range(1 << (level - 1))
                            for zb in range(self.zbs)
                        ]
                    )
                for xu in range(self.pair_x):
                    for yb in range(2):
                        inner.append(
                            [
                                (base + (hi * self.pair_x + xu) * 2 + side) * blocks + 2 * zb + yb
                                for hi in range(self.his)
                                for zb in range(self.zbs)
                            ]
                        )
        self.outer = outer
        self.inner = inner
        self.middle = middle
        self.inner_blk = [[2 * zb + yb for zb in range(self.zbs)] for yb in range(2)]

    @property
    def direct(self):
        return (2 * self.rows) % 128 == 0

    def natural(self):
        if not self.direct:
            return [(c * self.cell_rows, c, 0, self.cell_rows) for c in range(self.cells)]
        size = 2 * self.rows
        return [
            (
                ((hi * 2 * self.pair_x + side) * self.zbs + zb) * size,
                hi * self.zbs + zb,
                side * size,
                size,
            )
            for hi in range(self.his)
            for side in range(2 * self.pair_x)
            for zb in range(self.zbs)
        ]

    def position(self, rows):
        block, t = split_power(rows, 2 * self.rows)
        block, zpos = split_power(block, self.zbs)
        hi, side = split_power(block, 2 * self.pair_x)
        cell = hi * self.zbs + zpos
        return (cell * (2 * self.pair_x) + side) * (2 * self.rows) + t

    def target(self, hi, xu, zb, yb):
        return ((hi * self.pair_x + xu) * self.zbs + zb) * 2 + yb

    def lanes(self, cell):
        return slice(cell * self.cell_rows, (cell + 1) * self.cell_rows)

    def slots(self):
        for hi in range(self.his):
            for xu in range(self.pair_x):
                for zb in range(self.zbs):
                    index = (hi * self.pair_x + xu) * self.zbs + zb
                    yield hi * self.zbs + zb, xu, index

    def all_targets(self):
        for hi in range(self.his):
            for xu in range(self.pair_x):
                for zb in range(self.zbs):
                    for yb in range(2):
                        yield hi * self.zbs + zb, xu, yb, self.target(hi, xu, zb, yb)


CORE, YB, XU, SPOT = 0, 1, 2, 3


def first_kernel(rhs, out, rows, sem):
    copy = pltpu.make_async_copy(rhs.at[0 : rows.shape[0], :], rows, sem)
    copy.start()
    copy.wait()
    rounded = rows[...].astype(BF16)
    for n in range(out.shape[0]):
        out[n] = rounded


def expand_kernel(count, aboves, slots, begins, at, lists, *refs):
    blocks, outs = refs[:count], refs[count:]
    width = outs[0].shape[-1]
    step = min(512, width)
    for n, (info, out) in enumerate(zip(aboves, outs)):
        listed = info.position(lists[pl.ds(at[slots[n]], 1), :])
        if begins is None:
            block = jnp.concatenate([b[...] for b in blocks], 0)
        else:
            block = blocks[0][begins[n] : begins[n] + out.shape[0], :]
        for begin in range(0, width, step):
            ids = begin + lax.broadcasted_iota(jnp.int32, (step, listed.shape[-1]), 0)
            chosen = jnp.where(ids == listed, 1.0, 0.0).astype(BF16)
            out[:, begin : begin + step] = mm_nt(block, chosen).astype(BF16)


def subtree_kernel(infos, starts, at, full, inverse, rhs, *refs):
    depth = len(infos)
    sources = refs[:depth]
    outs = refs[depth : depth + 2 + 2 * depth]
    total, matrix, dense, rhs_copy, sems = refs[depth + 2 + 2 * depth :]
    loads = Loads(sems)
    rhs_load = loads.start([(rhs, rhs_copy)])
    groups = group_rows(matrix.shape[0])
    first = [start() for start in loads.groups([inverse], matrix, GROUPS)]
    later = [
        [start() for start in loads.groups([sources[n]], dense.at[n], GROUPS)]
        for n in range(depth)
    ]
    core = at[CORE]
    width = total.shape[-1]
    placed = []
    wait(rhs_load)
    for n, info in enumerate(infos):
        row_ids = at[SPOT + n] + lax.broadcasted_iota(jnp.int32, (info.rows, width), 0)
        lane_ids = lax.broadcasted_iota(jnp.int32, (info.rows, width), 1)
        spots = jnp.where(row_ids == lane_ids, 1.0, 0.0).astype(BF16)
        own = rhs_copy[starts[n] : starts[n] + info.rows, :].astype(BF16)
        placed.append(accumulate(None, own, spots))
    rounded = []
    for g, rows in enumerate(groups):
        wait(first[g])
        y = mm(matrix[rows, :], full[...])
        cut = y.shape[1] // 2
        low = at[YB] == 0
        outs[0][rows, :] = jnp.where(low, y[:, :cut], y[:, cut:])
        outs[1][rows, :] = jnp.where(low, y[:, cut:], y[:, :cut])
        rounded.append(y.astype(BF16))
    half = width // 2
    for n, info in enumerate(infos):
        term = None
        for g, rows in enumerate(groups):
            wait(later[n][g])
            term = accumulate(term, rounded[g], dense[n, rows, :])
        total[:, :half] = placed[n][0] - term[0]
        total[:, half:] = placed[n][1] - term[1]
        mine, other = outs[2 + 2 * n], outs[3 + 2 * n]
        for cell, xu, yb, target in info.all_targets():
            for side, ref in ((core, mine), (1 - core, other)):
                row = ((yb * 2 + side) * info.pair_x + xu) * info.chunk
                row = pl.multiple_of(row, info.chunk)
                value = total[pl.ds(row, info.chunk), info.lanes(cell)]
                ref[target] = value.astype(ref.dtype)


def sum_spread_kernel(parts, out):
    total = parts[0].astype(F32)
    for n in range(1, parts.shape[0]):
        total = total + parts[n].astype(F32)
    rounded = total.astype(BF16)
    for n in range(out.shape[0]):
        out[n] = rounded


def sum_parts_kernel(*refs):
    parts, out = refs[:-1], refs[-1]
    total = parts[0][...].astype(F32)
    for part in parts[1:]:
        total = total + part[...].astype(F32)
    rounded = total.astype(BF16)
    for n in range(out.shape[0]):
        out[n] = rounded


def natural_rows(info, gathered):
    blocks = [
        gathered[cell][:, inside : inside + size]
        for _, cell, inside, size in info.natural()
    ]
    return jnp.concatenate(blocks, 1)


def put_spread(info, halves, stage, own_cell, outs):
    value = jnp.concatenate(halves, 1).astype(BF16)
    for lane, cell, inside, size in info.natural():
        stage[cell, :, inside : inside + size] = value[:, lane : lane + size]
    for d, out in enumerate(outs):
        out[...] = stage[own_cell ^ d]


def forward_kernel(infos, k, at, *refs):
    info, above = infos[k - 1], infos[k]
    near = refs[: info.cells]
    mine_hbm, received_hbm = refs[info.cells : info.cells + 2]
    gathered, refs = refs[-1], refs[info.cells + 2 : -1]
    count = 4 * info.pair_x
    pieces = refs[:count]
    lower_y = refs[count : count + k - 1]
    sources = refs[count + k - 1 : count + 2 * k - 1]
    y_ref, out, total, matrix, mine, received, sems = refs[count + 2 * k - 1 : count + 2 * k + 6]
    dense = refs[count + 2 * k + 6 : count + 3 * k + 6]
    lower_copies = refs[count + 3 * k + 6 :]
    loads = Loads(sems)
    groups = group_rows(matrix.shape[0])
    first = [start() for start in loads.groups(pieces, matrix, GROUPS)]
    later = [
        [start() for start in loads.groups([source], dense[j], GROUPS)]
        for j, source in enumerate(sources)
    ]
    base = loads.start([(mine_hbm, mine), (received_hbm, received)])
    base += loads.start(list(zip(lower_y, lower_copies)))
    lower_y = lower_copies
    for d, value in enumerate(near):
        gathered[at[info.cell_slot] ^ d] = value[0]
    vector = natural_rows(info, gathered)
    ys = []
    for g, rows in enumerate(groups):
        wait(first[g])
        y = mm_nt(matrix[rows, :], vector)
        y_ref[rows, :] = y
        ys.append(y)
    wait(base)
    same = {}
    for j in range(1, k + 1):
        term = None
        for g, rows in enumerate(group_rows(dense[j - 1].shape[0])):
            value = ys[g] if j == k else lower_y[j - 1][rows, :]
            wait(later[j - 1][g])
            term = accumulate(term, value.astype(BF16), dense[j - 1][rows, :])
        term = jnp.concatenate(term, 1)
        same.setdefault(infos[j - 1].pair_x == above.pair_x, []).append(term)
    if False in same:
        total[...] = functools.reduce(jnp.add, same[False])
    else:
        total[...] = jnp.zeros(total.shape, F32)
    if True in same:
        term = functools.reduce(jnp.add, same[True])
        rows = pl.ds(pl.multiple_of(at[XU] * above.chunk, above.chunk), above.chunk)
        total[rows, :] = total[rows, :] + term
    for cell, xu, index in above.slots():
        value = mine[index].astype(F32) + received[index].astype(F32)
        minus = total[xu * above.chunk : (xu + 1) * above.chunk, above.lanes(cell)]
        out[index] = (value - minus).astype(BF16)


def top_kernel(info, at, gathered, *refs):
    pieces = refs[: 4 * info.pair_x]
    outs, stage = refs[4 * info.pair_x : -1], refs[-1]
    each = len(pieces) // GROUPS
    vector = natural_rows(info, gathered)
    halves = None
    for g in range(GROUPS):
        matrix = jnp.concatenate([p[...] for p in pieces[g * each : (g + 1) * each]], 0)
        y = mm_nt(matrix, vector)
        halves = accumulate(halves, y.astype(BF16), matrix)
    put_spread(info, halves, stage, at[info.cell_slot], outs)


def backward_kernel(infos, k, at, y_hbm, *refs):
    info = infos[k - 1]
    count = 4 * info.pair_x
    uppers = infos[k:]
    many = len(uppers)
    pieces = refs[:count]
    solved = refs[count : count + many]
    sources = refs[count + many : count + 2 * many]
    begin = count + 2 * many
    outs = refs[begin : begin + info.cells]
    stage, matrix, y, sems = refs[begin + info.cells : begin + info.cells + 4]
    dense = refs[begin + info.cells + 4 :]
    loads = Loads(sems)
    y_load = loads.start([(y_hbm, y)])
    dense_loads = [loads.groups([source], dense[n], GROUPS) for n, source in enumerate(sources)]
    matrix_loads = loads.groups(pieces, matrix, GROUPS)
    first = []
    last = []
    for g in range(GROUPS):
        first.append([start[g]() for start in dense_loads])
        last.append(matrix_loads[g]())
    vectors = []
    for n, above in enumerate(uppers):
        parts = []
        for hi in range(above.his):
            for zb in range(above.zbs):
                first_slot = hi * above.pair_x * above.zbs + zb
                if above.pair_x == info.pair_x:
                    parts.append(solved[n][first_slot + at[XU] * above.zbs])
                else:
                    slots = [first_slot + xu * above.zbs for xu in range(above.pair_x)]
                    parts.append(jnp.concatenate([solved[n][slot] for slot in slots], 0))
        vectors.append(jnp.concatenate(parts, 1))
    wait(y_load)
    halves = None
    for g, rows in enumerate(group_rows(matrix.shape[0])):
        z = y[rows, :]
        for n in range(many):
            wait(first[g][n])
            z = z - mm_nt(dense[n][rows, :], vectors[n])
        wait(last[g])
        halves = accumulate(halves, z.astype(BF16), matrix[rows, :])
    put_spread(info, halves, stage, at[info.cell_slot], outs)


def full_cases(info, core, mine, other, full):
    for cell, xu, index in info.slots():
        for side, ref in ((core, mine), (1 - core, other)):
            row = pl.multiple_of((side * info.pair_x + xu) * info.chunk, info.chunk)
            full[pl.ds(row, info.chunk), info.lanes(cell)] = ref[index]


def subtract_kernel(info, count, at, own, near, mine, other, *refs):
    y_parts = refs[:count]
    out, full, dense, y, sems = refs[count:]
    loads = Loads(sems)
    y_load = loads.rows(y_parts, y)
    copies = [start() for start in loads.groups([own, near], dense, GROUPS)]
    full_cases(info, at[CORE], mine, other, full)
    wait(y_load)
    for g, rows in enumerate(group_rows(dense.shape[0])):
        wait(copies[g])
        out[rows, :] = y[rows, :] - mm_nt(dense[rows, :], full[...])


def last_kernel(info, at, own, near, mine, other, inverse, inverse_near, y_hbm, *refs):
    out, full, dense, matrix, y, sems = refs
    loads = Loads(sems)
    y_load = loads.start([(y_hbm, y)])
    dense_loads = loads.groups([own, near], dense, GROUPS)
    inverse_own = inverse.at[0 : inverse_near.shape[0], :]
    matrix_loads = loads.groups([inverse_own, inverse_near], matrix, GROUPS)
    copies = [(dense_loads[g](), matrix_loads[g]()) for g in range(GROUPS)]
    full_cases(info, at[CORE], mine, other, full)
    wait(y_load)
    halves = None
    for g, rows in enumerate(group_rows(dense.shape[0])):
        wait(copies[g][0])
        z = y[rows, :] - mm_nt(dense[rows, :], full[...])
        wait(copies[g][1])
        halves = accumulate(halves, z.astype(BF16), matrix[rows, :])
    value = jnp.concatenate(halves, 1).astype(BF16)
    size = out.shape[-1]
    for n in range(out.shape[0]):
        out[n] = value[:, n * size : (n + 1) * size]


def output_kernel(parts, *refs):
    rows, out = refs[:-1], refs[-1]
    totals = [parts[0].astype(F32), parts[1].astype(F32)]
    for n in range(2, parts.shape[0]):
        totals[n % 2] = totals[n % 2] + parts[n].astype(F32)
    begin = totals[0].shape[1]
    out[0:begin, :] = jnp.concatenate(totals, 0).T
    for row in rows:
        out[begin : begin + row.shape[0], :] = row[...].astype(F32)
        begin += row.shape[0]


def solve(right_side, inverse_blocks, coupling, update_rows):
    leaves = lax.axis_size("leaf")
    blocks = lax.axis_size("blk")
    depth = leaves.bit_length() - 1
    leaf_id = lax.axis_index("leaf")
    blk_id = lax.axis_index("blk")
    core = leaf_id & 1
    yb = blk_id & 1
    zb = blk_id >> 1
    width = inverse_blocks.shape[-1]
    cases = right_side.shape[-1]
    rhs = right_side[0, 0]
    inverse = inverse_blocks[0, 0]
    couple = coupling[0, 0]
    listed_rows = coupling.shape[-1]
    counts = [width // (blocks << level) for level in range(depth + 1)]
    starts = [sum(counts[:level]) for level in range(depth + 1)]
    infos = [Level(l, leaves, blocks, width, cases) for l in range(1, depth + 1)]
    couple_starts = {}
    cursor = 0
    for level in range(depth):
        for above in range(level + 1, depth + 1):
            couple_starts[level, above] = cursor
            cursor += counts[level]
    pair_bases = []
    cursor = 0
    for level in range(depth + 1):
        pair_bases.append(cursor)
        cursor += (leaves >> level) * (depth - level)

    pair_slot = {}
    for level in range(depth):
        for above in range(level + 1, depth + 1):
            pair_slot[level, above] = SPOT + depth + len(pair_slot)

    def at():
        leaf = lax.axis_index("leaf")
        blk = lax.axis_index("blk")
        scalars = [leaf & 1, blk & 1, (leaf >> 1) & 1]
        own_cells = []
        for info in infos:
            member = leaf & ((1 << info.level) - 1)
            hi, side = split_power(member, 2 * info.pair_x)
            cell = hi * info.zbs + (blk >> 1)
            own_cells.append(cell)
            scalars.append(((cell * 2 * info.pair_x + side) * 2 + (blk & 1)) * info.rows)
        for level, above in pair_slot:
            node = leaf >> level
            scalars.append(pair_bases[level] + node * (depth - level) + (above - level - 1))
        return scalars + own_cells

    for n, info in enumerate(infos):
        info.cell_slot = SPOT + depth + len(pair_slot) + n

    def swap(value, axis, bit):
        size = leaves if axis == "leaf" else blocks
        return lax.ppermute(value, axis, [(i, i ^ bit) for i in range(size)])

    def cell_columns(rows, level):
        info = infos[level - 1]
        parts = rows.reshape(-1, info.his, 2 * info.pair_x, info.zbs, 2 * info.rows)
        return parts.transpose(0, 1, 3, 2, 4).reshape(-1, width)

    def exchange_outer(value, level):
        if level <= 1:
            return lax.all_to_all(value, "blk", 0, 0, tiled=True)
        return lax.all_to_all(
            value,
            ("leaf", "blk"),
            0,
            0,
            axis_index_groups=infos[level - 1].outer,
            tiled=True,
        )

    def exchange_middle(value, level):
        info = infos[level - 1]
        if level <= 1:
            return lax.all_to_all(
                value, "blk", 0, 0, axis_index_groups=info.inner_blk, tiled=True
            )
        return lax.all_to_all(
            value, ("leaf", "blk"), 0, 0, axis_index_groups=info.middle, tiled=True
        )

    def exchange_inner(value, level):
        info = infos[level - 1]
        if info.his == 1:
            return lax.all_to_all(
                value, "blk", 0, 0, axis_index_groups=info.inner_blk, tiled=True
            )
        return lax.all_to_all(
            value, ("leaf", "blk"), 0, 0, axis_index_groups=info.inner, tiled=True
        )

    def swap_inner(value, level, d):
        info = infos[level - 1]
        groups = info.inner_blk if info.his == 1 else info.inner
        axes = "blk" if info.his == 1 else ("leaf", "blk")
        pairs = [(device, group[i ^ d]) for group in groups for i, device in enumerate(group)]
        return lax.ppermute(value, axes, pairs)

    def coupling_block(level, above):
        begin = couple_starts[level, above]
        return couple[begin : begin + counts[level]]

    uppers = range(1, depth + 1)
    dense = {}
    expanded = kernel_call(
        functools.partial(
            expand_kernel,
            1,
            infos,
            [pair_slot[0, above] for above in uppers],
            [couple_starts[0, above] for above in uppers],
        ),
        [shaped((counts[0], width), BF16)] * depth,
        [update_rows, couple],
        scalars=at,
        flops=2 * depth * counts[0] * listed_rows * width,
    )
    for above in uppers:
        dense[0, above] = expanded[above - 1]

    spread = kernel_call(
        first_kernel,
        [shaped((blocks, counts[0], cases), BF16)],
        [(rhs, None)],
        scratch=[pltpu.VMEM((counts[0], cases), F32), pltpu.SemaphoreType.DMA],
    )[0]
    full = lax.all_to_all(spread, "blk", 0, 0, tiled=True).reshape(width, cases)
    outs = [shaped((counts[0], cases // 2), F32)] * 2
    for info in infos:
        shape = (info.targets, info.chunk, info.cell_rows)
        outs += [shaped(shape, BF16), shaped(shape, BF16)]
    matrix_scratch = pltpu.VMEM((counts[0], width), BF16)
    y_keep, y_send, *base = kernel_call(
        functools.partial(subtree_kernel, infos, starts[1:]),
        outs,
        [full, (inverse, None), (rhs, None)] + hbm([dense[0, above] for above in uppers]),
        scalars=at,
        scratch=[
            pltpu.VMEM((cases, width), F32),
            matrix_scratch,
            pltpu.VMEM((depth, counts[0], width), BF16),
            pltpu.VMEM(rhs.shape, F32),
            pltpu.SemaphoreType.DMA((1 + GROUPS * (1 + depth),)),
        ],
        flops=2 * (1 + depth) * counts[0] * width * cases,
        stay=[True, True, False, False] + [True, True] * (depth - 1),
    )
    received = []
    for level in uppers:
        received.append(swap(base[2 * level - 1], "leaf", 1))
    paired = {}
    for level in range(2, depth + 1):
        info = infos[level - 1]
        both = base[2 * level - 2].astype(F32) + received[level - 1].astype(F32)
        both = both.astype(BF16).reshape(-1, 2, info.chunk, info.cell_rows)
        keep = lax.dynamic_index_in_dim(both, yb, 1, keepdims=False)
        send = lax.dynamic_index_in_dim(both, 1 - yb, 1, keepdims=False)
        paired[level] = keep, swap(send, "blk", 1)

    def pieces_of(value, level):
        pieces = [value]
        if infos[level - 1].pair_x == 2:
            pieces += [swap(piece, "leaf", 2) for piece in pieces]
        pieces += [swap(piece, "blk", 1) for piece in pieces]
        pieces += [swap(piece, "leaf", 1) for piece in pieces]
        return pieces

    inverse_pieces = {}
    for level in uppers:
        rows = inverse[starts[level] : starts[level] + counts[level]]
        if not infos[level - 1].direct:
            rows = cell_columns(rows, level)
        inverse_pieces[level] = pieces_of(rows, level)
        for above in range(level + 1, depth + 1):
            pieces = pieces_of(coupling_block(level, above), level)
            rows = len(pieces) * counts[level]
            dense[level, above] = kernel_call(
                functools.partial(
                    expand_kernel,
                    len(pieces),
                    [infos[above - 1]],
                    [pair_slot[level, above]],
                    None,
                ),
                [shaped((rows, width), BF16)],
                [update_rows] + pieces,
                scalars=at,
                flops=2 * rows * listed_rows * width,
            )[0]

    y_near = swap(y_send, "blk", 1)
    dense_near = {}
    for above in range(depth, 0, -1):
        block = swap(coupling_block(0, above), "blk", 1)
        dense_near[above] = kernel_call(
            functools.partial(
                expand_kernel, 1, [infos[above - 1]], [pair_slot[0, above]], None
            ),
            [shaped((counts[0], width), BF16)],
            [update_rows, block],
            scalars=at,
            flops=2 * counts[0] * listed_rows * width,
        )[0]
    inverse_near = swap(inverse[: counts[0]], "blk", 1)

    def sum_spread(parts, copies):
        return kernel_call(
            sum_spread_kernel, [shaped((copies,) + parts.shape[1:], BF16)], [parts]
        )[0]

    def sum_parts(parts, copies):
        return kernel_call(
            sum_parts_kernel, [shaped((copies,) + parts[0].shape, BF16)], parts
        )[0]

    def stage_scratch(info):
        return pltpu.VMEM((info.cells, info.chunk, info.cell_rows), BF16)

    def cell_scratch(info):
        return pltpu.VMEM((info.cell_rows, width), BF16)

    ys = {}
    parts = (base[0].astype(F32) + received[0].astype(F32)).astype(BF16)
    for level in uppers:
        info = infos[level - 1]
        parts = (exchange_outer if level == 1 else exchange_middle)(parts, level)
        if level == depth:
            gathered = exchange_inner(sum_spread(parts, info.cells), level)
        else:
            own = sum_spread(parts, 1)
            gathered = [own] + [
                swap_inner(own, level, d) for d in range(info.cells - 1, 0, -1)
            ][::-1]
        size = info.cell_rows * width * info.chunk
        count = 4 * info.pair_x
        if level == depth:
            parts = kernel_call(
                functools.partial(top_kernel, info),
                [shaped((info.chunk, info.cell_rows), BF16)] * info.cells,
                [gathered] + [(piece, True) for piece in inverse_pieces[level]],
                scalars=at,
                scratch=[stage_scratch(info)],
                flops=4 * size,
                stay=[False] * info.cells,
            )
            break
        above = infos[level]
        ys[level], parts = kernel_call(
            functools.partial(forward_kernel, infos, level),
            [
                shaped((info.cell_rows, info.chunk), F32),
                shaped((above.targets // 2, above.chunk, above.cell_rows), BF16),
            ],
            gathered
            + hbm(
                list(paired[level + 1])
                + inverse_pieces[level]
                + [ys[j] for j in range(1, level)]
                + [dense[j, level + 1] for j in range(1, level + 1)]
            ),
            scalars=at,
            scratch=[
                pltpu.VMEM((above.chunk * above.pair_x, width), F32),
                cell_scratch(info),
                pltpu.VMEM((above.targets // 2, above.chunk, above.cell_rows), BF16),
                pltpu.VMEM((above.targets // 2, above.chunk, above.cell_rows), BF16),
                pltpu.SemaphoreType.DMA((count + GROUPS * level + 1 + level,)),
            ]
            + [cell_scratch(infos[j - 1]) for j in range(1, level + 1)]
            + [pltpu.VMEM(ys[j].shape, F32) for j in range(1, level)]
            + [stage_scratch(info)],
            flops=4 * size,
        )

    solved = {}
    swapped = {}
    pair_scratch = pltpu.VMEM((2 * counts[0], width), BF16)
    half_cases = cases // 2
    low = [y_keep, y_near]
    for level in range(depth, 0, -1):
        info = infos[level - 1]
        if level < depth:
            higher = range(level + 1, depth + 1)
            count = 4 * info.pair_x
            parts = kernel_call(
                functools.partial(backward_kernel, infos, level),
                [shaped((info.chunk, info.cell_rows), BF16)] * info.cells,
                hbm([ys[level]] + inverse_pieces[level])
                + [solved[above] for above in higher]
                + hbm([dense[level, above] for above in higher]),
                scalars=at,
                scratch=[
                    stage_scratch(info),
                    cell_scratch(info),
                    pltpu.VMEM(ys[level].shape, F32),
                    pltpu.SemaphoreType.DMA((1 + count + GROUPS * len(higher),)),
                ]
                + [cell_scratch(info)] * len(higher),
                flops=4 * info.cell_rows * width * info.chunk,
                stay=[False] * info.cells,
            )
        parts = [parts[0]] + [
            swap_inner(parts[d], level, d) for d in range(1, info.cells)
        ]
        solved[level] = exchange_middle(sum_parts(parts, info.cells * info.pair_x), level)
        swapped[level] = swap(solved[level], "leaf", 1)
        if level > 1:
            low = kernel_call(
                functools.partial(subtract_kernel, info, len(low)),
                [shaped((2 * counts[0], half_cases), F32)],
                hbm([dense[0, level], dense_near[level]])
                + [solved[level], swapped[level]]
                + [(low[0], None)]
                + [(value, False) for value in low[1:]],
                scalars=at,
                scratch=[
                    pltpu.VMEM((half_cases, width), BF16),
                    pair_scratch,
                    pltpu.VMEM((2 * counts[0], half_cases), F32),
                    pltpu.SemaphoreType.DMA((2 + GROUPS,)),
                ],
                flops=2 * counts[0] * width * cases,
            )

    part = kernel_call(
        functools.partial(last_kernel, infos[0]),
        [shaped((blocks, half_cases, counts[0]), BF16)],
        hbm([dense[0, 1], dense_near[1]])
        + [solved[1], swapped[1]]
        + [(inverse, None), (inverse_near, False), (low[0], None)],
        scalars=at,
        scratch=[
            pltpu.VMEM((half_cases, width), BF16),
            pair_scratch,
            pair_scratch,
            pltpu.VMEM((2 * counts[0], half_cases), F32),
            pltpu.SemaphoreType.DMA((1 + 2 * GROUPS,)),
        ],
        flops=4 * counts[0] * width * cases,
    )[0]
    parts = lax.all_to_all(part, "blk", 0, 0, tiled=True)

    keeps = []
    sends = []
    for level in uppers:
        info = infos[level - 1]
        member = leaf_id & ((1 << level) - 1)
        side = member & (2 * info.pair_x - 1)
        hi = member // (2 * info.pair_x)

        def own(value):
            shape = (info.his, info.pair_x, info.zbs, info.chunk, info.cell_rows)
            sizes = (1, info.pair_x, 1, info.chunk, 2 * info.rows)
            start = (hi, 0, zb, 0, side * 2 * info.rows)
            taken = lax.dynamic_slice(value.reshape(shape), start, sizes)
            return taken.reshape(half_cases // 2, 2 * info.rows)

        mine, other = own(solved[level]), own(swapped[level])
        both = jnp.where(
            core == 0, jnp.concatenate([mine, other], 0), jnp.concatenate([other, mine], 0)
        )
        keeps.append(jnp.where(yb == 0, both[:, : info.rows], both[:, info.rows :]))
        sends.append(jnp.where(yb == 0, both[:, info.rows :], both[:, : info.rows]))
    keep = jnp.concatenate(keeps, 1)
    near = swap(jnp.concatenate(sends, 1), "blk", 1)
    rows = jnp.where(
        yb == 0, jnp.concatenate([keep, near], 0), jnp.concatenate([near, keep], 0)
    )
    outputs = [rows.T]
    out = kernel_call(
        output_kernel, [shaped((sum(counts), cases), F32)], [parts] + outputs
    )[0]
    return out[None, None]


def solution(mesh):
    spec = P("leaf", "blk", None, None)
    return jax.shard_map(
        solve, mesh=mesh, in_specs=(spec, spec, spec, P()), out_specs=spec, check_vma=False
    )
```

```python
import functools

import jax
import jax.numpy as jnp
from jax import lax
from jax.experimental import pallas as pl
from jax.experimental.pallas import tpu as pltpu
from jax.sharding import PartitionSpec as P


BF16 = jnp.bfloat16
F32 = jnp.float32


def mm(a, b):
    return jnp.dot(a, b, preferred_element_type=F32)


def mm_tn(a, b):
    return lax.dot_general(a, b, (((0,), (0,)), ((), ())), preferred_element_type=F32)


def mm_nt(a, b):
    return lax.dot_general(a, b, (((1,), (1,)), ((), ())), preferred_element_type=F32)


def shaped(shape, dtype):
    return jax.ShapeDtypeStruct(tuple(shape), dtype)


def kernel_call(body, outs, args, scalars=None, scratch=(), flops=0, stay=None):
    stay = [True] * len(outs) if stay is None else stay
    values = []
    specs = []
    moved = sum(o.size * o.dtype.itemsize for o in outs)
    for arg in args:
        value, spec = arg, pl.BlockSpec(memory_space=pltpu.VMEM)
        if isinstance(arg, tuple):
            value = pltpu.with_memory_space_constraint(arg[0], pltpu.HBM)
            if arg[1] is None:
                spec = pl.BlockSpec(memory_space=pltpu.HBM)
            elif arg[1] is False:
                value, spec = arg[0], pl.BlockSpec(memory_space=pl.ANY)
        values.append(value)
        specs.append(spec)
        moved += value.size * value.dtype.itemsize
    return pl.pallas_call(
        body if scalars is None else lambda *refs: body(scalars(), *refs),
        out_shape=[
            pltpu.HBM(o.shape, o.dtype) if keep else o for o, keep in zip(outs, stay)
        ],
        in_specs=specs,
        out_specs=[pl.BlockSpec(memory_space=pltpu.VMEM)] * len(outs),
        scratch_shapes=list(scratch),
        compiler_params=pltpu.CompilerParams(vmem_limit_bytes=16 << 20),
        cost_estimate=pl.CostEstimate(flops=flops, bytes_accessed=moved, transcendentals=0),
    )(*values)


def hbm(values):
    return [(value, None) for value in values]


class Loads:
    def __init__(self, sems):
        self.sems = sems
        self.used = 0

    def start(self, pairs):
        copies = []
        for source, target in pairs:
            copies.append(pltpu.make_async_copy(source, target, self.sems.at[self.used]))
            copies[-1].start()
            self.used += 1
        return copies

    def rows(self, sources, target):
        pairs = []
        begin = 0
        for source in sources:
            count = source.shape[0]
            pairs.append((source, target.at[begin : begin + count, :]))
            begin += count
        return self.start(pairs)

    def groups(self, sources, target, order):
        rows = target.shape[0] // order
        if len(sources) == 1:
            source = sources[0]
            return [
                lambda g=g: self.start(
                    [(source.at[g * rows : (g + 1) * rows, :], target.at[g * rows : (g + 1) * rows, :])]
                )
                for g in range(order)
            ]
        each = len(sources) // order
        return [
            lambda g=g: self.rows(
                sources[g * each : (g + 1) * each], target.at[g * rows : (g + 1) * rows, :]
            )
            for g in range(order)
        ]


GROUPS = 2


def group_rows(total):
    size = total // GROUPS
    return [slice(g * size, (g + 1) * size) for g in range(GROUPS)]


def accumulate(total, left, right):
    half = right.shape[1] // 2
    terms = [mm_tn(left, right[:, :half]), mm_tn(left, right[:, half:])]
    return terms if total is None else [t + term for t, term in zip(total, terms)]


def wait(copies):
    for copy in copies:
        copy.wait()


def split_power(value, size):
    bits = size.bit_length() - 1
    if size == 1 << bits:
        return value >> bits, value & (size - 1)
    return value // size, value % size


class Level:
    def __init__(self, level, leaves, blocks, width, cases):
        self.level = level
        self.pair_x = 2 if level >= 2 else 1
        self.his = (1 << level) // (2 * self.pair_x)
        self.zbs = blocks // 2
        self.rows = width // (blocks << level)
        self.cells = self.his * self.zbs
        self.cell_rows = width // self.cells
        self.chunk = cases // (4 * self.pair_x)
        self.targets = self.cells * self.pair_x * 2
        outer = []
        inner = []
        middle = []
        for node in range(leaves >> level):
            base = node << level
            for side in range(2):
                outer.append(
                    [
                        (base + 2 * upper + side) * blocks + b
                        for upper in range(1 << (level - 1))
                        for b in range(blocks)
                    ]
                )
                for yb in range(2):
                    middle.append(
                        [
                            (base + 2 * upper + side) * blocks + 2 * zb + yb
                            for upper in range(1 << (level - 1))
                            for zb in range(self.zbs)
                        ]
                    )
                for xu in range(self.pair_x):
                    for yb in range(2):
                        inner.append(
                            [
                                (base + (hi * self.pair_x + xu) * 2 + side) * blocks + 2 * zb + yb
                                for hi in range(self.his)
                                for zb in range(self.zbs)
                            ]
                        )
        self.outer = outer
        self.inner = inner
        self.middle = middle
        self.inner_blk = [[2 * zb + yb for zb in range(self.zbs)] for yb in range(2)]

    @property
    def direct(self):
        return (2 * self.rows) % 128 == 0

    def natural(self):
        if not self.direct:
            return [(c * self.cell_rows, c, 0, self.cell_rows) for c in range(self.cells)]
        size = 2 * self.rows
        return [
            (
                ((hi * 2 * self.pair_x + side) * self.zbs + zb) * size,
                hi * self.zbs + zb,
                side * size,
                size,
            )
            for hi in range(self.his)
            for side in range(2 * self.pair_x)
            for zb in range(self.zbs)
        ]

    def position(self, rows):
        block, t = split_power(rows, 2 * self.rows)
        block, zpos = split_power(block, self.zbs)
        hi, side = split_power(block, 2 * self.pair_x)
        cell = hi * self.zbs + zpos
        return (cell * (2 * self.pair_x) + side) * (2 * self.rows) + t

    def target(self, hi, xu, zb, yb):
        return ((hi * self.pair_x + xu) * self.zbs + zb) * 2 + yb

    def lanes(self, cell):
        return slice(cell * self.cell_rows, (cell + 1) * self.cell_rows)

    def slots(self):
        for hi in range(self.his):
            for xu in range(self.pair_x):
                for zb in range(self.zbs):
                    index = (hi * self.pair_x + xu) * self.zbs + zb
                    yield hi * self.zbs + zb, xu, index

    def all_targets(self):
        for hi in range(self.his):
            for xu in range(self.pair_x):
                for zb in range(self.zbs):
                    for yb in range(2):
                        yield hi * self.zbs + zb, xu, yb, self.target(hi, xu, zb, yb)


CORE, YB, XU, SPOT = 0, 1, 2, 3


def first_kernel(rhs, out, rows, sem):
    copy = pltpu.make_async_copy(rhs.at[0 : rows.shape[0], :], rows, sem)
    copy.start()
    copy.wait()
    rounded = rows[...].astype(BF16)
    for n in range(out.shape[0]):
        out[n] = rounded


def expand_kernel(count, aboves, slots, begins, at, lists, *refs):
    blocks, outs = refs[:count], refs[count:]
    width = outs[0].shape[-1]
    step = min(512, width)
    for n, (info, out) in enumerate(zip(aboves, outs)):
        listed = info.position(lists[pl.ds(at[slots[n]], 1), :])
        if begins is None:
            block = jnp.concatenate([b[...] for b in blocks], 0)
        else:
            block = blocks[0][begins[n] : begins[n] + out.shape[0], :]
        for begin in range(0, width, step):
            ids = begin + lax.broadcasted_iota(jnp.int32, (step, listed.shape[-1]), 0)
            chosen = jnp.where(ids == listed, 1.0, 0.0).astype(BF16)
            out[:, begin : begin + step] = mm_nt(block, chosen).astype(BF16)


def subtree_kernel(infos, starts, at, full, inverse, rhs, *refs):
    depth = len(infos)
    sources = refs[:depth]
    outs = refs[depth : depth + 2 + 2 * depth]
    total, matrix, dense, rhs_copy, sems = refs[depth + 2 + 2 * depth :]
    loads = Loads(sems)
    rhs_load = loads.start([(rhs, rhs_copy)])
    groups = group_rows(matrix.shape[0])
    first = [start() for start in loads.groups([inverse], matrix, GROUPS)]
    later = [
        [start() for start in loads.groups([sources[n]], dense.at[n], GROUPS)]
        for n in range(depth)
    ]
    core = at[CORE]
    width = total.shape[-1]
    placed = []
    wait(rhs_load)
    for n, info in enumerate(infos):
        row_ids = at[SPOT + n] + lax.broadcasted_iota(jnp.int32, (info.rows, width), 0)
        lane_ids = lax.broadcasted_iota(jnp.int32, (info.rows, width), 1)
        spots = jnp.where(row_ids == lane_ids, 1.0, 0.0).astype(BF16)
        own = rhs_copy[starts[n] : starts[n] + info.rows, :].astype(BF16)
        placed.append(accumulate(None, own, spots))
    rounded = []
    for g, rows in enumerate(groups):
        wait(first[g])
        y = mm(matrix[rows, :], full[...])
        cut = y.shape[1] // 2
        low = at[YB] == 0
        outs[0][rows, :] = jnp.where(low, y[:, :cut], y[:, cut:])
        outs[1][rows, :] = jnp.where(low, y[:, cut:], y[:, :cut])
        rounded.append(y.astype(BF16))
    half = width // 2
    for n, info in enumerate(infos):
        term = None
        for g, rows in enumerate(groups):
            wait(later[n][g])
            term = accumulate(term, rounded[g], dense[n, rows, :])
        total[:, :half] = placed[n][0] - term[0]
        total[:, half:] = placed[n][1] - term[1]
        mine, other = outs[2 + 2 * n], outs[3 + 2 * n]
        for cell, xu, yb, target in info.all_targets():
            for side, ref in ((core, mine), (1 - core, other)):
                row = ((yb * 2 + side) * info.pair_x + xu) * info.chunk
                row = pl.multiple_of(row, info.chunk)
                value = total[pl.ds(row, info.chunk), info.lanes(cell)]
                ref[target] = value.astype(ref.dtype)


def sum_spread_kernel(parts, out):
    total = parts[0].astype(F32)
    for n in range(1, parts.shape[0]):
        total = total + parts[n].astype(F32)
    rounded = total.astype(BF16)
    for n in range(out.shape[0]):
        out[n] = rounded


def sum_parts_kernel(*refs):
    parts, out = refs[:-1], refs[-1]
    total = parts[0][...].astype(F32)
    for part in parts[1:]:
        total = total + part[...].astype(F32)
    rounded = total.astype(BF16)
    for n in range(out.shape[0]):
        out[n] = rounded


def natural_rows(info, gathered):
    blocks = [
        gathered[cell][:, inside : inside + size]
        for _, cell, inside, size in info.natural()
    ]
    return jnp.concatenate(blocks, 1)


def put_spread(info, halves, stage, own_cell, outs):
    value = jnp.concatenate(halves, 1).astype(BF16)
    for lane, cell, inside, size in info.natural():
        stage[cell, :, inside : inside + size] = value[:, lane : lane + size]
    for d, out in enumerate(outs):
        out[...] = stage[own_cell ^ d]


def forward_kernel(infos, k, at, *refs):
    info, above = infos[k - 1], infos[k]
    near = refs[: info.cells]
    mine_hbm, received_hbm = refs[info.cells : info.cells + 2]
    gathered, refs = refs[-1], refs[info.cells + 2 : -1]
    count = 4 * info.pair_x
    pieces = refs[:count]
    lower_y = refs[count : count + k - 1]
    sources = refs[count + k - 1 : count + 2 * k - 1]
    y_ref, out, total, matrix, mine, received, sems = refs[count + 2 * k - 1 : count + 2 * k + 6]
    dense = refs[count + 2 * k + 6 : count + 3 * k + 6]
    lower_copies = refs[count + 3 * k + 6 :]
    loads = Loads(sems)
    groups = group_rows(matrix.shape[0])
    first = [start() for start in loads.groups(pieces, matrix, GROUPS)]
    later = [
        [start() for start in loads.groups([source], dense[j], GROUPS)]
        for j, source in enumerate(sources)
    ]
    base = loads.start([(mine_hbm, mine), (received_hbm, received)])
    base += loads.start(list(zip(lower_y, lower_copies)))
    lower_y = lower_copies
    for d, value in enumerate(near):
        gathered[at[info.cell_slot] ^ d] = value[0]
    vector = natural_rows(info, gathered)
    ys = []
    for g, rows in enumerate(groups):
        wait(first[g])
        y = mm_nt(matrix[rows, :], vector)
        y_ref[rows, :] = y
        ys.append(y)
    wait(base)
    same = {}
    for j in range(1, k + 1):
        term = None
        for g, rows in enumerate(group_rows(dense[j - 1].shape[0])):
            value = ys[g] if j == k else lower_y[j - 1][rows, :]
            wait(later[j - 1][g])
            term = accumulate(term, value.astype(BF16), dense[j - 1][rows, :])
        term = jnp.concatenate(term, 1)
        same.setdefault(infos[j - 1].pair_x == above.pair_x, []).append(term)
    if False in same:
        total[...] = functools.reduce(jnp.add, same[False])
    else:
        total[...] = jnp.zeros(total.shape, F32)
    if True in same:
        term = functools.reduce(jnp.add, same[True])
        rows = pl.ds(pl.multiple_of(at[XU] * above.chunk, above.chunk), above.chunk)
        total[rows, :] = total[rows, :] + term
    for cell, xu, index in above.slots():
        value = mine[index].astype(F32) + received[index].astype(F32)
        minus = total[xu * above.chunk : (xu + 1) * above.chunk, above.lanes(cell)]
        out[index] = (value - minus).astype(BF16)


def top_kernel(info, at, gathered, *refs):
    pieces = refs[: 4 * info.pair_x]
    outs, stage = refs[4 * info.pair_x : -1], refs[-1]
    each = len(pieces) // GROUPS
    vector = natural_rows(info, gathered)
    halves = None
    for g in range(GROUPS):
        matrix = jnp.concatenate([p[...] for p in pieces[g * each : (g + 1) * each]], 0)
        y = mm_nt(matrix, vector)
        halves = accumulate(halves, y.astype(BF16), matrix)
    put_spread(info, halves, stage, at[info.cell_slot], outs)


def backward_kernel(infos, k, at, y_hbm, *refs):
    info = infos[k - 1]
    count = 4 * info.pair_x
    uppers = infos[k:]
    many = len(uppers)
    pieces = refs[:count]
    solved = refs[count : count + many]
    sources = refs[count + many : count + 2 * many]
    begin = count + 2 * many
    outs = refs[begin : begin + info.cells]
    stage, matrix, y, sems = refs[begin + info.cells : begin + info.cells + 4]
    dense = refs[begin + info.cells + 4 :]
    loads = Loads(sems)
    y_load = loads.start([(y_hbm, y)])
    dense_loads = [loads.groups([source], dense[n], GROUPS) for n, source in enumerate(sources)]
    matrix_loads = loads.groups(pieces, matrix, GROUPS)
    first = []
    last = []
    for g in range(GROUPS):
        first.append([start[g]() for start in dense_loads])
        last.append(matrix_loads[g]())
    vectors = []
    for n, above in enumerate(uppers):
        parts = []
        for hi in range(above.his):
            for zb in range(above.zbs):
                first_slot = hi * above.pair_x * above.zbs + zb
                if above.pair_x == info.pair_x:
                    parts.append(solved[n][first_slot + at[XU] * above.zbs])
                else:
                    slots = [first_slot + xu * above.zbs for xu in range(above.pair_x)]
                    parts.append(jnp.concatenate([solved[n][slot] for slot in slots], 0))
        vectors.append(jnp.concatenate(parts, 1))
    wait(y_load)
    halves = None
    for g, rows in enumerate(group_rows(matrix.shape[0])):
        z = y[rows, :]
        for n in range(many):
            wait(first[g][n])
            z = z - mm_nt(dense[n][rows, :], vectors[n])
        wait(last[g])
        halves = accumulate(halves, z.astype(BF16), matrix[rows, :])
    put_spread(info, halves, stage, at[info.cell_slot], outs)


def full_cases(info, core, mine, other, full):
    for cell, xu, index in info.slots():
        for side, ref in ((core, mine), (1 - core, other)):
            row = pl.multiple_of((side * info.pair_x + xu) * info.chunk, info.chunk)
            full[pl.ds(row, info.chunk), info.lanes(cell)] = ref[index]


def subtract_kernel(info, count, at, own, near, mine, other, *refs):
    y_parts = refs[:count]
    out, full, dense, y, sems = refs[count:]
    loads = Loads(sems)
    y_load = loads.rows(y_parts, y)
    copies = [start() for start in loads.groups([own, near], dense, GROUPS)]
    full_cases(info, at[CORE], mine, other, full)
    wait(y_load)
    for g, rows in enumerate(group_rows(dense.shape[0])):
        wait(copies[g])
        out[rows, :] = y[rows, :] - mm_nt(dense[rows, :], full[...])


def last_kernel(info, at, own, near, mine, other, inverse, inverse_near, y_hbm, *refs):
    out, full, dense, matrix, y, sems = refs
    loads = Loads(sems)
    y_load = loads.start([(y_hbm, y)])
    dense_loads = loads.groups([own, near], dense, GROUPS)
    inverse_own = inverse.at[0 : inverse_near.shape[0], :]
    matrix_loads = loads.groups([inverse_own, inverse_near], matrix, GROUPS)
    copies = [(dense_loads[g](), matrix_loads[g]()) for g in range(GROUPS)]
    full_cases(info, at[CORE], mine, other, full)
    wait(y_load)
    halves = None
    for g, rows in enumerate(group_rows(dense.shape[0])):
        wait(copies[g][0])
        z = y[rows, :] - mm_nt(dense[rows, :], full[...])
        wait(copies[g][1])
        halves = accumulate(halves, z.astype(BF16), matrix[rows, :])
    value = jnp.concatenate(halves, 1).astype(BF16)
    size = out.shape[-1]
    for n in range(out.shape[0]):
        out[n] = value[:, n * size : (n + 1) * size]


def output_kernel(parts, *refs):
    rows, out = refs[:-1], refs[-1]
    totals = [parts[0].astype(F32), parts[1].astype(F32)]
    for n in range(2, parts.shape[0]):
        totals[n % 2] = totals[n % 2] + parts[n].astype(F32)
    begin = totals[0].shape[1]
    out[0:begin, :] = jnp.concatenate(totals, 0).T
    for row in rows:
        out[begin : begin + row.shape[0], :] = row[...].astype(F32)
        begin += row.shape[0]


def solve(right_side, inverse_blocks, coupling, update_rows):
    leaves = lax.axis_size("leaf")
    blocks = lax.axis_size("blk")
    depth = leaves.bit_length() - 1
    leaf_id = lax.axis_index("leaf")
    blk_id = lax.axis_index("blk")
    core = leaf_id & 1
    yb = blk_id & 1
    zb = blk_id >> 1
    width = inverse_blocks.shape[-1]
    cases = right_side.shape[-1]
    rhs = right_side[0, 0]
    inverse = inverse_blocks[0, 0]
    couple = coupling[0, 0]
    listed_rows = coupling.shape[-1]
    counts = [width // (blocks << level) for level in range(depth + 1)]
    starts = [sum(counts[:level]) for level in range(depth + 1)]
    infos = [Level(l, leaves, blocks, width, cases) for l in range(1, depth + 1)]
    couple_starts = {}
    cursor = 0
    for level in range(depth):
        for above in range(level + 1, depth + 1):
            couple_starts[level, above] = cursor
            cursor += counts[level]
    pair_bases = []
    cursor = 0
    for level in range(depth + 1):
        pair_bases.append(cursor)
        cursor += (leaves >> level) * (depth - level)

    pair_slot = {}
    for level in range(depth):
        for above in range(level + 1, depth + 1):
            pair_slot[level, above] = SPOT + depth + len(pair_slot)

    def at():
        leaf = lax.axis_index("leaf")
        blk = lax.axis_index("blk")
        scalars = [leaf & 1, blk & 1, (leaf >> 1) & 1]
        own_cells = []
        for info in infos:
            member = leaf & ((1 << info.level) - 1)
            hi, side = split_power(member, 2 * info.pair_x)
            cell = hi * info.zbs + (blk >> 1)
            own_cells.append(cell)
            scalars.append(((cell * 2 * info.pair_x + side) * 2 + (blk & 1)) * info.rows)
        for level, above in pair_slot:
            node = leaf >> level
            scalars.append(pair_bases[level] + node * (depth - level) + (above - level - 1))
        return scalars + own_cells

    for n, info in enumerate(infos):
        info.cell_slot = SPOT + depth + len(pair_slot) + n

    def swap(value, axis, bit):
        size = leaves if axis == "leaf" else blocks
        return lax.ppermute(value, axis, [(i, i ^ bit) for i in range(size)])

    def cell_columns(rows, level):
        info = infos[level - 1]
        parts = rows.reshape(-1, info.his, 2 * info.pair_x, info.zbs, 2 * info.rows)
        return parts.transpose(0, 1, 3, 2, 4).reshape(-1, width)

    def exchange_outer(value, level):
        if level <= 1:
            return lax.all_to_all(value, "blk", 0, 0, tiled=True)
        return lax.all_to_all(
            value,
            ("leaf", "blk"),
            0,
            0,
            axis_index_groups=infos[level - 1].outer,
            tiled=True,
        )

    def exchange_middle(value, level):
        info = infos[level - 1]
        if level <= 1:
            return lax.all_to_all(
                value, "blk", 0, 0, axis_index_groups=info.inner_blk, tiled=True
            )
        return lax.all_to_all(
            value, ("leaf", "blk"), 0, 0, axis_index_groups=info.middle, tiled=True
        )

    def exchange_inner(value, level):
        info = infos[level - 1]
        if info.his == 1:
            return lax.all_to_all(
                value, "blk", 0, 0, axis_index_groups=info.inner_blk, tiled=True
            )
        return lax.all_to_all(
            value, ("leaf", "blk"), 0, 0, axis_index_groups=info.inner, tiled=True
        )

    def swap_inner(value, level, d):
        info = infos[level - 1]
        groups = info.inner_blk if info.his == 1 else info.inner
        axes = "blk" if info.his == 1 else ("leaf", "blk")
        pairs = [(device, group[i ^ d]) for group in groups for i, device in enumerate(group)]
        return lax.ppermute(value, axes, pairs)

    def coupling_block(level, above):
        begin = couple_starts[level, above]
        return couple[begin : begin + counts[level]]

    uppers = range(1, depth + 1)
    dense = {}
    expanded = kernel_call(
        functools.partial(
            expand_kernel,
            1,
            infos,
            [pair_slot[0, above] for above in uppers],
            [couple_starts[0, above] for above in uppers],
        ),
        [shaped((counts[0], width), BF16)] * depth,
        [update_rows, couple],
        scalars=at,
        flops=2 * depth * counts[0] * listed_rows * width,
    )
    for above in uppers:
        dense[0, above] = expanded[above - 1]

    spread = kernel_call(
        first_kernel,
        [shaped((blocks, counts[0], cases), BF16)],
        [(rhs, None)],
        scratch=[pltpu.VMEM((counts[0], cases), F32), pltpu.SemaphoreType.DMA],
    )[0]
    full = lax.all_to_all(spread, "blk", 0, 0, tiled=True).reshape(width, cases)
    outs = [shaped((counts[0], cases // 2), F32)] * 2
    for info in infos:
        shape = (info.targets, info.chunk, info.cell_rows)
        outs += [shaped(shape, BF16), shaped(shape, BF16)]
    matrix_scratch = pltpu.VMEM((counts[0], width), BF16)
    y_keep, y_send, *base = kernel_call(
        functools.partial(subtree_kernel, infos, starts[1:]),
        outs,
        [full, (inverse, None), (rhs, None)] + hbm([dense[0, above] for above in uppers]),
        scalars=at,
        scratch=[
            pltpu.VMEM((cases, width), F32),
            matrix_scratch,
            pltpu.VMEM((depth, counts[0], width), BF16),
            pltpu.VMEM(rhs.shape, F32),
            pltpu.SemaphoreType.DMA((1 + GROUPS * (1 + depth),)),
        ],
        flops=2 * (1 + depth) * counts[0] * width * cases,
        stay=[True, True, False, False] + [True, True] * (depth - 1),
    )
    received = []
    for level in uppers:
        received.append(swap(base[2 * level - 1], "leaf", 1))
    paired = {}
    for level in range(2, depth + 1):
        info = infos[level - 1]
        both = base[2 * level - 2].astype(F32) + received[level - 1].astype(F32)
        both = both.astype(BF16).reshape(-1, 2, info.chunk, info.cell_rows)
        keep = lax.dynamic_index_in_dim(both, yb, 1, keepdims=False)
        send = lax.dynamic_index_in_dim(both, 1 - yb, 1, keepdims=False)
        paired[level] = keep, swap(send, "blk", 1)

    def pieces_of(value, level):
        pieces = [value]
        if infos[level - 1].pair_x == 2:
            pieces += [swap(piece, "leaf", 2) for piece in pieces]
        pieces += [swap(piece, "blk", 1) for piece in pieces]
        pieces += [swap(piece, "leaf", 1) for piece in pieces]
        return pieces

    inverse_pieces = {}
    for level in uppers:
        rows = inverse[starts[level] : starts[level] + counts[level]]
        if not infos[level - 1].direct:
            rows = cell_columns(rows, level)
        inverse_pieces[level] = pieces_of(rows, level)
        for above in range(level + 1, depth + 1):
            pieces = pieces_of(coupling_block(level, above), level)
            rows = len(pieces) * counts[level]
            dense[level, above] = kernel_call(
                functools.partial(
                    expand_kernel,
                    len(pieces),
                    [infos[above - 1]],
                    [pair_slot[level, above]],
                    None,
                ),
                [shaped((rows, width), BF16)],
                [update_rows] + pieces,
                scalars=at,
                flops=2 * rows * listed_rows * width,
            )[0]

    y_near = swap(y_send, "blk", 1)
    dense_near = {}
    for above in range(depth, 0, -1):
        block = swap(coupling_block(0, above), "blk", 1)
        dense_near[above] = kernel_call(
            functools.partial(
                expand_kernel, 1, [infos[above - 1]], [pair_slot[0, above]], None
            ),
            [shaped((counts[0], width), BF16)],
            [update_rows, block],
            scalars=at,
            flops=2 * counts[0] * listed_rows * width,
        )[0]
    inverse_near = swap(inverse[: counts[0]], "blk", 1)

    def sum_spread(parts, copies):
        return kernel_call(
            sum_spread_kernel,
            [shaped((copies,) + parts.shape[1:], BF16)],
            [parts],
            stay=[copies > 1],
        )[0]

    def sum_parts(parts, copies):
        return kernel_call(
            sum_parts_kernel, [shaped((copies,) + parts[0].shape, BF16)], parts
        )[0]

    def stage_scratch(info):
        return pltpu.VMEM((info.cells, info.chunk, info.cell_rows), BF16)

    def cell_scratch(info):
        return pltpu.VMEM((info.cell_rows, width), BF16)

    ys = {}
    parts = (base[0].astype(F32) + received[0].astype(F32)).astype(BF16)
    for level in uppers:
        info = infos[level - 1]
        parts = (exchange_outer if level == 1 else exchange_middle)(parts, level)
        if level == depth:
            gathered = exchange_inner(sum_spread(parts, info.cells), level)
        else:
            own = sum_spread(parts, 1)
            gathered = [own] + [
                swap_inner(own, level, d) for d in range(info.cells - 1, 0, -1)
            ][::-1]
        size = info.cell_rows * width * info.chunk
        count = 4 * info.pair_x
        if level == depth:
            parts = kernel_call(
                functools.partial(top_kernel, info),
                [shaped((info.chunk, info.cell_rows), BF16)] * info.cells,
                [gathered] + [(piece, True) for piece in inverse_pieces[level]],
                scalars=at,
                scratch=[stage_scratch(info)],
                flops=4 * size,
                stay=[False] * info.cells,
            )
            break
        above = infos[level]
        ys[level], parts = kernel_call(
            functools.partial(forward_kernel, infos, level),
            [
                shaped((info.cell_rows, info.chunk), F32),
                shaped((above.targets // 2, above.chunk, above.cell_rows), BF16),
            ],
            gathered
            + hbm(
                list(paired[level + 1])
                + inverse_pieces[level]
                + [ys[j] for j in range(1, level)]
                + [dense[j, level + 1] for j in range(1, level + 1)]
            ),
            scalars=at,
            scratch=[
                pltpu.VMEM((above.chunk * above.pair_x, width), F32),
                cell_scratch(info),
                pltpu.VMEM((above.targets // 2, above.chunk, above.cell_rows), BF16),
                pltpu.VMEM((above.targets // 2, above.chunk, above.cell_rows), BF16),
                pltpu.SemaphoreType.DMA((count + GROUPS * level + 1 + level,)),
            ]
            + [cell_scratch(infos[j - 1]) for j in range(1, level + 1)]
            + [pltpu.VMEM(ys[j].shape, F32) for j in range(1, level)]
            + [stage_scratch(info)],
            flops=4 * size,
        )

    solved = {}
    swapped = {}
    pair_scratch = pltpu.VMEM((2 * counts[0], width), BF16)
    half_cases = cases // 2
    low = [y_keep, y_near]
    for level in range(depth, 0, -1):
        info = infos[level - 1]
        if level < depth:
            higher = range(level + 1, depth + 1)
            count = 4 * info.pair_x
            parts = kernel_call(
                functools.partial(backward_kernel, infos, level),
                [shaped((info.chunk, info.cell_rows), BF16)] * info.cells,
                hbm([ys[level]] + inverse_pieces[level])
                + [solved[above] for above in higher]
                + hbm([dense[level, above] for above in higher]),
                scalars=at,
                scratch=[
                    stage_scratch(info),
                    cell_scratch(info),
                    pltpu.VMEM(ys[level].shape, F32),
                    pltpu.SemaphoreType.DMA((1 + count + GROUPS * len(higher),)),
                ]
                + [cell_scratch(info)] * len(higher),
                flops=4 * info.cell_rows * width * info.chunk,
                stay=[False] * info.cells,
            )
        parts = [parts[0]] + [
            swap_inner(parts[d], level, d) for d in range(1, info.cells)
        ]
        solved[level] = exchange_middle(sum_parts(parts, info.cells * info.pair_x), level)
        swapped[level] = swap(solved[level], "leaf", 1)
        if level > 1:
            low = kernel_call(
                functools.partial(subtract_kernel, info, len(low)),
                [shaped((2 * counts[0], half_cases), F32)],
                hbm([dense[0, level], dense_near[level]])
                + [solved[level], swapped[level]]
                + [(low[0], None)]
                + [(value, False) for value in low[1:]],
                scalars=at,
                scratch=[
                    pltpu.VMEM((half_cases, width), BF16),
                    pair_scratch,
                    pltpu.VMEM((2 * counts[0], half_cases), F32),
                    pltpu.SemaphoreType.DMA((2 + GROUPS,)),
                ],
                flops=2 * counts[0] * width * cases,
            )

    part = kernel_call(
        functools.partial(last_kernel, infos[0]),
        [shaped((blocks, half_cases, counts[0]), BF16)],
        hbm([dense[0, 1], dense_near[1]])
        + [solved[1], swapped[1]]
        + [(inverse, None), (inverse_near, False), (low[0], None)],
        scalars=at,
        scratch=[
            pltpu.VMEM((half_cases, width), BF16),
            pair_scratch,
            pair_scratch,
            pltpu.VMEM((2 * counts[0], half_cases), F32),
            pltpu.SemaphoreType.DMA((1 + 2 * GROUPS,)),
        ],
        flops=4 * counts[0] * width * cases,
    )[0]
    parts = lax.all_to_all(part, "blk", 0, 0, tiled=True)

    keeps = []
    sends = []
    for level in uppers:
        info = infos[level - 1]
        member = leaf_id & ((1 << level) - 1)
        side = member & (2 * info.pair_x - 1)
        hi = member // (2 * info.pair_x)

        def own(value):
            shape = (info.his, info.pair_x, info.zbs, info.chunk, info.cell_rows)
            sizes = (1, info.pair_x, 1, info.chunk, 2 * info.rows)
            start = (hi, 0, zb, 0, side * 2 * info.rows)
            taken = lax.dynamic_slice(value.reshape(shape), start, sizes)
            return taken.reshape(half_cases // 2, 2 * info.rows)

        mine, other = own(solved[level]), own(swapped[level])
        both = jnp.where(
            core == 0, jnp.concatenate([mine, other], 0), jnp.concatenate([other, mine], 0)
        )
        keeps.append(jnp.where(yb == 0, both[:, : info.rows], both[:, info.rows :]))
        sends.append(jnp.where(yb == 0, both[:, info.rows :], both[:, : info.rows]))
    keep = jnp.concatenate(keeps, 1)
    near = swap(jnp.concatenate(sends, 1), "blk", 1)
    rows = jnp.where(
        yb == 0, jnp.concatenate([keep, near], 0), jnp.concatenate([near, keep], 0)
    )
    outputs = [rows.T]
    out = kernel_call(
        output_kernel, [shaped((sum(counts), cases), F32)], [parts] + outputs
    )[0]
    return out[None, None]


def solution(mesh):
    spec = P("leaf", "blk", None, None)
    return jax.shard_map(
        solve, mesh=mesh, in_specs=(spec, spec, spec, P()), out_specs=spec, check_vma=False
    )
```
